32 devices in a mesh: rep: 8 (over y, x, core), shard: 4 (over z).
Axes of the slice: x: 2, y: 2, z: 4, core: 2. Of those that a mesh axis runs over, the one named last changes fastest.
Arguments:
- inputs: bfloat16 [8192, 2048], P(('rep', 'shard')), may hold values from -6 to 6
- segments: int32 [8192], P(('rep', 'shard')), may hold values from 0 to 23, as said below
- positions: int32 [8192], P(('rep', 'shard')), may hold values from 0 to 1021, as said below
- ln_gain: float32 [2048], P('shard'), may hold values from 0.5 to 1.5
- ln_bias: float32 [2048], P('shard'), may hold values from -1 to 1
- w_qkv: bfloat16 [2048, 6144], P('shard'), may hold values from -0.125 to 0.125
- b_qkv: float32 [6144], P('shard'), may hold values from -1.5 to 1.5
- w_dense: bfloat16 [2048, 2048], P('shard'), may hold values from -0.75 to 0.75
- b_dense: float32 [2048], P('shard'), may hold values from -1.5 to 1.5
- w_fc1: bfloat16 [2048, 8192], P('shard'), may hold values from -0.125 to 0.125
- b_fc1: float32 [8192], P('shard'), may hold values from -1.5 to 1.5
- w_fc2: bfloat16 [8192, 2048], P('shard'), may hold values from -0.0625 to 0.0625
- b_fc2: float32 [2048], P('shard'), may hold values from -1.5 to 1.5
- cotangent: bfloat16 [8192, 2048], P(('rep', 'shard')), may hold values from -6 to 6
Outputs:
- block_out: float32 [8192, 2048], P(('rep', 'shard'))
- grad_inputs: float32 [8192, 2048], P(('rep', 'shard'))
- grad_ln_gain: float32 [2048], P('shard')
- grad_ln_bias: float32 [2048], P('shard')
- grad_w_qkv: float32 [2048, 6144], P('shard')
- grad_b_qkv: float32 [6144], P('shard')
- grad_w_dense: float32 [2048, 2048], P('shard')
- grad_b_dense: float32 [2048], P('shard')
- grad_w_fc1: float32 [2048, 8192], P('shard')
- grad_b_fc1: float32 [8192], P('shard')
- grad_w_fc2: float32 [8192, 2048], P('shard')
- grad_b_fc2: float32 [2048], P('shard')
The draws below stay inside these ranges and needn't reach their ends.
Inputs may be any that keep to these rules, and one draw needn't show every extreme that they name: `segments`: document numbers never fall along the tokens; each aligned block of 1024 tokens holds exactly three documents, numbered 3 b, 3 b + 1 and 3 b + 2 in block b. `positions`: A token's offset from the first token of its document.
All inputs are finite; a program needn't handle non-finite values.
Results may differ from the reference program's by a relative error of at most 0.0089.
Values may be sent and summed in bfloat16 or wider, within the bound.
No kernel may reach another device: no remote copies, remote signals or barrier semaphores. Data moves between devices by JAX's collectives and lax.ppermute only.
A program may use at most 640 MiB of HBM per device.

```python
import jax
import jax.numpy as jnp
from jax import lax

D = 2048
HEADS = 32
HEAD_DIM = 64
ROT = 32
FF = 8192
TOKENS = 8192
SEQ = 1024


def document_layout(key):
    pack_count = TOKENS // SEQ
    inner_key = jax.random.fold_in(key, 11)
    first_key, second_key = jax.random.split(inner_key)
    first_cut = jax.random.randint(first_key, (pack_count, 1), 1, SEQ // 2)
    second_cut = jax.random.randint(second_key, (pack_count, 1), SEQ // 2, SEQ)
    pack_ids = jnp.arange(pack_count, dtype=jnp.int32)[:, None]
    first_cut = jnp.where(pack_ids == 0, 1, first_cut).astype(jnp.int32)
    second_cut = jnp.where(pack_ids == 0, SEQ - 1, second_cut).astype(jnp.int32)
    offset = jnp.arange(SEQ, dtype=jnp.int32)[None, :]
    within = (offset >= first_cut).astype(jnp.int32) + (offset >= second_cut).astype(jnp.int32)
    begin_at = jnp.where(within == 0, 0, jnp.where(within == 1, first_cut, second_cut))
    numbers = (3 * pack_ids + within).reshape(TOKENS).astype(jnp.int32)
    offsets = (offset - begin_at).reshape(TOKENS).astype(jnp.int32)
    return (numbers, offsets)


def draw_segments(key, part):
    return document_layout(key)[0]


def draw_positions(key, part):
    return document_layout(key)[1]


def block_levels(own_key, extent, cuts, smallest, high):
    gain = 1.0
    for dim, blocks in cuts:
        draws = jax.random.uniform(jax.random.fold_in(jax.random.fold_in(own_key, 6), dim), (blocks,), jnp.float32, smallest / len(cuts), high / len(cuts))
        gain = gain * jnp.repeat(jnp.exp(draws), extent[dim] // blocks).reshape((-1,) + (1,) * (len(extent) - 1 - dim))
    return gain


def gaussian(own_key, extent, scale, reach, cuts=(), held_as=jnp.bfloat16):
    values = scale * jax.random.normal(own_key, extent, jnp.float32)
    if cuts:
        values = values * block_levels(own_key, extent, cuts, -0.22, 0.18)
    return jnp.clip(values, -reach, reach).astype(held_as)


def setup_inputs(seed: int = 0) -> dict:
    arg_keys = jax.random.split(jax.random.key(seed), 15)
    return {
        "inputs": gaussian(arg_keys[0], (TOKENS, D), 1.0, 6.0, ((0, 32),)),
        "segments": draw_segments(jax.random.fold_in(arg_keys[14], 71), 0),
        "positions": draw_positions(jax.random.fold_in(arg_keys[14], 71), 0),
        "ln_gain": jnp.clip(1.0 + 0.1 * jax.random.normal(arg_keys[3], (D,), jnp.float32), 0.5, 1.5),
        "ln_bias": gaussian(arg_keys[4], (D,), 0.2, 1.0, ((0, 4),), jnp.float32),
        "w_qkv": gaussian(arg_keys[5], (D, 3 * D), D ** -0.5, 0.125, ((0, 4),)),
        "b_qkv": gaussian(arg_keys[6], (3 * D,), 0.3, 1.5, ((0, 4),), jnp.float32),
        "w_dense": gaussian(arg_keys[7], (D, D), (D // 32) ** -0.5, 0.75, ((0, 4),)),
        "b_dense": gaussian(arg_keys[8], (D,), 0.3, 1.5, ((0, 4),), jnp.float32),
        "w_fc1": gaussian(arg_keys[9], (D, FF), D ** -0.5, 0.125, ((0, 4),)),
        "b_fc1": gaussian(arg_keys[10], (FF,), 0.3, 1.5, ((0, 4),), jnp.float32),
        "w_fc2": gaussian(arg_keys[11], (FF, D), FF ** -0.5, 0.0625, ((0, 4),)),
        "b_fc2": gaussian(arg_keys[12], (D,), 0.3, 1.5, ((0, 4),), jnp.float32),
        "cotangent": gaussian(arg_keys[13], (TOKENS, D), 1.0, 6.0, ((0, 32),)),
    }


@jax.custom_vjp
def low(v):
    return lax.optimization_barrier(v.astype(jnp.bfloat16)).astype(jnp.float32)

@jax.custom_vjp
def low_back(v):
    return v

def low_keep(v):
    return (low(v), None)

def low_pass(kept, grad):
    return (grad,)

def back_keep(v):
    return (v, None)

def back_low(kept, grad):
    return (low(grad),)
low.defvjp(low_keep, low_pass)
low_back.defvjp(back_keep, back_low)

def matmul(left, right):
    return jnp.dot(left, right, precision=lax.Precision.HIGHEST)

def rotary(per_head, positions):
    halfway = ROT // 2
    frequency = 10000.0 ** (-(jnp.arange(halfway, dtype=jnp.float32) * 2.0) / ROT)
    angles = positions.astype(jnp.float32)[:, None] * frequency[None, :]
    cosine = jnp.cos(angles)[:, None, :]
    sine_part = jnp.sin(angles)[:, None, :]
    leading = per_head[..., :halfway]
    trailing = per_head[..., halfway:ROT]
    return jnp.concatenate([leading * cosine - trailing * sine_part, trailing * cosine + leading * sine_part, per_head[..., ROT:]], axis=-1)

def reference(inputs, segments, positions, ln_gain, ln_bias, w_qkv, b_qkv, w_dense, b_dense, w_fc1, b_fc1, w_fc2, b_fc2, cotangent):
    scaling = HEAD_DIM ** (-0.5)
    pack_count = TOKENS // SEQ
    seq_order = jnp.arange(SEQ, dtype=jnp.int32)

    def attend(operands):
        queries, key_heads, value_heads, segment_block = operands
        scores = low_back(jnp.einsum('qhd,khd->hqk', queries, key_heads, precision=lax.Precision.HIGHEST) * scaling)
        allowed = (segment_block[:, None] == segment_block[None, :]) & (seq_order[None, :] <= seq_order[:, None])
        masked = jnp.where(allowed[None], scores, -1e+30)
        row_max = lax.optimization_barrier(jnp.max(masked, axis=-1, keepdims=True))
        exponent = jnp.exp(masked - row_max)
        attention = low(exponent / lax.optimization_barrier(jnp.sum(exponent, axis=-1, keepdims=True)))
        return jnp.einsum('hqk,khd->qhd', attention, value_heads, precision=lax.Precision.HIGHEST)

    def packed(array):
        return array.reshape((pack_count, SEQ) + array.shape[1:])

    def forward(inputs_wide, norm_gain, norm_shift, weight_qkv, bias_qkv, weight_dense, bias_dense, weight_fc1, bias_fc1, weight_fc2, bias_fc2):
        average = lax.optimization_barrier(jnp.mean(inputs_wide, axis=-1, keepdims=True))
        centred = inputs_wide - average
        spread = lax.optimization_barrier(jnp.mean(centred * centred, axis=-1, keepdims=True))
        normed = low(centred * lax.rsqrt(spread + 1e-05) * norm_gain + norm_shift)
        projected = low_back(matmul(normed, weight_qkv) + bias_qkv)
        queries = low(rotary(projected[:, :D].reshape(TOKENS, HEADS, HEAD_DIM), positions))
        key_part = low(rotary(projected[:, D:2 * D].reshape(TOKENS, HEADS, HEAD_DIM), positions))
        value_part = low(projected[:, 2 * D:].reshape(TOKENS, HEADS, HEAD_DIM))
        attended = lax.map(jax.checkpoint(attend), (packed(queries), packed(key_part), packed(value_part), packed(segments)))
        attended = low_back(low(attended.reshape(TOKENS, D)))
        pre_act = low_back(matmul(normed, weight_fc1) + bias_fc1)
        activation = low(jax.nn.gelu(pre_act, approximate=True))
        return inputs_wide + matmul(attended, weight_dense) + bias_dense + matmul(activation, weight_fc2) + bias_fc2
    primals = (inputs.astype(jnp.float32), ln_gain.astype(jnp.float32), ln_bias.astype(jnp.float32), w_qkv.astype(jnp.float32), b_qkv.astype(jnp.float32), w_dense.astype(jnp.float32), b_dense.astype(jnp.float32), w_fc1.astype(jnp.float32), b_fc1.astype(jnp.float32), w_fc2.astype(jnp.float32), b_fc2.astype(jnp.float32))
    block_out, pullback = jax.vjp(forward, *primals)
    gradients = pullback(cotangent.astype(jnp.float32))
    return (block_out, gradients[0], gradients[1], gradients[2], gradients[3], gradients[4], gradients[5], gradients[6], gradients[7], gradients[8], gradients[9], gradients[10])
```

```python
import functools

import jax
import jax.numpy as jnp
from jax import lax
from jax.experimental import pallas as pl
from jax.experimental.pallas import tpu as pltpu
from jax.sharding import PartitionSpec as P

HEAD_DIM = 64
ROT = 32
SEQ = 1024
PAIR = 2 * HEAD_DIM
BF = jnp.bfloat16
F32 = jnp.float32


def ring(array, axis, distance):
    size = lax.axis_size(axis)
    return lax.ppermute(array, axis, [(i, (i + distance) % size) for i in range(size)])


def swap(array, axis, bit):
    size = lax.axis_size(axis)
    return lax.ppermute(array, axis, [(i, i ^ bit) for i in range(size)])


def contract_rows(left_side, right_side):
    return lax.dot_general(
        left_side, right_side, (((0,), (0,)), ((), ())), preferred_element_type=F32
    )


def times_transpose(left_side, right_side):
    return lax.dot_general(
        left_side, right_side, (((1,), (1,)), ((), ())), preferred_element_type=F32
    )


def times(left_side, right_side):
    return jnp.dot(left_side, right_side, preferred_element_type=F32)


def gelu_tanh(pre_act):
    return jax.nn.gelu(pre_act, approximate=True)


def ring_gather(block, place):
    size = lax.axis_size("shard")
    whole = jnp.zeros((size,) + block.shape, block.dtype)
    held = block
    for hop in range(size):
        whole = lax.dynamic_update_index_in_dim(whole, held, (place - hop) % size, 0)
        if hop < size - 1:
            held = ring(held, "shard", 1)
    return whole.reshape((size * block.shape[0],) + block.shape[1:])


def exchange(pick, place):
    size = lax.axis_size("shard")
    own = pick(place)
    whole = jnp.zeros((size,) + own.shape, own.dtype)
    whole = lax.dynamic_update_index_in_dim(whole, own, place, 0)
    for hop in range(1, size):
        came = ring(pick((place + hop) % size), "shard", hop)
        whole = lax.dynamic_update_index_in_dim(whole, came, (place - hop) % size, 0)
    return whole


def scatter_sum(pick, place):
    size = lax.axis_size("shard")
    total = pick(place).astype(F32)
    for hop in range(1, size):
        total = total + ring(pick((place + hop) % size), "shard", hop).astype(F32)
    return total


def rep_sum(values):
    bit = 1
    while bit < lax.axis_size("rep"):
        values = values + swap(values, "rep", bit)
        bit *= 2
    return values


def attention_kernel(
    block,
    proj_ref,
    bias_ref,
    turn_ref,
    datt_ref,
    start_ref,
    att_ref,
    dproj_ref,
    bsum_ref,
    dq_ref,
    dk_ref,
    dv_ref,
):
    rows = proj_ref.shape[0]
    scaling = HEAD_DIM ** (-0.5)
    cosine = turn_ref[0]
    minus = turn_ref[1]
    plus = turn_ref[2]

    def turned(u):
        return (
            u * cosine
            + pltpu.roll(u, PAIR - ROT // 2, 1) * minus
            + pltpu.roll(u, ROT // 2, 1) * plus
        )

    def turned_back(u):
        return (
            u * cosine
            - pltpu.roll(u, PAIR - ROT // 2, 1) * minus
            - pltpu.roll(u, ROT // 2, 1) * plus
        )

    query = turned(proj_ref[:, :PAIR] + bias_ref[:, :PAIR]).astype(BF) * scaling
    query = query.astype(BF)
    key = turned(proj_ref[:, PAIR : 2 * PAIR] + bias_ref[:, PAIR : 2 * PAIR]).astype(BF)
    value = (proj_ref[:, 2 * PAIR :] + bias_ref[:, 2 * PAIR :]).astype(BF)
    d_att = datt_ref[...]
    start = start_ref[0]
    dk_ref[...] = jnp.zeros_like(dk_ref)
    dv_ref[...] = jnp.zeros_like(dv_ref)
    for head in range(2):
        lanes = slice(head * HEAD_DIM, (head + 1) * HEAD_DIM)
        key_h, value_h = key[:, lanes], value[:, lanes]
        key_t, value_t = key_h.T, value_h.T
        for part in range(rows // block):
            own = slice(part * block, (part + 1) * block)
            length = (part + 1) * block
            query_p = query[own, lanes]
            d_att_p = d_att[own, lanes]
            scores = times_transpose(key_h[:length], query_p)
            place = lax.broadcasted_iota(jnp.int32, (length, block), 0)
            asker = lax.broadcasted_iota(jnp.int32, (length, block), 1) + part * block
            allowed = (place >= start[:, own]) & (place <= asker)
            scores = jnp.where(allowed, scores, -1e30)
            exponent = jnp.exp(scores - jnp.max(scores, axis=0, keepdims=True))
            softmax = exponent * (1.0 / jnp.sum(exponent, axis=0, keepdims=True))
            attention = softmax.astype(BF)
            att_ref[own, lanes] = times(value_t[:, :length], attention).T.astype(BF)
            d_attention = times_transpose(value_h[:length], d_att_p)
            dv_ref[:length, lanes] += times(attention, d_att_p)
            weighted = softmax * d_attention
            d_scores = (
                weighted - softmax * jnp.sum(weighted, axis=0, keepdims=True)
            ).astype(BF)
            dq_ref[own, lanes] = times(key_t[:, :length], d_scores).T * scaling
            dk_ref[:length, lanes] += times(d_scores, query_p)
    d_query = turned_back(dq_ref[...]).astype(BF)
    d_key = turned_back(dk_ref[...]).astype(BF)
    d_value = dv_ref[...].astype(BF)
    for at, piece in enumerate((d_query, d_key, d_value)):
        lanes = slice(at * PAIR, (at + 1) * PAIR)
        dproj_ref[:, lanes] = piece
        bsum_ref[0, :, lanes] = jnp.sum(piece.astype(F32), axis=0, keepdims=True)


def attention(projected, bias, turns, d_attended, start):
    tokens, width = projected.shape
    pairs, seqs = width // (3 * PAIR), tokens // SEQ
    block = min(256, SEQ)
    return pl.pallas_call(
        functools.partial(attention_kernel, block),
        grid=(seqs, pairs),
        in_specs=[
            pl.BlockSpec((SEQ, 3 * PAIR), lambda s, p: (s, p)),
            pl.BlockSpec((1, 3 * PAIR), lambda s, p: (0, p)),
            pl.BlockSpec((3, SEQ, PAIR), lambda s, p: (0, s, 0)),
            pl.BlockSpec((SEQ, PAIR), lambda s, p: (s, p)),
            pl.BlockSpec((1, 1, SEQ), lambda s, p: (s, 0, 0)),
        ],
        out_specs=[
            pl.BlockSpec((SEQ, PAIR), lambda s, p: (s, p)),
            pl.BlockSpec((SEQ, 3 * PAIR), lambda s, p: (s, p)),
            pl.BlockSpec((1, 1, 3 * PAIR), lambda s, p: (s, 0, p)),
        ],
        out_shape=[
            jax.ShapeDtypeStruct((tokens, pairs * PAIR), BF),
            jax.ShapeDtypeStruct((tokens, width), BF),
            jax.ShapeDtypeStruct((seqs, 1, width), F32),
        ],
        scratch_shapes=[pltpu.VMEM((SEQ, PAIR), F32)] * 3,
        compiler_params=pltpu.CompilerParams(vmem_limit_bytes=48 * 2**20),
        name="attention",
    )(projected, bias, turns, d_attended, start)


def shards(
    inputs,
    segments,
    positions,
    ln_gain,
    ln_bias,
    w_qkv,
    b_qkv,
    w_dense,
    b_dense,
    w_fc1,
    b_fc1,
    w_fc2,
    b_fc2,
    cotangent,
):
    reps, group = lax.axis_size("rep"), lax.axis_size("shard")
    rep, place = lax.axis_index("rep"), lax.axis_index("shard")
    tokens, width = inputs.shape
    rows = width // group
    slab = rows // reps
    hidden = w_fc1.shape[1] // group
    heads_width = width // group
    pairs = heads_width // PAIR

    slab_fc1 = lax.dynamic_slice_in_dim(w_fc1, rep * slab, slab, 0)
    slab_qkv = lax.dynamic_slice_in_dim(w_qkv, rep * slab, slab, 0)

    def fc1_for(owner):
        return lax.dynamic_slice_in_dim(slab_fc1, owner * hidden, hidden, 1)

    def qkv_for(owner):
        split = slab_qkv.reshape(slab, 3, group, pairs, PAIR)
        return (
            lax.dynamic_index_in_dim(split, owner, 2, keepdims=False)
            .transpose(0, 2, 1, 3)
            .reshape(slab, 3 * heads_width)
        )

    fc1_cols = lax.all_gather(
        exchange(fc1_for, place).reshape(group * slab, hidden), "rep", axis=0, tiled=True
    )
    qkv_cols = lax.all_gather(
        exchange(qkv_for, place).reshape(group * slab, 3 * heads_width), "rep", axis=0, tiled=True
    )

    small = jnp.concatenate([ln_gain, ln_bias, b_qkv, b_dense + b_fc2])
    small = lax.all_gather(small, "shard", axis=0)
    all_positions = lax.all_gather(positions, "shard", axis=0, tiled=True)
    gain = small[:, :rows].reshape(width)
    shift = small[:, rows : 2 * rows].reshape(width)
    bias_qkv = (
        lax.dynamic_index_in_dim(
            small[:, 2 * rows : 5 * rows].reshape(3, group, pairs, PAIR), place, 1, keepdims=False
        )
        .transpose(1, 0, 2)
        .reshape(1, 3 * heads_width)
    )
    bias_out = small[:, 5 * rows :].reshape(width)

    inputs_wide = inputs.astype(F32)
    average = jnp.mean(inputs_wide, axis=-1, keepdims=True)
    centred = inputs_wide - average
    spread = jnp.mean(centred * centred, axis=-1, keepdims=True)
    inverse = lax.rsqrt(spread + 1e-05)
    normed = (centred * inverse * gain + shift).astype(BF)
    normed = normed.reshape(tokens, group, reps, slab).transpose(0, 2, 1, 3).reshape(tokens, width)
    normed_all = ring_gather(normed, place)
    cot_all = ring_gather(cotangent, place)

    frequency = 10000.0 ** (-(jnp.arange(ROT // 2, dtype=F32) * 2.0) / ROT)
    angles = all_positions.astype(F32)[:, None] * frequency[None, :]
    cosine, sine = jnp.cos(angles), jnp.sin(angles)
    none = jnp.zeros_like(sine)
    still = jnp.zeros((sine.shape[0], HEAD_DIM - ROT), F32)
    turns = jnp.stack(
        [
            jnp.concatenate([cosine, cosine, still + 1.0] * 2, axis=1),
            jnp.concatenate([-sine, none, still] * 2, axis=1),
            jnp.concatenate([none, sine, still] * 2, axis=1),
        ]
    )
    start = jnp.arange(SEQ, dtype=jnp.int32)[None, None] - all_positions.reshape(-1, 1, SEQ)

    pre_act = times(normed_all, fc1_cols) + b_fc1
    activation = gelu_tanh(pre_act).astype(BF)
    d_activation = times_transpose(cot_all, w_fc2)
    d_pre = jax.vjp(gelu_tanh, pre_act)[1](d_activation)[0].astype(BF)
    grad_fc2 = contract_rows(activation, cot_all).astype(BF)
    grad_fc1 = contract_rows(normed_all, d_pre).astype(BF)

    projected = times(normed_all, qkv_cols)
    d_attended = times_transpose(cot_all, w_dense).astype(BF)
    attended, d_projected, d_bias_qkv = attention(projected, bias_qkv, turns, d_attended, start)
    grad_qkv = contract_rows(normed_all, d_projected).astype(BF)
    grad_dense = contract_rows(attended, cot_all).astype(BF)

    out_part = (times(attended, w_dense) + times(activation, w_fc2)).astype(BF)
    d_normed_part = (
        times_transpose(d_projected, qkv_cols) + times_transpose(d_pre, fc1_cols)
    ).astype(BF)

    def rows_of(array):
        return lambda owner: lax.dynamic_slice_in_dim(array, owner * tokens, tokens, 0)

    block_out = inputs_wide + scatter_sum(rows_of(out_part), place) + bias_out
    d_normed = scatter_sum(rows_of(d_normed_part), place)
    d_normed = (
        d_normed.reshape(tokens, reps, group, slab).transpose(0, 2, 1, 3).reshape(tokens, width)
    )
    xhat = centred * inverse
    d_gain = jnp.sum(d_normed * xhat, axis=0)
    d_shift = jnp.sum(d_normed, axis=0)
    scaled = d_normed * gain
    grad_inputs = cotangent.astype(F32) + inverse * (
        scaled
        - jnp.mean(scaled, axis=-1, keepdims=True)
        - xhat * jnp.mean(scaled * xhat, axis=-1, keepdims=True)
    )

    def reduced(array):
        return lax.psum_scatter(array, "rep", scatter_dimension=0, tiled=True)

    def spread_out(array):
        return lax.all_gather(array, "rep", axis=0, tiled=True).astype(F32)

    def slab_of(array):
        return lambda owner: lax.dynamic_slice_in_dim(array, owner * slab, slab, 0)

    fc2_total = spread_out(reduced(grad_fc2))
    fc1_slab = exchange(slab_of(reduced(grad_fc1)), place)
    fc1_total = spread_out(fc1_slab.transpose(1, 0, 2).reshape(slab, group * hidden))
    dense_total = spread_out(reduced(grad_dense))
    qkv_slab = exchange(slab_of(reduced(grad_qkv)), place)
    qkv_total = spread_out(
        qkv_slab.reshape(group, slab, pairs, 3, PAIR)
        .transpose(1, 3, 0, 2, 4)
        .reshape(slab, 3 * width)
    )

    d_bias_qkv = jnp.sum(d_bias_qkv[:, 0], axis=0).reshape(pairs, 3, PAIR).transpose(1, 0, 2)
    d_bias_all = jnp.zeros((3, group, pairs, PAIR), F32)
    d_bias_all = lax.dynamic_update_index_in_dim(d_bias_all, d_bias_qkv, place, 1)
    early = jnp.concatenate(
        [
            d_bias_all.reshape(group, 3 * rows),
            jnp.sum(cotangent.astype(F32), axis=0).reshape(group, rows),
        ],
        axis=1,
    )
    pick = lambda array: lambda owner: lax.dynamic_index_in_dim(array, owner, 0, keepdims=False)
    early = scatter_sum(pick(early), place)
    early = rep_sum(jnp.concatenate([early, jnp.sum(d_pre.astype(F32), axis=0)]))
    late = jnp.concatenate([d_gain.reshape(group, rows), d_shift.reshape(group, rows)], axis=1)
    late = rep_sum(scatter_sum(pick(late), place))
    cot_total = early[3 * rows : 4 * rows]
    return (
        block_out,
        grad_inputs,
        late[:rows],
        late[rows:],
        qkv_total,
        early[: 3 * rows],
        dense_total,
        cot_total,
        fc1_total,
        early[4 * rows :],
        fc2_total,
        cot_total,
    )


def solution(mesh):
    both, shard = P(("rep", "shard")), P("shard")
    wide, held = P(("rep", "shard"), None), P("shard", None)
    return jax.shard_map(
        shards,
        mesh=mesh,
        in_specs=(
            wide, both, both, shard, shard, held, shard, held, shard, held, shard, held, shard, wide
        ),
        out_specs=(
            wide, wide, shard, shard, held, shard, held, shard, held, shard, held, shard
        ),
        check_vma=False,
    )
```

```python
import functools

import jax
import jax.numpy as jnp
from jax import lax
from jax.experimental import pallas as pl
from jax.experimental.pallas import tpu as pltpu
from jax.sharding import PartitionSpec as P

HEAD_DIM = 64
ROT = 32
SEQ = 1024
PAIR = 2 * HEAD_DIM
BF = jnp.bfloat16
F32 = jnp.float32


def ring(array, axis, distance):
    size = lax.axis_size(axis)
    return lax.ppermute(array, axis, [(i, (i + distance) % size) for i in range(size)])


def swap(array, axis, bit):
    size = lax.axis_size(axis)
    return lax.ppermute(array, axis, [(i, i ^ bit) for i in range(size)])


def contract_rows(left_side, right_side):
    return lax.dot_general(
        left_side, right_side, (((0,), (0,)), ((), ())), preferred_element_type=F32
    )


def times_transpose(left_side, right_side):
    return lax.dot_general(
        left_side, right_side, (((1,), (1,)), ((), ())), preferred_element_type=F32
    )


def times(left_side, right_side):
    return jnp.dot(left_side, right_side, preferred_element_type=F32)


def gelu_tanh(pre_act):
    return jax.nn.gelu(pre_act, approximate=True)


class Order:
    def __init__(self):
        self.last = None

    def step(self, work, *operands):
        if self.last is not None:
            *operands, _ = lax.optimization_barrier((*operands, self.last))
        result = work(*operands)
        self.last = jax.tree.leaves(result)[0]
        return result

    def hold(self, array):
        return self.step(lambda a: a, array)


def after(array, *others):
    return lax.optimization_barrier((array, *others))[0]


def placed(pieces, place, axis):
    size, length = len(pieces), pieces[0].shape[axis]
    shape = list(pieces[0].shape)
    shape[axis] *= size
    whole = jnp.zeros(shape, pieces[0].dtype)
    for hop, piece in enumerate(pieces):
        whole = lax.dynamic_update_slice_in_dim(
            whole, piece, (place - hop) % size * length, axis
        )
    return whole


def direct(pick, place):
    size = lax.axis_size("shard")
    return [pick(place)] + [
        ring(pick((place + hop) % size), "shard", hop) for hop in range(1, size)
    ]


def doubled(row, place):
    bit = 1
    while bit < lax.axis_size("shard"):
        other = swap(row, "shard", bit)
        upper = (place & bit) > 0
        row = jnp.concatenate([jnp.where(upper, other, row), jnp.where(upper, row, other)])
        bit *= 2
    return row


def rep_sum(values):
    bit = 1
    while bit < lax.axis_size("rep"):
        values = values + swap(values, "rep", bit)
        bit *= 2
    return values


class Halving:
    def __init__(self, rep, array, parts):
        count = lax.axis_size("rep").bit_length() - 2
        self.rep = rep
        array = array.reshape((2,) * count + (array.shape[0] >> count,) + array.shape[1:])
        rows = array.shape[count] // parts
        self.arrays = [array] * parts
        self.spans = [(part * rows, rows) for part in range(parts)]
        bits = list(range(count, 0, -1))
        self.bits = [list(bits) for _ in range(parts)]
        self.todo = [
            bits[::-1][part % count :] + bits[::-1][: part % count] for part in range(parts)
        ]

    def pick(self, part, array, mine):
        axis = self.bits[part].index(self.todo[part][0])
        bit = (self.rep >> self.todo[part][0]) & 1
        starts, sizes = [0] * array.ndim, list(array.shape)
        starts[axis], sizes[axis] = (bit if mine else 1 - bit), 1
        starts[len(self.bits[part])], sizes[len(self.bits[part])] = self.spans[part]
        half = lax.dynamic_slice(array, starts, sizes)
        return half.reshape(half.shape[:axis] + half.shape[axis + 1 :])

    def outgoing(self, *arrays):
        return tuple(self.pick(part, array, False) for part, array in enumerate(arrays))

    def added(self, *operands):
        count = len(operands) // 2
        return tuple(
            (self.pick(part, operands[part], True).astype(F32) + operands[count + part].astype(F32))
            .astype(BF)
            for part in range(count)
        )

    def send(self, line):
        sent = line.step(self.outgoing, *self.arrays)
        self.came = [
            swap(piece, "rep", 1 << todo[0]) for piece, todo in zip(sent, self.todo)
        ]

    def take(self, line):
        self.arrays = line.step(self.added, *self.arrays, *self.came)
        for part, todo in enumerate(self.todo):
            self.bits[part].remove(todo[0])
            self.todo[part] = todo[1:]
            self.spans[part] = (0, self.spans[part][1])

    def further(self, line):
        self.take(line)
        self.send(line)

    def end(self, line):
        while len(self.todo[0]) > 1:
            self.further(line)
        self.take(line)
        return jnp.concatenate(self.arrays, axis=0)


def grad_kernel(which_ref, left_ref, right_ref, *refs):
    total = contract_rows(left_ref[...], right_ref[...])
    if len(refs) > 1:
        total = total + refs[0][...].astype(F32)
    refs[-1][...] = total.astype(BF)


def half_grads(left, right, which, reps, by_rows, came=None):
    tokens, height = left.shape
    length = right.shape[1]
    if by_rows:
        height //= reps
    else:
        length //= reps
    if (height if by_rows else length) % 128:
        side = left if by_rows else right
        split = side.reshape(tokens, reps // 2, 2, -1)
        split = lax.dynamic_index_in_dim(split, which, 2, keepdims=False)
        total = lax.dot_general(
            split if by_rows else left,
            right if by_rows else split,
            (((0,), (0,)), ((), ())),
            preferred_element_type=F32,
        )
        if not by_rows:
            total = total.transpose(1, 0, 2)
        total = total.reshape(-1, length)
        return (total if came is None else total + came.astype(F32)).astype(BF)
    chosen = lambda b, w: (0, 2 * b + w[0])
    fixed = lambda b, w: (0, 0)
    block = pl.BlockSpec((height, length), lambda b, w: (b, 0))
    return pl.pallas_call(
        grad_kernel,
        grid_spec=pltpu.PrefetchScalarGridSpec(
            num_scalar_prefetch=1,
            grid=(reps // 2,),
            in_specs=[
                pl.BlockSpec((tokens, height), chosen if by_rows else fixed),
                pl.BlockSpec((tokens, length), fixed if by_rows else chosen),
            ]
            + ([] if came is None else [block]),
            out_specs=block,
        ),
        out_shape=jax.ShapeDtypeStruct((reps // 2 * height, length), BF),
        compiler_params=pltpu.CompilerParams(vmem_limit_bytes=48 * 2**20),
        name="half_grads",
    )(which.reshape(1), left, right, *([] if came is None else [came]))


def ln_forward_kernel(reps, group, x_ref, gain_ref, shift_ref, out_ref):
    x = x_ref[...].astype(F32)
    centred = x - jnp.mean(x, axis=-1, keepdims=True)
    spread = jnp.mean(centred * centred, axis=-1, keepdims=True)
    normed = (centred * lax.rsqrt(spread + 1e-05)) * gain_ref[...] + shift_ref[...]
    slab = x.shape[1] // (reps * group)
    out_ref[...] = jnp.concatenate(
        [
            normed[:, (g * reps + r) * slab : (g * reps + r + 1) * slab]
            for r in range(reps)
            for g in range(group)
        ],
        axis=1,
    ).astype(BF)


def ln_forward(inputs, gain, shift, reps, group):
    tokens, width = inputs.shape
    return pl.pallas_call(
        functools.partial(ln_forward_kernel, reps, group),
        out_shape=jax.ShapeDtypeStruct((tokens, width), BF),
        compiler_params=pltpu.CompilerParams(vmem_limit_bytes=48 * 2**20),
        name="ln_forward",
    )(inputs, gain.reshape(1, width), shift.reshape(1, width))


def ln_backward_kernel(reps, group, *refs):
    x_ref, gain_ref, cot_ref, *parts, out_ref, sums_ref = refs
    x = x_ref[...].astype(F32)
    centred = x - jnp.mean(x, axis=-1, keepdims=True)
    spread = jnp.mean(centred * centred, axis=-1, keepdims=True)
    inverse = lax.rsqrt(spread + 1e-05)
    xhat = centred * inverse
    mixed = parts[0][...].astype(F32)
    for part in parts[1:]:
        mixed = mixed + part[...].astype(F32)
    slab = x.shape[1] // (reps * group)
    d_normed = jnp.concatenate(
        [
            mixed[:, (r * group + g) * slab : (r * group + g + 1) * slab]
            for g in range(group)
            for r in range(reps)
        ],
        axis=1,
    )
    sums_ref[0:1] = jnp.sum(d_normed * xhat, axis=0, keepdims=True)
    sums_ref[1:2] = jnp.sum(d_normed, axis=0, keepdims=True)
    scaled = d_normed * gain_ref[...]
    out_ref[...] = cot_ref[...].astype(F32) + inverse * (
        scaled
        - jnp.mean(scaled, axis=-1, keepdims=True)
        - xhat * jnp.mean(scaled * xhat, axis=-1, keepdims=True)
    )


def ln_backward(inputs, gain, cotangent, parts, reps, group):
    tokens, width = inputs.shape
    return pl.pallas_call(
        functools.partial(ln_backward_kernel, reps, group),
        out_shape=[
            jax.ShapeDtypeStruct((tokens, width), F32),
            jax.ShapeDtypeStruct((2, width), F32),
        ],
        compiler_params=pltpu.CompilerParams(vmem_limit_bytes=56 * 2**20),
        name="ln_backward",
    )(inputs, gain.reshape(1, width), cotangent, *parts)


def attention_kernel(block, *refs):
    q_ref, k_ref, v_ref, turn_ref, datt_ref, start_ref = refs[:6]
    att_ref, dproj_ref, bsum_ref, dq_ref, dk_ref, dv_ref = refs[-6:]
    rows = q_ref.shape[0]
    scaling = HEAD_DIM ** (-0.5)
    stage = pl.program_id(1)

    @pl.when(stage == 0)
    def _():
        cosine = turn_ref[0]
        minus = turn_ref[1]
        plus = turn_ref[2]

        def turned(u, sign):
            return (
                u * cosine
                + sign * (pltpu.roll(u, PAIR - ROT // 2, 1) * minus)
                + sign * (pltpu.roll(u, ROT // 2, 1) * plus)
            )

        query = turned(q_ref[...], 1.0).astype(BF) * scaling
        query = query.astype(BF)
        key = turned(k_ref[...], 1.0).astype(BF)
        value = v_ref[...].astype(BF)
        d_att = datt_ref[...]
        start = start_ref[0]
        dk_ref[...] = jnp.zeros_like(dk_ref)
        dv_ref[...] = jnp.zeros_like(dv_ref)
        for head in range(2):
            lanes = slice(head * HEAD_DIM, (head + 1) * HEAD_DIM)
            key_h, value_h = key[:, lanes], value[:, lanes]
            key_t, value_t = key_h.T, value_h.T
            for part in range(rows // block):
                own = slice(part * block, (part + 1) * block)
                length = (part + 1) * block
                query_p = query[own, lanes]
                d_att_p = d_att[own, lanes]
                scores = times_transpose(key_h[:length], query_p)
                place = lax.broadcasted_iota(jnp.int32, (length, block), 0)
                asker = lax.broadcasted_iota(jnp.int32, (length, block), 1) + part * block
                allowed = (place >= start[:, own]) & (place <= asker)
                scores = jnp.where(allowed, scores, -1e30)
                exponent = jnp.exp(scores - jnp.max(scores, axis=0, keepdims=True))
                softmax = exponent * (1.0 / jnp.sum(exponent, axis=0, keepdims=True))
                attention = softmax.astype(BF)
                att_ref[own, lanes] = times(value_t[:, :length], attention).T.astype(BF)
                d_attention = times_transpose(value_h[:length], d_att_p)
                dv_ref[:length, lanes] += times(attention, d_att_p)
                weighted = softmax * d_attention
                d_scores = (
                    weighted - softmax * jnp.sum(weighted, axis=0, keepdims=True)
                ).astype(BF)
                dq_ref[own, lanes] = times(key_t[:, :length], d_scores).T * scaling
                dk_ref[:length, lanes] += times(d_scores, query_p)
        dq_ref[...] = turned(dq_ref[...], -1.0)
        dk_ref[...] = turned(dk_ref[...], -1.0)

    for at, held in enumerate((dq_ref, dk_ref, dv_ref)):

        @pl.when(stage == at)
        def _(held=held):
            piece = held[...].astype(BF)
            dproj_ref[...] = piece
            bsum_ref[0] = jnp.sum(piece.astype(F32), axis=0, keepdims=True)


def attention(projected, turns, d_attended, start, pair, before):
    tokens, width = projected.shape
    pairs, seqs = width // (3 * PAIR), tokens // SEQ
    block = min(256, SEQ)
    wide = lambda at: pl.BlockSpec((SEQ, PAIR), lambda s, j: (s, at * pairs + pair))
    aliases = {6 + k: k for k in range(3)} if before else {}
    return pl.pallas_call(
        functools.partial(attention_kernel, block),
        grid=(seqs, 3),
        in_specs=[
            wide(0),
            wide(1),
            wide(2),
            pl.BlockSpec((3, SEQ, PAIR), lambda s, j: (0, s, 0)),
            pl.BlockSpec((SEQ, PAIR), lambda s, j: (s, pair)),
            pl.BlockSpec((1, 1, SEQ), lambda s, j: (s, 0, 0)),
        ]
        + [pl.BlockSpec(memory_space=pl.ANY)] * len(before),
        out_specs=[
            pl.BlockSpec((SEQ, PAIR), lambda s, j: (s, pair)),
            pl.BlockSpec((SEQ, PAIR), lambda s, j: (s, j * pairs + pair)),
            pl.BlockSpec((1, 1, PAIR), lambda s, j: (s, 0, j * pairs + pair)),
        ],
        out_shape=[
            jax.ShapeDtypeStruct((tokens, pairs * PAIR), BF),
            jax.ShapeDtypeStruct((tokens, width), BF),
            jax.ShapeDtypeStruct((seqs, 1, width), F32),
        ],
        scratch_shapes=[pltpu.VMEM((SEQ, PAIR), F32)] * 3,
        input_output_aliases=aliases,
        compiler_params=pltpu.CompilerParams(vmem_limit_bytes=48 * 2**20),
        name="attention",
    )(projected, projected, projected, turns, d_attended, start, *before)


def shards(
    inputs,
    segments,
    positions,
    ln_gain,
    ln_bias,
    w_qkv,
    b_qkv,
    w_dense,
    b_dense,
    w_fc1,
    b_fc1,
    w_fc2,
    b_fc2,
    cotangent,
):
    reps, group = lax.axis_size("rep"), lax.axis_size("shard")
    rep, place = lax.axis_index("rep"), lax.axis_index("shard")
    core = rep & 1
    tokens, width = inputs.shape
    rows = width // group
    slab = rows // reps
    hidden = w_fc1.shape[1] // group
    pairs = rows // PAIR

    line = Order()
    owners = [(place + hop) % group for hop in range(group)]

    def sends(pieces):
        return [pieces[0]] + [ring(piece, "shard", k + 1) for k, piece in enumerate(pieces[1:])]

    def gathered(array):
        return lax.all_gather(array, "rep", axis=0, tiled=True)

    fc1_pieces = sends(
        line.step(
            lambda w: tuple(
                lax.dynamic_slice(w, (rep * slab, owner * hidden), (slab, hidden))
                for owner in owners
            ),
            w_fc1,
        )
    )
    small = jnp.concatenate(
        [ln_gain, ln_bias, b_qkv, b_dense + b_fc2, positions.astype(F32)]
    ).reshape(1, -1)
    small = doubled(line.hold(small), place)
    gain = small[:, :rows].reshape(width)
    shift = small[:, rows : 2 * rows].reshape(width)
    bias_qkv = lax.dynamic_slice_in_dim(
        small[:, 2 * rows : 5 * rows].reshape(3, width), place * rows, rows, 1
    ).reshape(3 * rows)
    bias_out = small[:, 5 * rows : 6 * rows].reshape(width)
    all_positions = small[:, 6 * rows :].reshape(group * tokens)

    normed = [line.step(lambda *o: ln_forward(*o, reps, group), inputs, gain, shift)]
    normed.append(ring(normed[0], "shard", 1))
    fc1_cols = gathered(line.step(lambda *p: placed(p, place, 0), *fc1_pieces))
    qkv_pieces = sends(
        line.step(
            lambda w: tuple(
                jnp.concatenate(
                    [
                        lax.dynamic_slice(w, (rep * slab, at * width + owner * rows), (slab, rows))
                        for at in range(3)
                    ],
                    axis=1,
                )
                for owner in owners
            ),
            w_qkv,
        )
    )
    qkv_cols = gathered(line.step(lambda *p: placed(p, place, 0), *qkv_pieces))

    def tables(all_positions):
        frequency = 10000.0 ** (-(jnp.arange(ROT // 2, dtype=F32) * 2.0) / ROT)
        angles = frequency[:, None] * all_positions[None, :]
        cosine, sine = jnp.cos(angles).T, jnp.sin(angles).T
        none = jnp.zeros_like(sine)
        still = jnp.zeros((sine.shape[0], HEAD_DIM - ROT), F32)
        return jnp.stack(
            [
                jnp.concatenate([cosine, cosine, still + 1.0] * 2, axis=1),
                jnp.concatenate([-sine, none, still] * 2, axis=1),
                jnp.concatenate([none, sine, still] * 2, axis=1),
            ]
        )

    def start_whole(block):
        whole = jnp.zeros((group * tokens, width), block.dtype)
        return lax.dynamic_update_slice_in_dim(whole, block, place * tokens, 0)

    def put(hop):
        return lambda whole, block: lax.dynamic_update_slice_in_dim(
            whole, block, (place - hop) % group * tokens, 0
        )

    for hop in range(1, group):
        normed[hop] = line.hold(normed[hop])
        if hop + 1 < group:
            normed.append(ring(normed[hop], "shard", 1))
        else:
            cots = [line.hold(cotangent)]
            cots.append(ring(cots[0], "shard", 1))
        if hop == 1:
            turns = line.step(tables, all_positions)
            normed_all = line.step(start_whole, normed[0])
        normed_all = line.step(put(hop), normed_all, normed[hop])
    start = (
        jnp.arange(SEQ, dtype=jnp.int32)[None, None]
        - all_positions.astype(jnp.int32).reshape(-1, 1, SEQ)
    )

    def feed_forward(normed_all, fc1_cols, bias):
        pre_act = times(normed_all, fc1_cols) + bias
        root = (2.0 / jnp.pi) ** 0.5
        square = pre_act * pre_act
        curve = jnp.tanh(root * pre_act * (1.0 + 0.044715 * square))
        activation = (0.5 * pre_act * (1.0 + curve)).astype(BF)
        slope = (
            0.5 * (1.0 + curve)
            + 0.5 * pre_act * (1.0 - curve * curve) * root * (1.0 + 3 * 0.044715 * square)
        ).astype(BF)
        return activation, slope

    for hop in range(1, group):
        if hop == 1:
            activation, slope = line.step(feed_forward, normed_all, fc1_cols, b_fc1)
        if hop == 2:
            projected = line.step(
                lambda a, b, c: times(a, b) + c, normed_all, qkv_cols, bias_qkv
            )
        cots[hop] = line.hold(cots[hop])
        if hop + 1 < group:
            cots.append(ring(cots[hop], "shard", 1))
        if hop == 1:
            cot_all = line.step(start_whole, cots[0])
        cot_all = line.step(put(hop), cot_all, cots[hop])

    def grad(left, right, by_rows=True):
        sent = line.step(
            lambda a, b: half_grads(a, b, 1 - core, reps, by_rows), left, right
        )
        return swap(sent, "rep", 1)

    def grad_sum(left, right, came, parts, by_rows=True):
        own = line.step(
            lambda a, b, c: half_grads(a, b, core, reps, by_rows, c), left, right, came
        )
        halving = Halving(rep, own, parts)
        halving.send(line)
        return halving

    def attend(pair, results):
        return line.step(
            lambda p, d, *r: attention(p, turns, d, start, pair, tuple(r)),
            projected,
            d_attended,
            *results,
        )

    def cut(array, count, owners):
        return line.step(
            lambda a: tuple(
                lax.dynamic_slice_in_dim(a, owner * count, count, 0) for owner in owners
            ),
            array,
        )

    class Passing:
        def __init__(self, array):
            self.own = cut(array, tokens, [(place - hop) % group for hop in range(1, group + 1)])
            self.hop = 1
            self.came = ring(self.own[0], "shard", 1)

        def further(self):
            sent = line.step(
                lambda a, b: (a.astype(F32) + b.astype(F32)).astype(BF),
                self.own[self.hop],
                self.came,
            )
            self.hop += 1
            self.came = ring(sent, "shard", 1)

        def end(self):
            while self.hop + 1 < group:
                self.further()
            return self.own[-1], self.came

    fc2_came = grad(activation, cot_all)
    d_pre = line.step(
        lambda c, w, s: (times_transpose(c, w) * s.astype(F32)).astype(BF), cot_all, w_fc2, slope
    )
    fc2_sum = grad_sum(activation, cot_all, fc2_came, 2)
    fc1_came = grad(normed_all, d_pre)
    d_attended = line.step(lambda c, w: times_transpose(c, w).astype(BF), cot_all, w_dense)
    results = attend(0, ())
    fc1_sum = grad_sum(normed_all, d_pre, fc1_came, 2)
    fc2_sum.further(line)
    if pairs > 1:
        results = attend(1, results)
    fc2_whole = gathered(line.hold(fc2_sum.end(line)))
    for pair in range(2, max(2, pairs - 1)):
        results = attend(pair, results)
    fc1_sum.further(line)
    for pair in range(max(2, pairs - 1), pairs):
        results = attend(pair, results)
    attended, d_projected, d_bias_qkv = results
    fc1_pieces = sends(cut(fc1_sum.end(line), slab, owners))

    qkv_came = grad(normed_all, d_projected)
    dense_came = grad(attended, cot_all, False)
    d_normed_first = line.step(times_transpose, d_pre, fc1_cols)
    fc1_whole = gathered(line.step(lambda *p: placed(p, place, 1), *fc1_pieces))
    d_normed_part = line.step(
        lambda a, b, c: (times_transpose(a, b) + c).astype(BF),
        d_projected,
        qkv_cols,
        d_normed_first,
    )
    d_normed_sum = Passing(d_normed_part)
    qkv_sum = grad_sum(normed_all, d_projected, qkv_came, 2)
    dense_sum = grad_sum(attended, cot_all, dense_came, 1, False)
    out_first = line.step(times, activation, w_fc2)
    d_normed_sum.further()
    out_part = line.step(
        lambda a, b, c: (times(a, b) + c).astype(BF), attended, w_dense, out_first
    )
    qkv_sum.further(line)
    dense_sum.further(line)
    out_sum = Passing(out_part)
    d_normed_sum.further()
    fc2_total = line.step(lambda a: a.astype(F32), fc2_whole)
    qkv_pieces = sends(cut(qkv_sum.end(line), slab, owners))
    dense_piece = line.hold(dense_sum.end(line))
    grad_inputs, norm_sums = line.step(
        lambda x, g, c, *p: ln_backward(x, g, c, p, reps, group),
        inputs,
        gain,
        cotangent,
        *d_normed_sum.end(),
    )

    def last_slab(dense_piece, *pieces):
        qkv_slab = placed([a.reshape(slab, 3, rows) for a in pieces], place, 2)
        dense_slab = dense_piece.reshape(reps, rows // reps, width // reps).transpose(1, 0, 2)
        return jnp.concatenate(
            [qkv_slab.reshape(slab, -1), dense_slab.reshape(slab, width)], axis=1
        )

    last_whole = gathered(line.step(last_slab, dense_piece, *qkv_pieces))
    out_sum.further()

    def all_sums(d_bias_qkv, cotangent, norm_sums, d_pre):
        d_bias_all = lax.dynamic_update_slice_in_dim(
            jnp.zeros((3, width), F32),
            jnp.sum(d_bias_qkv[:, 0], axis=0).reshape(3, rows),
            place * rows,
            1,
        )
        ones = jnp.ones((8, group * tokens), BF)
        return (
            jnp.concatenate(
                [
                    d_bias_all.reshape(group, 3 * rows),
                    jnp.sum(cotangent.astype(F32), axis=0).reshape(group, rows),
                    norm_sums[0].reshape(group, rows),
                    norm_sums[1].reshape(group, rows),
                ],
                axis=1,
            ),
            times(ones, d_pre)[0],
        )

    sums, d_bias_fc1 = line.step(all_sums, d_bias_qkv, cotangent, norm_sums, d_pre)
    came = [
        ring(lax.dynamic_slice_in_dim(sums, owners[hop], 1, 0), "shard", hop)
        for hop in range(1, group)
    ]
    sums = sum(came, lax.dynamic_slice_in_dim(sums, place, 1, 0))[0]
    sums = rep_sum(line.hold(jnp.concatenate([sums, d_bias_fc1])))
    out_sum.further()
    fc1_total = line.step(lambda a: a.astype(F32), fc1_whole)
    block_out = line.step(
        lambda x, b, *p: sum((a.astype(F32) for a in p), x.astype(F32) + b),
        inputs,
        bias_out,
        *out_sum.end(),
    )
    qkv_total, dense_total = line.step(
        lambda a: (
            a[:, : 3 * width].astype(F32),
            a[:, 3 * width :]
            .reshape(reps, slab, reps, width // reps)
            .transpose(2, 1, 0, 3)
            .reshape(rows, width)
            .astype(F32),
        ),
        last_whole,
    )
    cot_total = sums[3 * rows : 4 * rows]
    return (
        block_out,
        grad_inputs,
        sums[4 * rows : 5 * rows],
        sums[5 * rows : 6 * rows],
        qkv_total,
        sums[: 3 * rows],
        dense_total,
        cot_total,
        fc1_total,
        sums[6 * rows :],
        fc2_total,
        cot_total,
    )


def solution(mesh):
    both, shard = P(("rep", "shard")), P("shard")
    wide, held = P(("rep", "shard"), None), P("shard", None)
    return jax.shard_map(
        shards,
        mesh=mesh,
        in_specs=(
            wide, both, both, shard, shard, held, shard, held, shard, held, shard, held, shard, wide
        ),
        out_specs=(
            wide, wide, shard, shard, held, shard, held, shard, held, shard, held, shard
        ),
        check_vma=False,
    )
```

```python
import functools

import jax
import jax.numpy as jnp
from jax import lax
from jax.experimental import pallas as pl
from jax.experimental.pallas import tpu as pltpu
from jax.sharding import PartitionSpec as P

HEAD_DIM = 64
ROT = 32
SEQ = 1024
PAIR = 2 * HEAD_DIM
BF = jnp.bfloat16
F32 = jnp.float32
ROOM = pltpu.CompilerParams(vmem_limit_bytes=56 * 2**20)
ANY = pl.BlockSpec(memory_space=pl.ANY)


def ring(array, axis, distance):
    size = lax.axis_size(axis)
    return lax.ppermute(array, axis, [(i, (i + distance) % size) for i in range(size)])


def swap(array, axis, mask):
    size = lax.axis_size(axis)
    return lax.ppermute(array, axis, [(i, i ^ mask) for i in range(size)])


def contract_rows(left_side, right_side):
    return lax.dot_general(
        left_side, right_side, (((0,), (0,)), ((), ())), preferred_element_type=F32
    )


def times_transpose(left_side, right_side):
    return lax.dot_general(
        left_side, right_side, (((1,), (1,)), ((), ())), preferred_element_type=F32
    )


def times(left_side, right_side):
    return jnp.dot(left_side, right_side, preferred_element_type=F32)


class Order:
    def __init__(self):
        self.last = None

    def step(self, work, *operands):
        if self.last is not None:
            operands, _ = lax.optimization_barrier((operands, self.last))
        result = work(*operands)
        self.last = jax.tree.leaves(result)
        return result

    def hold(self, array):
        return self.step(lambda a: a, array)


def doubled(row, place, line):
    bit = 1
    while bit < lax.axis_size("shard"):
        row = line.hold(row)
        other = swap(row, "shard", bit)
        upper = (place & bit) > 0
        row = jnp.concatenate([jnp.where(upper, other, row), jnp.where(upper, row, other)])
        bit *= 2
    return row


def owned_sum(line, values, place):
    bit = lax.axis_size("shard") >> 1
    while bit:
        upper = ((place & bit) > 0).astype(jnp.int32)
        count = values.shape[0] // 2
        sent, kept = (
            lax.dynamic_slice_in_dim(values, side * count, count, 0) for side in (1 - upper, upper)
        )
        values = line.hold(kept + swap(sent, "shard", bit))
        bit >>= 1
    return values[0]


class Halving:
    def __init__(self, rep, array, parts):
        count = lax.axis_size("rep").bit_length() - 2
        self.rep = rep
        array = array.reshape((2,) * count + (array.shape[0] >> count,) + array.shape[1:])
        rows = array.shape[count] // parts
        self.arrays = [array] * parts
        self.spans = [(part * rows, rows) for part in range(parts)]
        bits = list(range(count, 0, -1))
        self.bits = [list(bits) for _ in range(parts)]
        self.todo = [
            bits[::-1][part % count :] + bits[::-1][: part % count] for part in range(parts)
        ]

    def pick(self, part, array, mine):
        axis = self.bits[part].index(self.todo[part][0])
        bit = (self.rep >> self.todo[part][0]) & 1
        starts, sizes = [0] * array.ndim, list(array.shape)
        starts[axis], sizes[axis] = (bit if mine else 1 - bit), 1
        starts[len(self.bits[part])], sizes[len(self.bits[part])] = self.spans[part]
        half = lax.dynamic_slice(array, starts, sizes)
        return half.reshape(half.shape[:axis] + half.shape[axis + 1 :])

    def outgoing(self, *arrays):
        return tuple(self.pick(part, array, False) for part, array in enumerate(arrays))

    def added(self, *operands):
        count = len(operands) // 2
        return tuple(
            (self.pick(part, operands[part], True).astype(F32) + operands[count + part].astype(F32))
            .astype(BF)
            for part in range(count)
        )

    def send(self, line):
        sent = line.step(self.outgoing, *self.arrays)
        self.came = [
            swap(piece, "rep", 1 << todo[0]) for piece, todo in zip(sent, self.todo)
        ]

    def take(self, line):
        self.arrays = line.step(self.added, *self.arrays, *self.came)
        for part, todo in enumerate(self.todo):
            self.bits[part].remove(todo[0])
            self.todo[part] = todo[1:]
            self.spans[part] = (0, self.spans[part][1])

    def further(self, line):
        self.take(line)
        self.send(line)

    def end(self, line):
        while len(self.todo[0]) > 1:
            self.further(line)
        self.take(line)
        return jnp.concatenate(self.arrays, axis=0)


class Passing:
    def __init__(self, line, array, tokens):
        self.line, self.group = line, array.shape[0] // tokens
        self.block = lambda hop: (hop % self.group * tokens, tokens)
        self.array, self.hop = array, 1
        sent = line.step(lambda a: lax.slice_in_dim(a, tokens, 2 * tokens, axis=0), array)
        self.came = ring(sent, "shard", 1)

    def hold(self):
        self.came = self.line.hold(self.came)

    def further(self):
        self.hop += 1
        first, count = self.block(self.hop)
        sent = self.line.step(
            lambda a, b: (
                lax.slice_in_dim(a, first, first + count, axis=0).astype(F32) + b.astype(F32)
            ).astype(BF),
            self.array,
            self.came,
        )
        self.came = ring(sent, "shard", 1)

    def end(self):
        while self.hop + 1 < self.group:
            self.further()
        return lax.slice_in_dim(self.array, 0, self.block(0)[1], axis=0), self.came


def exchanged(array):
    return lax.all_to_all(array, "shard", 0, 0, tiled=True)


def widen_kernel(size, width, rows_ref, out_ref):
    length = rows_ref.shape[0] // size
    for owner in range(size):
        for at in range(rows_ref.shape[1] // width):
            first = (at * size + owner) * width
            out_ref[:, first : first + width] = rows_ref[
                owner * length : (owner + 1) * length, at * width : (at + 1) * width
            ]


def widened(array, size, width):
    rows, columns = array.shape
    return pl.pallas_call(
        functools.partial(widen_kernel, size, width),
        out_shape=jax.ShapeDtypeStruct((rows // size, columns * size), array.dtype),
        compiler_params=ROOM,
        name="widened",
    )(array)


def split_kernel(in_ref, *refs):
    first = 0
    for ref in refs:
        ref[...] = in_ref[first : first + ref.shape[0]].astype(F32)
        first += ref.shape[0]


def split_rows(array, reps, heights):
    rows, columns = array.shape
    return pl.pallas_call(
        split_kernel,
        grid=(reps,),
        in_specs=[pl.BlockSpec((rows // reps, columns), lambda r: (r, 0))],
        out_specs=[pl.BlockSpec((height, columns), lambda r: (r, 0)) for height in heights],
        out_shape=[jax.ShapeDtypeStruct((height * reps, columns), F32) for height in heights],
        compiler_params=ROOM,
        name="split_rows",
    )(array)


class Spread:
    def __init__(self, line, array):
        self.line, self.size = line, lax.axis_size("rep")
        self.pieces = {0: array}
        steps = (2, 4) if self.size == 8 else range(2, self.size, 2)
        for mask in steps:
            self.pieces[mask] = swap(array, "rep", mask)

    def across(self):
        if self.size != 8:
            return
        half = self.pieces[0].shape[0] // 2
        self.pieces[2], self.pieces[4], first, second = self.line.step(
            lambda a, b: (a, b, a[:half], b[half:]), self.pieces[2], self.pieces[4]
        )
        self.halves = (swap(first, "rep", 4), swap(second, "rep", 2))

    def shared(self):
        masks = range(0, self.size, 2)
        if self.size == 8:
            self.pieces[6] = self.line.step(lambda *h: jnp.concatenate(h), *self.halves)
        held = self.line.step(lambda *p: p, *[self.pieces[mask] for mask in masks])
        return [piece for one in held for piece in (one, swap(one, "rep", 1))]


def assemble_kernel(rep_ref, *refs):
    for mask, piece in enumerate(refs[:-1]):

        @pl.when(pl.program_id(0) == mask)
        def _(piece=piece):
            refs[-1][...] = piece[...].astype(F32)


def assemble(pieces, rep):
    size = len(pieces)
    rows, columns = pieces[0].shape
    whole = pl.BlockSpec((rows, columns), lambda m, r: (0, 0), pipeline_mode=pl.Buffered(1))
    return pl.pallas_call(
        assemble_kernel,
        grid_spec=pltpu.PrefetchScalarGridSpec(
            num_scalar_prefetch=1,
            grid=(size,),
            in_specs=[whole] * size,
            out_specs=pl.BlockSpec((rows, columns), lambda m, r: (r[0] ^ m, 0)),
        ),
        out_shape=jax.ShapeDtypeStruct((rows * size, columns), F32),
        compiler_params=ROOM,
        name="assemble",
    )(rep.reshape(1), *pieces)


def grad_kernel(which_ref, left_ref, right_ref, *refs):
    *more, out_ref = refs
    left = left_ref[...]
    if more and more[0].shape[0] == left.shape[0]:
        both = more.pop(0)
        lanes = both.shape[1] // 2
        left = jnp.concatenate(
            [left, jnp.where(which_ref[0] == 0, both[:, :lanes], both[:, lanes:])], axis=1
        )
    total = contract_rows(left, right_ref[...])
    if more:
        total = total + more[0][...].astype(F32)
    out_ref[...] = total.astype(BF)


def half_grads(left, right, which, reps, came=None, also=None):
    tokens, height = left.shape
    length = right.shape[1]
    height //= reps
    extra = 0 if also is None else also.shape[1] // reps
    if height % 128 or extra not in (0, 64):
        sides = [left] if also is None else [left, also]
        total = [
            contract_rows(
                lax.dynamic_index_in_dim(
                    side.reshape(tokens, reps // 2, 2, -1), which, 2, keepdims=False
                ).reshape(tokens, -1),
                right,
            ).reshape(reps // 2, -1, length)
            for side in sides
        ]
        total = jnp.concatenate(total, axis=1).reshape(-1, length)
        return (total if came is None else total + came.astype(F32)).astype(BF)
    block = pl.BlockSpec((height + extra, length), lambda b, w: (b, 0))
    more = [] if also is None else [also]
    more_specs = [] if also is None else [pl.BlockSpec((tokens, 128), lambda b, w: (0, b))]
    return pl.pallas_call(
        grad_kernel,
        grid_spec=pltpu.PrefetchScalarGridSpec(
            num_scalar_prefetch=1,
            grid=(reps // 2,),
            in_specs=[
                pl.BlockSpec((tokens, height), lambda b, w: (0, 2 * b + w[0])),
                pl.BlockSpec((tokens, length), lambda b, w: (0, 0)),
            ]
            + more_specs
            + ([] if came is None else [block]),
            out_specs=block,
        ),
        out_shape=jax.ShapeDtypeStruct((reps // 2 * (height + extra), length), BF),
        compiler_params=ROOM,
        name="half_grads",
    )(which.reshape(1), left, right, *more, *([] if came is None else [came]))


def ln_forward_kernel(reps, group, x_ref, gain_ref, shift_ref, out_ref):
    x = x_ref[...].astype(F32)
    centred = x - jnp.mean(x, axis=-1, keepdims=True)
    spread = jnp.mean(centred * centred, axis=-1, keepdims=True)
    normed = (centred * lax.rsqrt(spread + 1e-05)) * gain_ref[...] + shift_ref[...]
    slab = x.shape[1] // (reps * group)
    out_ref[...] = jnp.concatenate(
        [
            normed[:, (g * reps + r) * slab : (g * reps + r + 1) * slab]
            for r in range(reps)
            for g in range(group)
        ],
        axis=1,
    ).astype(BF)


def ln_forward(inputs, gain, shift, reps, group):
    tokens, width = inputs.shape
    return pl.pallas_call(
        functools.partial(ln_forward_kernel, reps, group),
        out_shape=jax.ShapeDtypeStruct((tokens, width), BF),
        compiler_params=ROOM,
        name="ln_forward",
    )(inputs, gain.reshape(1, width), shift.reshape(1, width))


def ln_backward_kernel(reps, group, x_ref, gain_ref, cot_ref, a_ref, b_ref, out_ref, sums_ref):
    x = x_ref[...].astype(F32)
    centred = x - jnp.mean(x, axis=-1, keepdims=True)
    spread = jnp.mean(centred * centred, axis=-1, keepdims=True)
    inverse = lax.rsqrt(spread + 1e-05)
    xhat = centred * inverse
    mixed = a_ref[...].astype(F32) + b_ref[...].astype(F32)
    slab = x.shape[1] // (reps * group)
    d_normed = jnp.concatenate(
        [
            mixed[:, (r * group + g) * slab : (r * group + g + 1) * slab]
            for g in range(group)
            for r in range(reps)
        ],
        axis=1,
    )
    sums_ref[0:1] = jnp.sum(d_normed * xhat, axis=0, keepdims=True)
    sums_ref[1:2] = jnp.sum(d_normed, axis=0, keepdims=True)
    scaled = d_normed * gain_ref[...]
    out_ref[...] = cot_ref[...].astype(F32) + inverse * (
        scaled
        - jnp.mean(scaled, axis=-1, keepdims=True)
        - xhat * jnp.mean(scaled * xhat, axis=-1, keepdims=True)
    )


def ln_backward(inputs, gain, cotangent, parts, reps, group):
    tokens, width = inputs.shape
    return pl.pallas_call(
        functools.partial(ln_backward_kernel, reps, group),
        out_shape=[
            jax.ShapeDtypeStruct((tokens, width), F32),
            jax.ShapeDtypeStruct((2, width), F32),
        ],
        compiler_params=ROOM,
        name="ln_backward",
    )(inputs, gain.reshape(1, width), cotangent, *parts)


def pull_kernel(cot_ref, weight_ref, *refs):
    total = times_transpose(cot_ref[...], weight_ref[...])
    if len(refs) > 1:
        total = total * refs[0][...].astype(F32)
    refs[-1][...] = total.astype(BF)


def pull(cot_all, weight, *slope):
    height, width = cot_all.shape
    hidden = weight.shape[0]
    tile = min(512, hidden)
    block = pl.BlockSpec((height, tile), lambda j: (0, j))
    return pl.pallas_call(
        pull_kernel,
        grid=(hidden // tile,),
        in_specs=[
            pl.BlockSpec((height, width), lambda j: (0, 0)),
            pl.BlockSpec((tile, width), lambda j: (j, 0)),
        ]
        + [block] * len(slope),
        out_specs=block,
        out_shape=jax.ShapeDtypeStruct((height, hidden), BF),
        compiler_params=ROOM,
        name="pull",
    )(cot_all, weight, *slope)


def push_kernel(transposed, size, place_ref, a_ref, b_ref, c_ref, d_ref, out_ref):
    product = times_transpose if transposed else times
    total = product(a_ref[...], b_ref[...]) + product(c_ref[...], d_ref[...])
    if size is None:
        out_ref[...] = total.astype(BF)
        return
    block = out_ref.shape[0] // size
    for hop in range(size):
        out_ref[token_block(place_ref[0], hop, size, block)] = total[
            hop * block : (hop + 1) * block
        ].astype(BF)


def push(a, b, c, d, transposed, place, size=None):
    height = a.shape[0]
    length = b.shape[0 if transposed else 1]
    tile = min(512, length)
    full = lambda x: pl.BlockSpec(x.shape, lambda j, z: (0, 0))
    if transposed:
        part = lambda x: pl.BlockSpec((tile, x.shape[1]), lambda j, z: (j, 0))
    else:
        part = lambda x: pl.BlockSpec((x.shape[0], tile), lambda j, z: (0, j))
    return pl.pallas_call(
        functools.partial(push_kernel, transposed, size),
        grid_spec=pltpu.PrefetchScalarGridSpec(
            num_scalar_prefetch=1,
            grid=(length // tile,),
            in_specs=[full(a), part(b), full(c), part(d)],
            out_specs=pl.BlockSpec((height, tile), lambda j, z: (0, j)),
        ),
        out_shape=jax.ShapeDtypeStruct((height, length), BF),
        compiler_params=ROOM,
        name="push",
    )(place.reshape(1), a, b, c, d)


def turned(u, turn, sign):
    return (
        u * turn[0]
        + sign * (pltpu.roll(u, PAIR - ROT // 2, 1) * turn[1])
        + sign * (pltpu.roll(u, ROT // 2, 1) * turn[2])
    )


def spans(rows, block):
    first = 0
    for part in range(rows // block):
        yield part, first, (part + 1) * block
        first += (part + 1) * block


def token_block(place, hop, count, block):
    return pl.ds(pl.multiple_of(lax.rem(place - hop + count, count) * block, block), block)


def attend_kernel(block, place_ref, q_ref, k_ref, v_ref, turn_ref, start_ref, *refs):
    att_ref, prob_ref, low_ref, out_ref = refs[-4:]
    rows = q_ref.shape[0]
    count = rows // block
    for hop in range(count):
        here, there = slice(hop * block, (hop + 1) * block), token_block(place_ref[0], hop, count, block)
        turn = [turn_ref[k, here] for k in range(3)]
        query = turned(q_ref[here], turn, 1.0).astype(BF)
        low_ref[0, there] = (query * HEAD_DIM ** (-0.5)).astype(BF)
        low_ref[1, there] = turned(k_ref[here], turn, 1.0).astype(BF)
        low_ref[2, there] = v_ref[here].astype(BF)
    start = start_ref[0]
    for head in range(2):
        lanes = slice(head * HEAD_DIM, (head + 1) * HEAD_DIM)
        key_h = low_ref[1, :, lanes]
        value_t = low_ref[2, :, lanes].T
        for part, first, length in spans(rows, block):
            own = slice(part * block, (part + 1) * block)
            scores = times_transpose(key_h[:length], low_ref[0, own, lanes])
            place = lax.broadcasted_iota(jnp.int32, (length, block), 0)
            asker = lax.broadcasted_iota(jnp.int32, (length, block), 1) + part * block
            allowed = (place >= start[:, own]) & (place <= asker)
            scores = jnp.where(allowed, scores, -1e30)
            exponent = jnp.exp(scores - jnp.max(scores, axis=0, keepdims=True))
            softmax = exponent * (1.0 / jnp.sum(exponent, axis=0, keepdims=True))
            attention = softmax.astype(BF)
            prob_ref[0, head, first : first + length] = attention
            out_ref[own, lanes] = times(value_t[:, :length], attention).T.astype(BF)
    for hop in range(count):
        att_ref[hop * block : (hop + 1) * block] = out_ref[token_block(place_ref[0], hop, count, block)]


def attend(projected, turns, start, place, first, count, block, before):
    tokens, width = projected.shape
    pairs, seqs = width // (3 * PAIR), tokens // SEQ
    stored = sum(length for _, _, length in spans(SEQ, block))
    wide = lambda at: pl.BlockSpec((SEQ, PAIR), lambda s, p, z: (s, at * pairs + first + p))
    return pl.pallas_call(
        functools.partial(attend_kernel, block),
        grid_spec=pltpu.PrefetchScalarGridSpec(
            num_scalar_prefetch=1,
            grid=(seqs, count),
            in_specs=[
                wide(0),
                wide(1),
                wide(2),
                pl.BlockSpec((3, SEQ, PAIR), lambda s, p, z: (0, s, 0)),
                pl.BlockSpec((1, 1, SEQ), lambda s, p, z: (s, 0, 0)),
            ]
            + [ANY] * len(before),
            out_specs=[
                pl.BlockSpec((SEQ, PAIR), lambda s, p, z: (s, first + p)),
                pl.BlockSpec((1, 2, stored, block), lambda s, p, z: (s, p, 0, 0)),
                pl.BlockSpec((3, SEQ, PAIR), lambda s, p, z: (0, s, p)),
            ],
            scratch_shapes=[pltpu.VMEM((SEQ, PAIR), BF)],
        ),
        out_shape=[
            jax.ShapeDtypeStruct((tokens, pairs * PAIR), BF),
            jax.ShapeDtypeStruct((seqs, 2 * count, stored, block), BF),
            jax.ShapeDtypeStruct((3, tokens, count * PAIR), BF),
        ],
        input_output_aliases={6: 0} if before else {},
        compiler_params=ROOM,
        name="attend",
    )(place.reshape(1), projected, projected, projected, turns, start, *before)


def attend_back_kernel(block, place_ref, prob_ref, low_ref, datt_ref, turn_ref, *refs):
    dproj_ref, bsum_ref, d_ref, dq_ref, dk_ref, dv_ref, done_ref = refs[-7:]
    rows = datt_ref.shape[0]
    count = rows // block
    stage = pl.program_id(2)

    @pl.when(stage == 0)
    def _():
        for hop in range(count):
            d_ref[token_block(place_ref[0], hop, count, block)] = datt_ref[
                hop * block : (hop + 1) * block
            ]
        for head in range(2):
            lanes = slice(head * HEAD_DIM, (head + 1) * HEAD_DIM)
            key_t = low_ref[1, :, lanes].T
            value_h = low_ref[2, :, lanes]
            for part, first, length in reversed(list(spans(rows, block))):
                own = slice(part * block, (part + 1) * block)
                query_p = low_ref[0, own, lanes]
                d_att_p = d_ref[own, lanes]
                attention = prob_ref[0, head, first : first + length]
                d_attention = times_transpose(value_h[:length], d_att_p)
                softmax = attention.astype(F32)
                weighted = softmax * d_attention
                d_scores = (
                    weighted - softmax * jnp.sum(weighted, axis=0, keepdims=True)
                ).astype(BF)
                dq_ref[own, lanes] = times(key_t[:, :length], d_scores).T * HEAD_DIM ** (-0.5)
                d_value = times(attention, d_att_p)
                d_key = times(d_scores, query_p)
                if length == rows:
                    dv_ref[:, lanes] = d_value
                    dk_ref[:, lanes] = d_key
                else:
                    dv_ref[:length, lanes] += d_value
                    dk_ref[:length, lanes] += d_key
        for hop in range(count):
            here = slice(hop * block, (hop + 1) * block)
            there = token_block(place_ref[0], hop, count, block)
            turn = [turn_ref[k, here] for k in range(3)]
            done_ref[0, here] = turned(dq_ref[there], turn, -1.0).astype(BF)
            done_ref[1, here] = turned(dk_ref[there], turn, -1.0).astype(BF)
            done_ref[2, here] = dv_ref[there].astype(BF)

    piece = done_ref[stage]
    dproj_ref[...] = piece
    bsum_ref[0] = jnp.sum(piece.astype(F32), axis=0, keepdims=True)


def attend_back(kept, d_attended, turns, place, first, block, pairs, before):
    prob, low = kept
    tokens = d_attended.shape[0]
    seqs, count = tokens // SEQ, prob.shape[1] // 2
    width = 3 * pairs * PAIR
    return pl.pallas_call(
        functools.partial(attend_back_kernel, block),
        grid_spec=pltpu.PrefetchScalarGridSpec(
            num_scalar_prefetch=1,
            grid=(seqs, count, 3),
            in_specs=[
                pl.BlockSpec((1, 2) + prob.shape[2:], lambda s, p, j, z: (s, p, 0, 0)),
                pl.BlockSpec((3, SEQ, PAIR), lambda s, p, j, z: (0, s, p)),
                pl.BlockSpec((SEQ, PAIR), lambda s, p, j, z: (s, first + p)),
                pl.BlockSpec((3, SEQ, PAIR), lambda s, p, j, z: (0, s, 0)),
            ]
            + [ANY] * len(before),
            out_specs=[
                pl.BlockSpec((SEQ, PAIR), lambda s, p, j, z: (s, j * pairs + first + p)),
                pl.BlockSpec((1, 1, PAIR), lambda s, p, j, z: (s, 0, j * pairs + first + p)),
            ],
            scratch_shapes=[pltpu.VMEM((SEQ, PAIR), BF)]
            + [pltpu.VMEM((SEQ, PAIR), F32)] * 3
            + [pltpu.VMEM((3, SEQ, PAIR), BF)],
        ),
        out_shape=[
            jax.ShapeDtypeStruct((tokens, width), BF),
            jax.ShapeDtypeStruct((seqs, 1, width), F32),
        ],
        input_output_aliases={5: 0, 6: 1} if before else {},
        compiler_params=ROOM,
        name="attend_back",
    )(place.reshape(1), prob, low, d_attended, turns, *before)


def tables(positions):
    frequency = 10000.0 ** (-(jnp.arange(ROT // 2, dtype=F32) * 2.0) / ROT)
    angles = frequency[:, None] * positions[None, :]
    cosine, sine = jnp.cos(angles).T, jnp.sin(angles).T
    none = jnp.zeros_like(sine)
    still = jnp.zeros((sine.shape[0], HEAD_DIM - ROT), F32)
    return jnp.stack(
        [
            jnp.concatenate([cosine, cosine, still + 1.0] * 2, axis=1),
            jnp.concatenate([-sine, none, still] * 2, axis=1),
            jnp.concatenate([none, sine, still] * 2, axis=1),
        ]
    )


def feed_forward(normed_all, fc1_cols, bias):
    pre_act = times(normed_all, fc1_cols) + bias
    root = (2.0 / jnp.pi) ** 0.5
    square = pre_act * pre_act
    curve = jnp.tanh(root * pre_act * (1.0 + 0.044715 * square))
    activation = (0.5 * pre_act * (1.0 + curve)).astype(BF)
    slope = (
        0.5 * (1.0 + curve)
        + 0.5 * pre_act * (1.0 - curve * curve) * root * (1.0 + 3 * 0.044715 * square)
    ).astype(BF)
    return activation, slope


def shards(
    inputs,
    segments,
    positions,
    ln_gain,
    ln_bias,
    w_qkv,
    b_qkv,
    w_dense,
    b_dense,
    w_fc1,
    b_fc1,
    w_fc2,
    b_fc2,
    cotangent,
):
    reps, group = lax.axis_size("rep"), lax.axis_size("shard")
    rep, place = lax.axis_index("rep"), lax.axis_index("shard")
    core = rep & 1
    tokens, width = inputs.shape
    rows = width // group
    slab = rows // reps
    hidden = w_fc1.shape[1] // group
    pairs = rows // PAIR
    line = Order()
    def gathered(array):
        return lax.all_gather(array, "rep", axis=0, tiled=True)

    small = jnp.concatenate(
        [ln_gain, ln_bias, b_qkv, b_dense + b_fc2, positions.astype(F32)]
    ).reshape(1, -1)
    small = doubled(small, place, line)
    def qkv_rows(w):
        return jnp.concatenate(
            [
                jnp.concatenate(
                    [
                        lax.dynamic_slice(w, (rep * slab, at * width + owner * rows), (slab, rows))
                        for at in range(3)
                    ],
                    axis=1,
                )
                for owner in range(group)
            ]
        )

    def fc1_rows(w):
        return jnp.concatenate(
            [
                lax.dynamic_slice(w, (rep * slab, owner * hidden), (slab, hidden))
                for owner in range(group)
            ]
        )

    qkv_pieces = exchanged(line.step(qkv_rows, w_qkv))
    fc1_pieces = exchanged(line.step(fc1_rows, w_fc1))
    gain = small[:, :rows].reshape(width)
    shift = small[:, rows : 2 * rows].reshape(width)
    bias_qkv = lax.dynamic_slice_in_dim(
        small[:, 2 * rows : 5 * rows].reshape(3, width), place * rows, rows, 1
    ).reshape(3 * rows)
    bias_out = small[:, 5 * rows : 6 * rows].reshape(width)
    group_positions = small[:, 6 * rows :]

    normed = [line.step(lambda *o: ln_forward(*o, reps, group), inputs, gain, shift)]
    normed.append(ring(line.hold(normed[0]), "shard", 1))
    qkv_cols = gathered(line.hold(qkv_pieces))

    ring_order = [(place - hop) % group for hop in range(group)]
    ring_positions = jnp.concatenate(
        [lax.dynamic_index_in_dim(group_positions, at, 0, keepdims=False) for at in ring_order]
    )
    start = (
        jnp.arange(SEQ, dtype=jnp.int32)[None, None]
        - group_positions.astype(jnp.int32).reshape(-1, 1, SEQ)
    )
    per_seq = SEQ // tokens
    if group == per_seq:
        turn_place = place
        by_seq = from_seq = lambda array, axis=0: array
    else:
        turn_place = jnp.zeros_like(place)
        seq_order = [at // per_seq * per_seq + (-at) % per_seq for at in range(group)]

        def taken(array, order, axis):
            return jnp.concatenate(
                [
                    lax.dynamic_slice_in_dim(array, at * tokens, tokens, axis)
                    for at in order
                ],
                axis=axis,
            )

        by_seq = lambda array, axis=0: taken(
            array, [(place - at) % group for at in seq_order], axis
        )
        from_seq = lambda array, axis=0: taken(
            array, [at // per_seq * per_seq + (-at) % per_seq for at in ring_order], axis
        )

    turns = line.step(lambda p: by_seq(tables(p), 1), ring_positions)

    def begin(block):
        return jnp.concatenate([block, jnp.zeros(((group - 1) * tokens, width), BF)])

    def put(hop):
        return lambda whole, block: lax.dynamic_update_slice_in_dim(
            whole, block, hop * tokens, 0
        )

    normed_all = line.step(begin, normed[0])
    cot_all = line.step(begin, cotangent)
    for hop in range(1, group):
        normed[hop] = line.hold(normed[hop])
        if hop == 1:
            fc1_cols = gathered(line.hold(fc1_pieces))
        if hop + 1 < group:
            normed.append(ring(normed[hop], "shard", 1))
        else:
            cots = [line.hold(cotangent)]
            cots.append(ring(cots[0], "shard", 1))
        normed_all = line.step(put(hop), normed_all, normed[hop])

    projected = line.step(
        lambda a, b, c: by_seq(times(a, b) + c), normed_all, qkv_cols, bias_qkv
    )
    calls = 2 if pairs > 1 else 1
    each = pairs // calls
    kept = []

    def attend_some(call, before):
        attended, *rest = line.step(
            lambda p, *b: attend(p, turns, start, turn_place, call * each, each, tokens, b),
            projected,
            *before,
        )
        kept.append(rest)
        return (attended,)

    attended = attend_some(0, ())
    for hop in range(1, group):
        cots[hop] = line.hold(cots[hop])
        if hop + 1 < group:
            cots.append(ring(cots[hop], "shard", 1))
        cot_all = line.step(put(hop), cot_all, cots[hop])
        if hop == 1:
            activation, slope = line.step(feed_forward, normed_all, fc1_cols, b_fc1)
        if hop == 2:
            if calls > 1:
                attended = attend_some(1, attended)
            out_part = line.step(
                lambda a, b, c, d: push(a, b, c, d, False, place, group),
                from_seq(attended[0]),
                w_dense,
                activation,
                w_fc2,
            )
            out_sum = lax.psum_scatter(out_part, "shard", scatter_dimension=0, tiled=True)
    (attended,) = attended
    attended = from_seq(attended)

    def grad(left, right, *also):
        sent = line.step(
            lambda a, b, *c: half_grads(a, b, 1 - core, reps, None, *c), left, right, *also
        )
        return swap(sent, "rep", 1)

    def grad_sum(left, right, came, *also):
        own = line.step(
            lambda a, b, c, *d: half_grads(a, b, core, reps, c, *d), left, right, came, *also
        )
        halving = Halving(rep, own, 2)
        halving.send(line)
        return halving

    def attend_back_some(call, before):
        return line.step(
            lambda d, t, *b: attend_back(
                kept[call], d, t, turn_place, call * each, tokens, pairs, b
            ),
            d_attended,
            turns,
            *before,
        )

    out_came = grad(activation, cot_all, attended)
    d_pre = line.step(pull, cot_all, w_fc2, slope)
    fc1_came = grad(normed_all, d_pre)
    out_grads = grad_sum(activation, cot_all, out_came, attended)
    d_attended = by_seq(line.step(pull, cot_all, w_dense))
    back = attend_back_some(0, ())
    fc1_sum = grad_sum(normed_all, d_pre, fc1_came)
    out_grads.further(line)
    for call in range(1, calls):
        back = attend_back_some(call, back)
    d_projected, d_bias_qkv = back
    d_projected = from_seq(d_projected)
    d_normed_part = line.step(
        lambda a, b, c, d: push(a, b, c, d, True, place), d_projected, qkv_cols, d_pre, fc1_cols
    )
    d_normed_sum = Passing(line, d_normed_part, tokens)
    out_piece = out_grads.end(line)
    fc1_sum.further(line)
    out_whole = gathered(line.hold(out_piece))
    qkv_came = grad(normed_all, d_projected)
    block_out = line.step(
        lambda x, b, p: x.astype(F32) + b + p.astype(F32), inputs, bias_out, out_sum
    )
    qkv_sum = grad_sum(normed_all, d_projected, qkv_came)
    fc1_pieces = exchanged(line.hold(fc1_sum.end(line)))
    d_normed_sum.further()
    qkv_sum.further(line)

    def bias_sums(d_bias_qkv, cotangent, d_pre):
        d_bias_all = lax.dynamic_update_slice_in_dim(
            jnp.zeros((3, width), F32),
            jnp.sum(d_bias_qkv[:, 0], axis=0).reshape(3, rows),
            place * rows,
            1,
        )
        ones = jnp.ones((8, group * tokens), BF)
        return (
            jnp.concatenate(
                [
                    d_bias_all.reshape(group, 3 * rows),
                    jnp.sum(cotangent.astype(F32), axis=0).reshape(group, rows),
                ],
                axis=1,
            ),
            times(ones, d_pre)[0],
        )

    early_sums, d_bias_fc1 = line.step(bias_sums, d_bias_qkv, cotangent, d_pre)
    qkv_piece = qkv_sum.end(line)
    d_normed_sum.hold()
    fc1_slab = line.step(lambda p: widened(p, group, hidden), fc1_pieces)
    qkv_pieces = exchanged(line.hold(qkv_piece))
    fc1_whole = gathered(line.hold(fc1_slab))
    qkv_spread = Spread(line, line.step(lambda p: widened(p, group, rows), qkv_pieces))
    d_normed_sum.further()
    fc2_total, dense_total = line.step(
        lambda a: split_rows(a, reps, (hidden // reps, slab)), out_whole
    )
    grad_inputs, norm_sums = line.step(
        lambda x, g, c, *p: ln_backward(x, g, c, p, reps, group),
        inputs,
        gain,
        cotangent,
        *d_normed_sum.end(),
    )

    sums = line.step(
        lambda early, norm_sums: jnp.concatenate(
            [early, norm_sums[0].reshape(group, rows), norm_sums[1].reshape(group, rows)], axis=1
        ),
        early_sums,
        norm_sums,
    )
    qkv_spread.across()
    sums = owned_sum(line, sums, place)
    sums = line.hold(jnp.concatenate([sums, d_bias_fc1]))
    sums = line.hold(sums + swap(sums, "rep", 1))
    fc1_total = line.step(lambda a: a.astype(F32), fc1_whole)
    qkv_spread = qkv_spread.shared()
    bit = 2
    while bit < reps:
        sums = line.hold(sums + swap(sums, "rep", bit))
        bit *= 2
    qkv_total = line.step(lambda *p: assemble(p, rep), *qkv_spread)
    cot_total = sums[3 * rows : 4 * rows]
    return (
        block_out,
        grad_inputs,
        sums[4 * rows : 5 * rows],
        sums[5 * rows : 6 * rows],
        qkv_total,
        sums[: 3 * rows],
        dense_total,
        cot_total,
        fc1_total,
        sums[6 * rows :],
        fc2_total,
        cot_total,
    )


def solution(mesh):
    both, shard = P(("rep", "shard")), P("shard")
    wide, held = P(("rep", "shard"), None), P("shard", None)
    return jax.shard_map(
        shards,
        mesh=mesh,
        in_specs=(
            wide, both, both, shard, shard, held, shard, held, shard, held, shard, held, shard, wide
        ),
        out_specs=(
            wide, wide, shard, shard, held, shard, held, shard, held, shard, held, shard
        ),
        check_vma=False,
    )
```

```python
import functools

import jax
import jax.numpy as jnp
from jax import lax
from jax.experimental import pallas as pl
from jax.experimental.pallas import tpu as pltpu
from jax.sharding import PartitionSpec as P

HEAD_DIM = 64
ROT = 32
SEQ = 1024
PAIR = 2 * HEAD_DIM
BF = jnp.bfloat16
F32 = jnp.float32
ROOM = pltpu.CompilerParams(vmem_limit_bytes=56 * 2**20)
ANY = pl.BlockSpec(memory_space=pl.ANY)


def ring(array, axis, distance):
    size = lax.axis_size(axis)
    return lax.ppermute(array, axis, [(i, (i + distance) % size) for i in range(size)])


def swap(array, axis, mask):
    size = lax.axis_size(axis)
    return lax.ppermute(array, axis, [(i, i ^ mask) for i in range(size)])


def contract_rows(left_side, right_side):
    return lax.dot_general(
        left_side, right_side, (((0,), (0,)), ((), ())), preferred_element_type=F32
    )


def times_transpose(left_side, right_side):
    return lax.dot_general(
        left_side, right_side, (((1,), (1,)), ((), ())), preferred_element_type=F32
    )


def times(left_side, right_side):
    return jnp.dot(left_side, right_side, preferred_element_type=F32)


class Order:
    def __init__(self):
        self.last = None

    def step(self, work, *operands):
        if self.last is not None:
            operands, _ = lax.optimization_barrier((operands, self.last))
        result = work(*operands)
        self.last = jax.tree.leaves(result)
        return result

    def hold(self, array):
        return self.step(lambda a: a, array)


def doubled(row, place, line):
    bit = 1
    while bit < lax.axis_size("shard"):
        row = line.hold(row)
        other = swap(row, "shard", bit)
        upper = (place & bit) > 0
        row = jnp.concatenate([jnp.where(upper, other, row), jnp.where(upper, row, other)])
        bit *= 2
    return row


def owned_sum(line, values, place):
    bit = lax.axis_size("shard") >> 1
    while bit:
        upper = ((place & bit) > 0).astype(jnp.int32)
        count = values.shape[0] // 2
        sent, kept = (
            lax.dynamic_slice_in_dim(values, side * count, count, 0) for side in (1 - upper, upper)
        )
        values = line.hold(kept + swap(sent, "shard", bit))
        bit >>= 1
    return values[0]


class Halving:
    def __init__(self, rep, array, parts):
        count = lax.axis_size("rep").bit_length() - 2
        self.rep = rep
        array = array.reshape((2,) * count + (array.shape[0] >> count,) + array.shape[1:])
        rows = array.shape[count] // parts
        self.arrays = [array] * parts
        self.spans = [(part * rows, rows) for part in range(parts)]
        bits = list(range(count, 0, -1))
        self.bits = [list(bits) for _ in range(parts)]
        self.todo = [
            bits[::-1][part % count :] + bits[::-1][: part % count] for part in range(parts)
        ]

    def pick(self, part, array, mine):
        axis = self.bits[part].index(self.todo[part][0])
        bit = (self.rep >> self.todo[part][0]) & 1
        starts, sizes = [0] * array.ndim, list(array.shape)
        starts[axis], sizes[axis] = (bit if mine else 1 - bit), 1
        starts[len(self.bits[part])], sizes[len(self.bits[part])] = self.spans[part]
        half = lax.dynamic_slice(array, starts, sizes)
        return half.reshape(half.shape[:axis] + half.shape[axis + 1 :])

    def outgoing(self, *arrays):
        return tuple(self.pick(part, array, False) for part, array in enumerate(arrays))

    def added(self, *operands):
        count = len(operands) // 2
        return tuple(
            (self.pick(part, operands[part], True).astype(F32) + operands[count + part].astype(F32))
            .astype(BF)
            for part in range(count)
        )

    def send(self, line, sent=None):
        if sent is None:
            sent = line.step(self.outgoing, *self.arrays)
        self.came = [
            swap(piece, "rep", 1 << todo[0]) for piece, todo in zip(sent, self.todo)
        ]

    def take(self, line):
        self.arrays = line.step(self.added, *self.arrays, *self.came)
        for part, todo in enumerate(self.todo):
            self.bits[part].remove(todo[0])
            self.todo[part] = todo[1:]
            self.spans[part] = (0, self.spans[part][1])

    def further(self, line):
        self.take(line)
        self.send(line)

    def end(self, line):
        while len(self.todo[0]) > 1:
            self.further(line)
        self.take(line)
        return jnp.concatenate(self.arrays, axis=0)


class Passing:
    def __init__(self, line, array, tokens):
        self.line, self.group = line, array.shape[0] // tokens
        self.block = lambda hop: (hop % self.group * tokens, tokens)
        self.array, self.hop = array, 1
        sent = line.step(lambda a: lax.slice_in_dim(a, tokens, 2 * tokens, axis=0), array)
        self.came = ring(sent, "shard", 1)

    def hold(self):
        self.came = self.line.hold(self.came)

    def further(self):
        self.hop += 1
        first, count = self.block(self.hop)
        sent = self.line.step(
            lambda a, b: (
                lax.slice_in_dim(a, first, first + count, axis=0).astype(F32) + b.astype(F32)
            ).astype(BF),
            self.array,
            self.came,
        )
        self.came = ring(sent, "shard", 1)

    def end(self):
        while self.hop + 1 < self.group:
            self.further()
        return lax.slice_in_dim(self.array, 0, self.block(0)[1], axis=0), self.came


def place_kernel(width, place_ref, *refs):
    *pieces, out_ref = refs
    size = len(pieces)
    length, columns = pieces[0].shape
    for hop, piece in enumerate(pieces):
        owner = lax.rem(place_ref[0] - hop + size, size)
        if width is None:
            out_ref[pl.ds(pl.multiple_of(owner * length, length), length), :] = piece[...]
        else:
            count = columns // width
            for at in range(count):
                first = pl.multiple_of((at * size + owner) * width, width)
                out_ref[:, pl.ds(first, width)] = piece[:, at * width : (at + 1) * width]


def placed(pieces, place, width=None):
    length, columns = pieces[0].shape
    shape = (
        (length * len(pieces), columns) if width is None else (length, columns * len(pieces))
    )
    whole = pl.BlockSpec(memory_space=pltpu.VMEM)
    return pl.pallas_call(
        functools.partial(place_kernel, width),
        in_specs=[pl.BlockSpec(memory_space=pltpu.SMEM)] + [whole] * len(pieces),
        out_specs=whole,
        out_shape=jax.ShapeDtypeStruct(shape, pieces[0].dtype),
        compiler_params=ROOM,
        name="placed",
    )(place.reshape(1), *pieces)


def exchanged(array):
    return lax.all_to_all(array, "shard", 0, 0, tiled=True)


def widen_kernel(size, width, rows_ref, out_ref):
    length = rows_ref.shape[0] // size
    for owner in range(size):
        for at in range(rows_ref.shape[1] // width):
            first = (at * size + owner) * width
            out_ref[:, first : first + width] = rows_ref[
                owner * length : (owner + 1) * length, at * width : (at + 1) * width
            ]


def widened(array, size, width):
    rows, columns = array.shape
    return pl.pallas_call(
        functools.partial(widen_kernel, size, width),
        out_shape=jax.ShapeDtypeStruct((rows // size, columns * size), array.dtype),
        compiler_params=ROOM,
        name="widened",
    )(array)


def split_kernel(in_ref, *refs):
    first = 0
    for ref in refs:
        ref[...] = in_ref[first : first + ref.shape[0]].astype(F32)
        first += ref.shape[0]


def split_rows(array, reps, heights):
    rows, columns = array.shape
    return pl.pallas_call(
        split_kernel,
        grid=(reps,),
        in_specs=[pl.BlockSpec((rows // reps, columns), lambda r: (r, 0))],
        out_specs=[pl.BlockSpec((height, columns), lambda r: (r, 0)) for height in heights],
        out_shape=[jax.ShapeDtypeStruct((height * reps, columns), F32) for height in heights],
        compiler_params=ROOM,
        name="split_rows",
    )(array)


class Spread:
    def __init__(self, line, array):
        self.line, self.size = line, lax.axis_size("rep")
        self.pieces = {0: array}
        steps = (2, 4) if self.size == 8 else range(2, self.size, 2)
        for mask in steps:
            self.pieces[mask] = swap(array, "rep", mask)

    def across(self):
        if self.size != 8:
            return
        half = self.pieces[0].shape[0] // 2
        self.pieces[2], self.pieces[4], first, second = self.line.step(
            lambda a, b: (a, b, a[:half], b[half:]), self.pieces[2], self.pieces[4]
        )
        self.halves = (swap(first, "rep", 4), swap(second, "rep", 2))

    def shared(self):
        masks = range(0, self.size, 2)
        if self.size == 8:
            self.pieces[6] = self.line.step(lambda *h: jnp.concatenate(h), *self.halves)
        held = self.line.step(lambda *p: p, *[self.pieces[mask] for mask in masks])
        return [piece for one in held for piece in (one, swap(one, "rep", 1))]


def assemble_kernel(rep_ref, *refs):
    for mask, piece in enumerate(refs[:-1]):

        @pl.when(pl.program_id(0) == mask)
        def _(piece=piece):
            refs[-1][...] = piece[...].astype(F32)


def assemble(pieces, rep):
    size = len(pieces)
    rows, columns = pieces[0].shape
    whole = pl.BlockSpec((rows, columns), lambda m, r: (0, 0), pipeline_mode=pl.Buffered(1))
    return pl.pallas_call(
        assemble_kernel,
        grid_spec=pltpu.PrefetchScalarGridSpec(
            num_scalar_prefetch=1,
            grid=(size,),
            in_specs=[whole] * size,
            out_specs=pl.BlockSpec((rows, columns), lambda m, r: (r[0] ^ m, 0)),
        ),
        out_shape=jax.ShapeDtypeStruct((rows * size, columns), F32),
        compiler_params=ROOM,
        name="assemble",
    )(rep.reshape(1), *pieces)


def grad_kernel(which_ref, left_ref, right_ref, *refs):
    *more, out_ref = refs
    left = left_ref[...]
    if more and more[0].shape[0] == left.shape[0]:
        both = more.pop(0)
        lanes = both.shape[1] // 2
        left = jnp.concatenate(
            [left, jnp.where(which_ref[0] == 0, both[:, :lanes], both[:, lanes:])], axis=1
        )
    total = contract_rows(left, right_ref[...])
    if more:
        total = total + more[0][...].astype(F32)
    out_ref[...] = total.astype(BF)


def chip_of(step):
    return step // 2, (step + 1) // 2 % 2


def grad_sum_kernel(at_ref, left_ref, right_ref, *refs):
    *more, came_ref, own_ref, fast_ref, slow_ref = refs
    left = left_ref[...]
    if more:
        both = more[0][...]
        lanes = both.shape[1] // 2
        left = jnp.concatenate(
            [left, jnp.where(at_ref[0] == 0, both[:, :lanes], both[:, lanes:])], axis=1
        )
    total = (contract_rows(left, right_ref[...]) + came_ref[...].astype(F32)).astype(BF)
    own_ref[...] = total
    slow, fast = chip_of(pl.program_id(0))
    half = total.shape[0] // 2

    @pl.when(fast == 1)
    def _():
        fast_ref[0] = total[:half]

    @pl.when(slow == 1)
    def _():
        slow_ref[0] = total[half:]


def grad_sums(left, right, rep, came, also=None):
    tokens, height = left.shape
    length = right.shape[1]
    height //= 8
    extra = 0 if also is None else also.shape[1] // 8
    total = height + extra
    block = lambda j, at: 2 * (at[2] ^ chip_of(j)[0]) + (at[1] ^ chip_of(j)[1])
    half = (1, total // 2, length)
    return pl.pallas_call(
        grad_sum_kernel,
        grid_spec=pltpu.PrefetchScalarGridSpec(
            num_scalar_prefetch=1,
            grid=(4,),
            in_specs=[
                pl.BlockSpec((tokens, height), lambda j, at: (0, 2 * block(j, at) + at[0])),
                pl.BlockSpec(memory_space=pltpu.VMEM),
            ]
            + (
                []
                if also is None
                else [pl.BlockSpec((tokens, 128), lambda j, at: (0, block(j, at)))]
            )
            + [pl.BlockSpec((total, length), lambda j, at: (block(j, at), 0))],
            out_specs=[
                pl.BlockSpec((total, length), lambda j, at: (block(j, at), 0)),
                pl.BlockSpec(half, lambda j, at: (at[2] ^ (j // 2), 0, 0)),
                pl.BlockSpec(half, lambda j, at: (at[1] ^ (1 - j // 3), 0, 0)),
            ],
        ),
        out_shape=[
            jax.ShapeDtypeStruct((4 * total, length), BF),
            jax.ShapeDtypeStruct((2,) + half[1:], BF),
            jax.ShapeDtypeStruct((2,) + half[1:], BF),
        ],
        compiler_params=ROOM,
        name="grad_sums",
    )(
        jnp.stack([rep & 1, (rep >> 1) & 1, rep >> 2]),
        left,
        right,
        *([] if also is None else [also]),
        came,
    )


def half_grads(left, right, which, reps, came=None, also=None):
    tokens, height = left.shape
    length = right.shape[1]
    height //= reps
    extra = 0 if also is None else also.shape[1] // reps
    if height % 128 or extra not in (0, 64):
        sides = [left] if also is None else [left, also]
        total = [
            contract_rows(
                lax.dynamic_index_in_dim(
                    side.reshape(tokens, reps // 2, 2, -1), which, 2, keepdims=False
                ).reshape(tokens, -1),
                right,
            ).reshape(reps // 2, -1, length)
            for side in sides
        ]
        total = jnp.concatenate(total, axis=1).reshape(-1, length)
        return (total if came is None else total + came.astype(F32)).astype(BF)
    block = pl.BlockSpec((height + extra, length), lambda b, w: (b, 0))
    more = [] if also is None else [also]
    more_specs = [] if also is None else [pl.BlockSpec((tokens, 128), lambda b, w: (0, b))]
    return pl.pallas_call(
        grad_kernel,
        grid_spec=pltpu.PrefetchScalarGridSpec(
            num_scalar_prefetch=1,
            grid=(reps // 2,),
            in_specs=[
                pl.BlockSpec((tokens, height), lambda b, w: (0, 2 * b + w[0])),
                pl.BlockSpec(memory_space=pltpu.VMEM),
            ]
            + more_specs
            + ([] if came is None else [block]),
            out_specs=block,
        ),
        out_shape=jax.ShapeDtypeStruct((reps // 2 * (height + extra), length), BF),
        compiler_params=ROOM,
        name="half_grads",
    )(which.reshape(1), left, right, *more, *([] if came is None else [came]))


def ln_forward_kernel(reps, group, x_ref, gain_ref, shift_ref, out_ref):
    x = x_ref[...].astype(F32)
    centred = x - jnp.mean(x, axis=-1, keepdims=True)
    spread = jnp.mean(centred * centred, axis=-1, keepdims=True)
    normed = (centred * lax.rsqrt(spread + 1e-05)) * gain_ref[...] + shift_ref[...]
    slab = x.shape[1] // (reps * group)
    out_ref[...] = jnp.concatenate(
        [
            normed[:, (g * reps + r) * slab : (g * reps + r + 1) * slab]
            for r in range(reps)
            for g in range(group)
        ],
        axis=1,
    ).astype(BF)


def ln_forward(inputs, gain, shift, reps, group):
    tokens, width = inputs.shape
    return pl.pallas_call(
        functools.partial(ln_forward_kernel, reps, group),
        out_shape=jax.ShapeDtypeStruct((tokens, width), BF),
        compiler_params=ROOM,
        name="ln_forward",
    )(inputs, gain.reshape(1, width), shift.reshape(1, width))


def ln_backward_kernel(reps, group, x_ref, gain_ref, cot_ref, a_ref, b_ref, out_ref, sums_ref):
    x = x_ref[...].astype(F32)
    centred = x - jnp.mean(x, axis=-1, keepdims=True)
    spread = jnp.mean(centred * centred, axis=-1, keepdims=True)
    inverse = lax.rsqrt(spread + 1e-05)
    xhat = centred * inverse
    mixed = a_ref[...].astype(F32) + b_ref[...].astype(F32)
    slab = x.shape[1] // (reps * group)
    d_normed = jnp.concatenate(
        [
            mixed[:, (r * group + g) * slab : (r * group + g + 1) * slab]
            for g in range(group)
            for r in range(reps)
        ],
        axis=1,
    )
    sums_ref[0:1] = jnp.sum(d_normed * xhat, axis=0, keepdims=True)
    sums_ref[1:2] = jnp.sum(d_normed, axis=0, keepdims=True)
    scaled = d_normed * gain_ref[...]
    out_ref[...] = cot_ref[...].astype(F32) + inverse * (
        scaled
        - jnp.mean(scaled, axis=-1, keepdims=True)
        - xhat * jnp.mean(scaled * xhat, axis=-1, keepdims=True)
    )


def ln_backward(inputs, gain, cotangent, parts, reps, group):
    tokens, width = inputs.shape
    return pl.pallas_call(
        functools.partial(ln_backward_kernel, reps, group),
        out_shape=[
            jax.ShapeDtypeStruct((tokens, width), F32),
            jax.ShapeDtypeStruct((2, width), F32),
        ],
        compiler_params=ROOM,
        name="ln_backward",
    )(inputs, gain.reshape(1, width), cotangent, *parts)


def pull_kernel(cot_ref, weight_ref, *refs):
    total = times_transpose(cot_ref[...], weight_ref[...])
    if len(refs) > 1:
        total = total * refs[0][...].astype(F32)
    refs[-1][...] = total.astype(BF)


def pull(cot_all, weight, *slope):
    height, width = cot_all.shape
    hidden = weight.shape[0]
    tile = min(512, hidden)
    block = pl.BlockSpec((height, tile), lambda j: (0, j))
    return pl.pallas_call(
        pull_kernel,
        grid=(hidden // tile,),
        in_specs=[
            pl.BlockSpec(memory_space=pltpu.VMEM),
            pl.BlockSpec((tile, width), lambda j: (j, 0)),
        ]
        + [block] * len(slope),
        out_specs=block,
        out_shape=jax.ShapeDtypeStruct((height, hidden), BF),
        compiler_params=ROOM,
        name="pull",
    )(cot_all, weight, *slope)


def push_kernel(transposed, size, place_ref, a_ref, b_ref, c_ref, d_ref, out_ref):
    product = times_transpose if transposed else times
    total = product(a_ref[...], b_ref[...]) + product(c_ref[...], d_ref[...])
    if size is None:
        out_ref[...] = total.astype(BF)
        return
    block = out_ref.shape[0] // size
    for hop in range(size):
        out_ref[token_block(place_ref[0], hop, size, block)] = total[
            hop * block : (hop + 1) * block
        ].astype(BF)


def push(a, b, c, d, transposed, place, size=None):
    height = a.shape[0]
    length = b.shape[0 if transposed else 1]
    tile = min(512, length)
    full = lambda x: pl.BlockSpec(memory_space=pltpu.VMEM)
    if transposed:
        part = lambda x: pl.BlockSpec((tile, x.shape[1]), lambda j, z: (j, 0))
    else:
        part = lambda x: pl.BlockSpec((x.shape[0], tile), lambda j, z: (0, j))
    return pl.pallas_call(
        functools.partial(push_kernel, transposed, size),
        grid_spec=pltpu.PrefetchScalarGridSpec(
            num_scalar_prefetch=1,
            grid=(length // tile,),
            in_specs=[full(a), part(b), full(c), part(d)],
            out_specs=pl.BlockSpec((height, tile), lambda j, z: (0, j)),
        ),
        out_shape=jax.ShapeDtypeStruct((height, length), BF),
        compiler_params=ROOM,
        name="push",
    )(place.reshape(1), a, b, c, d)


def project_kernel(rows_ref, weight_ref, bias_ref, *refs):
    refs[-1][...] = times(rows_ref[...], weight_ref[...]) + bias_ref[...]


def project(normed_all, weight, bias, tokens, first, count, before):
    height, width = normed_all.shape
    length = weight.shape[1]
    tile = length // 3
    here = first // count
    return pl.pallas_call(
        project_kernel,
        grid=(3,),
        in_specs=[
            pl.BlockSpec((count * tokens, width), lambda j: (here, 0)),
            pl.BlockSpec((width, tile), lambda j: (0, j)),
            pl.BlockSpec((1, tile), lambda j: (0, j)),
        ]
        + [ANY] * len(before),
        out_specs=pl.BlockSpec((count * tokens, tile), lambda j: (here, j)),
        out_shape=jax.ShapeDtypeStruct((height, length), F32),
        input_output_aliases={3: 0} if before else {},
        compiler_params=ROOM,
        name="project",
    )(normed_all, weight, bias, *before)


def turned(u, turn, sign):
    return (
        u * turn[0]
        + sign * (pltpu.roll(u, PAIR - ROT // 2, 1) * turn[1])
        + sign * (pltpu.roll(u, ROT // 2, 1) * turn[2])
    )


def spans(rows, block):
    first = 0
    for part in range(rows // block):
        yield part, first, (part + 1) * block
        first += (part + 1) * block


def token_block(place, hop, count, block):
    return pl.ds(pl.multiple_of(lax.rem(place - hop + count, count) * block, block), block)


def attend_kernel(block, place_ref, q_ref, k_ref, v_ref, turn_ref, start_ref, *refs):
    att_ref, prob_ref, low_ref, out_ref = refs[-4:]
    rows = q_ref.shape[0]
    count = rows // block
    for hop in range(count):
        here, there = slice(hop * block, (hop + 1) * block), token_block(place_ref[0], hop, count, block)
        turn = [turn_ref[k, here] for k in range(3)]
        query = turned(q_ref[here], turn, 1.0).astype(BF)
        low_ref[0, there] = (query * HEAD_DIM ** (-0.5)).astype(BF)
        low_ref[1, there] = turned(k_ref[here], turn, 1.0).astype(BF)
        low_ref[2, there] = v_ref[here].astype(BF)
    start = start_ref[0]
    for head in range(2):
        lanes = slice(head * HEAD_DIM, (head + 1) * HEAD_DIM)
        key_h = low_ref[1, :, lanes]
        value_t = low_ref[2, :, lanes].T
        for part, first, length in spans(rows, block):
            own = slice(part * block, (part + 1) * block)
            scores = times_transpose(key_h[:length], low_ref[0, own, lanes])
            place = lax.broadcasted_iota(jnp.int32, (length, block), 0)
            asker = lax.broadcasted_iota(jnp.int32, (length, block), 1) + part * block
            allowed = (place >= start[:, own]) & (place <= asker)
            scores = jnp.where(allowed, scores, -1e30)
            exponent = jnp.exp(scores - jnp.max(scores, axis=0, keepdims=True))
            softmax = exponent * (1.0 / jnp.sum(exponent, axis=0, keepdims=True))
            attention = softmax.astype(BF)
            prob_ref[0, head, first : first + length] = attention
            out_ref[own, lanes] = times(value_t[:, :length], attention).T.astype(BF)
    for hop in range(count):
        att_ref[hop * block : (hop + 1) * block] = out_ref[token_block(place_ref[0], hop, count, block)]


def attend(projected, turns, start, place, first, count, block, before):
    tokens, width = projected.shape
    pairs, seqs = width // (3 * PAIR), tokens // SEQ
    stored = sum(length for _, _, length in spans(SEQ, block))
    wide = lambda at: pl.BlockSpec((SEQ, PAIR), lambda s, p, z: (s, at * pairs + first + p))
    return pl.pallas_call(
        functools.partial(attend_kernel, block),
        grid_spec=pltpu.PrefetchScalarGridSpec(
            num_scalar_prefetch=1,
            grid=(seqs, count),
            in_specs=[
                wide(0),
                wide(1),
                wide(2),
                pl.BlockSpec((3, SEQ, PAIR), lambda s, p, z: (0, s, 0)),
                pl.BlockSpec((1, 1, SEQ), lambda s, p, z: (s, 0, 0)),
            ]
            + [ANY] * len(before),
            out_specs=[
                pl.BlockSpec((SEQ, PAIR), lambda s, p, z: (s, first + p)),
                pl.BlockSpec((1, 2, stored, block), lambda s, p, z: (s, p, 0, 0)),
                pl.BlockSpec((3, SEQ, PAIR), lambda s, p, z: (0, s, p)),
            ],
            scratch_shapes=[pltpu.VMEM((SEQ, PAIR), BF)],
        ),
        out_shape=[
            jax.ShapeDtypeStruct((tokens, pairs * PAIR), BF),
            jax.ShapeDtypeStruct((seqs, 2 * count, stored, block), BF),
            jax.ShapeDtypeStruct((3, tokens, count * PAIR), BF),
        ],
        input_output_aliases={6: 0} if before else {},
        compiler_params=ROOM,
        name="attend",
    )(place.reshape(1), projected, projected, projected, turns, start, *before)


def attend_back_kernel(block, place_ref, prob_ref, low_ref, datt_ref, turn_ref, *refs):
    dproj_ref, bsum_ref, d_ref, dq_ref, dk_ref, dv_ref, done_ref = refs[-7:]
    rows = datt_ref.shape[0]
    count = rows // block
    stage = pl.program_id(2)

    @pl.when(stage == 0)
    def _():
        for hop in range(count):
            d_ref[token_block(place_ref[0], hop, count, block)] = datt_ref[
                hop * block : (hop + 1) * block
            ]
        for head in range(2):
            lanes = slice(head * HEAD_DIM, (head + 1) * HEAD_DIM)
            key_t = low_ref[1, :, lanes].T
            value_h = low_ref[2, :, lanes]
            for part, first, length in reversed(list(spans(rows, block))):
                own = slice(part * block, (part + 1) * block)
                query_p = low_ref[0, own, lanes]
                d_att_p = d_ref[own, lanes]
                attention = prob_ref[0, head, first : first + length]
                d_attention = times_transpose(value_h[:length], d_att_p)
                softmax = attention.astype(F32)
                weighted = softmax * d_attention
                d_scores = (
                    weighted - softmax * jnp.sum(weighted, axis=0, keepdims=True)
                ).astype(BF)
                dq_ref[own, lanes] = times(key_t[:, :length], d_scores).T * HEAD_DIM ** (-0.5)
                d_value = times(attention, d_att_p)
                d_key = times(d_scores, query_p)
                if length == rows:
                    dv_ref[:, lanes] = d_value
                    dk_ref[:, lanes] = d_key
                else:
                    dv_ref[:length, lanes] += d_value
                    dk_ref[:length, lanes] += d_key
        for hop in range(count):
            here = slice(hop * block, (hop + 1) * block)
            there = token_block(place_ref[0], hop, count, block)
            turn = [turn_ref[k, here] for k in range(3)]
            done_ref[0, here] = turned(dq_ref[there], turn, -1.0).astype(BF)
            done_ref[1, here] = turned(dk_ref[there], turn, -1.0).astype(BF)
            done_ref[2, here] = dv_ref[there].astype(BF)

    piece = done_ref[stage]
    dproj_ref[...] = piece
    bsum_ref[0] = jnp.sum(piece.astype(F32), axis=0, keepdims=True)


def attend_back(kept, d_attended, turns, place, first, block, pairs, before):
    prob, low = kept
    tokens = d_attended.shape[0]
    seqs, count = tokens // SEQ, prob.shape[1] // 2
    width = 3 * pairs * PAIR
    return pl.pallas_call(
        functools.partial(attend_back_kernel, block),
        grid_spec=pltpu.PrefetchScalarGridSpec(
            num_scalar_prefetch=1,
            grid=(seqs, count, 3),
            in_specs=[
                pl.BlockSpec((1, 2) + prob.shape[2:], lambda s, p, j, z: (s, p, 0, 0)),
                pl.BlockSpec((3, SEQ, PAIR), lambda s, p, j, z: (0, s, p)),
                pl.BlockSpec((SEQ, PAIR), lambda s, p, j, z: (s, first + p)),
                pl.BlockSpec((3, SEQ, PAIR), lambda s, p, j, z: (0, s, 0)),
            ]
            + [ANY] * len(before),
            out_specs=[
                pl.BlockSpec((SEQ, PAIR), lambda s, p, j, z: (s, j * pairs + first + p)),
                pl.BlockSpec((1, 1, PAIR), lambda s, p, j, z: (s, 0, j * pairs + first + p)),
            ],
            scratch_shapes=[pltpu.VMEM((SEQ, PAIR), BF)]
            + [pltpu.VMEM((SEQ, PAIR), F32)] * 3
            + [pltpu.VMEM((3, SEQ, PAIR), BF)],
        ),
        out_shape=[
            jax.ShapeDtypeStruct((tokens, width), BF),
            jax.ShapeDtypeStruct((seqs, 1, width), F32),
        ],
        input_output_aliases={5: 0, 6: 1} if before else {},
        compiler_params=ROOM,
        name="attend_back",
    )(place.reshape(1), prob, low, d_attended, turns, *before)


def tables(positions):
    frequency = 10000.0 ** (-(jnp.arange(ROT // 2, dtype=F32) * 2.0) / ROT)
    angles = frequency[:, None] * positions[None, :]
    cosine, sine = jnp.cos(angles).T, jnp.sin(angles).T
    none = jnp.zeros_like(sine)
    still = jnp.zeros((sine.shape[0], HEAD_DIM - ROT), F32)
    return jnp.stack(
        [
            jnp.concatenate([cosine, cosine, still + 1.0] * 2, axis=1),
            jnp.concatenate([-sine, none, still] * 2, axis=1),
            jnp.concatenate([none, sine, still] * 2, axis=1),
        ]
    )


def feed_forward(normed_all, fc1_cols, bias):
    pre_act = times(normed_all, fc1_cols) + bias
    root = (2.0 / jnp.pi) ** 0.5
    square = pre_act * pre_act
    curve = jnp.tanh(root * pre_act * (1.0 + 0.044715 * square))
    activation = (0.5 * pre_act * (1.0 + curve)).astype(BF)
    slope = (
        0.5 * (1.0 + curve)
        + 0.5 * pre_act * (1.0 - curve * curve) * root * (1.0 + 3 * 0.044715 * square)
    ).astype(BF)
    return activation, slope


def shards(
    inputs,
    segments,
    positions,
    ln_gain,
    ln_bias,
    w_qkv,
    b_qkv,
    w_dense,
    b_dense,
    w_fc1,
    b_fc1,
    w_fc2,
    b_fc2,
    cotangent,
):
    reps, group = lax.axis_size("rep"), lax.axis_size("shard")
    rep, place = lax.axis_index("rep"), lax.axis_index("shard")
    core = rep & 1
    tokens, width = inputs.shape
    rows = width // group
    slab = rows // reps
    hidden = w_fc1.shape[1] // group
    pairs = rows // PAIR
    line = Order()
    def gathered(array):
        return lax.all_gather(array, "rep", axis=0, tiled=True)

    owners = [(place + hop) % group for hop in range(group)]

    def qkv_rows(w):
        return tuple(
            jnp.concatenate(
                [
                    lax.dynamic_slice(w, (rep * slab, at * width + owner * rows), (slab, rows))
                    for at in range(3)
                ],
                axis=1,
            )
            for owner in owners
        )

    def fc1_rows(w):
        return jnp.concatenate(
            [
                lax.dynamic_slice(w, (rep * slab, owner * hidden), (slab, hidden))
                for owner in range(group)
            ]
        )

    qkv_pieces = [
        piece if hop == 0 else ring(piece, "shard", hop)
        for hop, piece in enumerate(line.step(qkv_rows, w_qkv))
    ]
    fc1_pieces = exchanged(line.step(fc1_rows, w_fc1))
    small = jnp.concatenate(
        [ln_gain, ln_bias, b_qkv, b_dense + b_fc2, positions.astype(F32)]
    ).reshape(1, -1)
    small = doubled(small, place, line)
    gain = small[:, :rows].reshape(width)
    shift = small[:, rows : 2 * rows].reshape(width)
    bias_qkv = lax.dynamic_slice_in_dim(
        small[:, 2 * rows : 5 * rows].reshape(3, width), place * rows, rows, 1
    ).reshape(1, 3 * rows)
    bias_out = small[:, 5 * rows : 6 * rows].reshape(width)
    group_positions = small[:, 6 * rows :]

    normed = [line.step(lambda *o: ln_forward(*o, reps, group), inputs, gain, shift)]
    normed.append(ring(line.hold(normed[0]), "shard", 1))
    qkv_cols = gathered(line.step(lambda *p: placed(p, place), *qkv_pieces))

    ring_order = [(place - hop) % group for hop in range(group)]
    ring_positions = jnp.concatenate(
        [lax.dynamic_index_in_dim(group_positions, at, 0, keepdims=False) for at in ring_order]
    )
    start = (
        jnp.arange(SEQ, dtype=jnp.int32)[None, None]
        - group_positions.astype(jnp.int32).reshape(-1, 1, SEQ)
    )
    per_seq = SEQ // tokens
    if group == per_seq:
        turn_place = place
        by_seq = from_seq = lambda array, axis=0: array
    else:
        turn_place = jnp.zeros_like(place)
        seq_order = [at // per_seq * per_seq + (-at) % per_seq for at in range(group)]

        def taken(array, order, axis):
            return jnp.concatenate(
                [
                    lax.dynamic_slice_in_dim(array, at * tokens, tokens, axis)
                    for at in order
                ],
                axis=axis,
            )

        by_seq = lambda array, axis=0: taken(
            array, [(place - at) % group for at in seq_order], axis
        )
        from_seq = lambda array, axis=0: taken(
            array, [at // per_seq * per_seq + (-at) % per_seq for at in ring_order], axis
        )

    turns = line.step(lambda p: by_seq(tables(p), 1), ring_positions)

    def begin(block):
        return jnp.concatenate([block, jnp.zeros(((group - 1) * tokens, width), BF)])

    def put(hop):
        return lambda whole, block: lax.dynamic_update_slice_in_dim(
            whole, block, hop * tokens, 0
        )

    normed_all = line.step(begin, normed[0])
    cot_all = line.step(begin, cotangent)
    def project_some(first, count, *before):
        return line.step(
            lambda a, b, c, *d: project(a, b, c, tokens, first, count, d),
            normed_all,
            qkv_cols,
            bias_qkv,
            *before,
        )

    for hop in range(1, group):
        normed[hop] = line.hold(normed[hop])
        if hop == 1:
            fc1_cols = gathered(line.hold(fc1_pieces))
        if hop + 1 < group:
            normed.append(ring(normed[hop], "shard", 1))
        else:
            cots = [line.hold(cotangent)]
            cots.append(ring(cots[0], "shard", 1))
        normed_all = line.step(put(hop), normed_all, normed[hop])
        if hop == group - 2:
            projected = project_some(0, group - 1)

    projected = by_seq(project_some(group - 1, 1, projected))
    calls = 2 if pairs > 1 else 1
    each = pairs // calls
    kept = []

    def attend_some(call, before):
        attended, *rest = line.step(
            lambda p, *b: attend(p, turns, start, turn_place, call * each, each, tokens, b),
            projected,
            *before,
        )
        kept.append(rest)
        return (attended,)

    attended = attend_some(0, ())
    for hop in range(1, group):
        cots[hop] = line.hold(cots[hop])
        if hop + 1 < group:
            cots.append(ring(cots[hop], "shard", 1))
        cot_all = line.step(put(hop), cot_all, cots[hop])
        if hop == 1:
            activation, slope = line.step(feed_forward, normed_all, fc1_cols, b_fc1)
        if hop == 2:
            if calls > 1:
                attended = attend_some(1, attended)
            out_part = line.step(
                lambda a, b, c, d: push(a, b, c, d, False, place, group),
                from_seq(attended[0]),
                w_dense,
                activation,
                w_fc2,
            )
            out_sum = lax.psum_scatter(out_part, "shard", scatter_dimension=0, tiled=True)
    (attended,) = attended
    attended = from_seq(attended)

    def grad(left, right, *also):
        sent = line.step(
            lambda a, b, *c: half_grads(a, b, 1 - core, reps, None, *c), left, right, *also
        )
        return swap(sent, "rep", 1)

    def grad_sum(left, right, came, *also):
        if reps == 8 and not (left.shape[1] // reps % 128):
            own, *sent = line.step(
                lambda a, b, c, *d: grad_sums(a, b, rep, c, *d), left, right, came, *also
            )
            halving = Halving(rep, own, 2)
            halving.send(line, sent)
            return halving
        own = line.step(
            lambda a, b, c, *d: half_grads(a, b, core, reps, c, *d), left, right, came, *also
        )
        halving = Halving(rep, own, 2)
        halving.send(line)
        return halving

    def attend_back_some(call, before):
        return line.step(
            lambda d, t, *b: attend_back(
                kept[call], d, t, turn_place, call * each, tokens, pairs, b
            ),
            d_attended,
            turns,
            *before,
        )

    out_came = grad(activation, cot_all, attended)
    d_pre = line.step(pull, cot_all, w_fc2, slope)
    fc1_came = grad(normed_all, d_pre)
    out_grads = grad_sum(activation, cot_all, out_came, attended)
    d_attended = by_seq(line.step(pull, cot_all, w_dense))
    back = attend_back_some(0, ())
    fc1_sum = grad_sum(normed_all, d_pre, fc1_came)
    out_grads.further(line)
    for call in range(1, calls):
        back = attend_back_some(call, back)
    d_projected, d_bias_qkv = back
    d_projected = from_seq(d_projected)
    d_normed_part = line.step(
        lambda a, b, c, d: push(a, b, c, d, True, place), d_projected, qkv_cols, d_pre, fc1_cols
    )
    d_normed_sum = Passing(line, d_normed_part, tokens)
    out_piece = out_grads.end(line)
    fc1_sum.further(line)
    out_whole = gathered(line.hold(out_piece))
    qkv_came = grad(normed_all, d_projected)
    block_out = line.step(
        lambda x, b, p: x.astype(F32) + b + p.astype(F32), inputs, bias_out, out_sum
    )
    qkv_sum = grad_sum(normed_all, d_projected, qkv_came)
    fc1_pieces = exchanged(line.hold(fc1_sum.end(line)))
    d_normed_sum.further()
    qkv_sum.further(line)

    def bias_sums(d_bias_qkv, cotangent, d_pre):
        d_bias_all = lax.dynamic_update_slice_in_dim(
            jnp.zeros((3, width), F32),
            jnp.sum(d_bias_qkv[:, 0], axis=0).reshape(3, rows),
            place * rows,
            1,
        )
        ones = jnp.ones((8, group * tokens), BF)
        return (
            jnp.concatenate(
                [
                    d_bias_all.reshape(group, 3 * rows),
                    jnp.sum(cotangent.astype(F32), axis=0).reshape(group, rows),
                ],
                axis=1,
            ),
            times(ones, d_pre)[0],
        )

    early_sums, d_bias_fc1 = line.step(bias_sums, d_bias_qkv, cotangent, d_pre)
    qkv_piece = qkv_sum.end(line)
    d_normed_sum.hold()
    fc1_slab = line.step(lambda p: widened(p, group, hidden), fc1_pieces)
    qkv_pieces = exchanged(line.hold(qkv_piece))
    fc1_whole = gathered(line.hold(fc1_slab))
    qkv_spread = Spread(line, line.step(lambda p: widened(p, group, rows), qkv_pieces))
    d_normed_sum.further()
    fc2_total, dense_total = line.step(
        lambda a: split_rows(a, reps, (hidden // reps, slab)), out_whole
    )
    grad_inputs, norm_sums = line.step(
        lambda x, g, c, *p: ln_backward(x, g, c, p, reps, group),
        inputs,
        gain,
        cotangent,
        *d_normed_sum.end(),
    )

    sums = line.step(
        lambda early, norm_sums: jnp.concatenate(
            [early, norm_sums[0].reshape(group, rows), norm_sums[1].reshape(group, rows)], axis=1
        ),
        early_sums,
        norm_sums,
    )
    qkv_spread.across()
    sums = owned_sum(line, sums, place)
    sums = line.hold(jnp.concatenate([sums, d_bias_fc1]))
    sums = line.hold(sums + swap(sums, "rep", 1))
    fc1_total = line.step(lambda a: a.astype(F32), fc1_whole)
    qkv_spread = qkv_spread.shared()
    bit = 2
    while bit < reps:
        sums = line.hold(sums + swap(sums, "rep", bit))
        bit *= 2
    qkv_total = line.step(lambda *p: assemble(p, rep), *qkv_spread)
    cot_total = sums[3 * rows : 4 * rows]
    return (
        block_out,
        grad_inputs,
        sums[4 * rows : 5 * rows],
        sums[5 * rows : 6 * rows],
        qkv_total,
        sums[: 3 * rows],
        dense_total,
        cot_total,
        fc1_total,
        sums[6 * rows :],
        fc2_total,
        cot_total,
    )


def solution(mesh):
    both, shard = P(("rep", "shard")), P("shard")
    wide, held = P(("rep", "shard"), None), P("shard", None)
    return jax.shard_map(
        shards,
        mesh=mesh,
        in_specs=(
            wide, both, both, shard, shard, held, shard, held, shard, held, shard, held, shard, wide
        ),
        out_specs=(
            wide, wide, shard, shard, held, shard, held, shard, held, shard, held, shard
        ),
        check_vma=False,
    )
```

```python
import functools

import jax
import jax.numpy as jnp
from jax import lax
from jax.experimental import pallas as pl
from jax.experimental.pallas import tpu as pltpu
from jax.sharding import PartitionSpec as P

HEAD_DIM = 64
ROT = 32
SEQ = 1024
PAIR = 2 * HEAD_DIM
BF = jnp.bfloat16
F32 = jnp.float32
ROOM = pltpu.CompilerParams(vmem_limit_bytes=56 * 2**20)
ANY = pl.BlockSpec(memory_space=pl.ANY)


def ring(array, axis, distance):
    size = lax.axis_size(axis)
    return lax.ppermute(array, axis, [(i, (i + distance) % size) for i in range(size)])


def swap(array, axis, mask):
    size = lax.axis_size(axis)
    return lax.ppermute(array, axis, [(i, i ^ mask) for i in range(size)])


def contract_rows(left_side, right_side):
    return lax.dot_general(
        left_side, right_side, (((0,), (0,)), ((), ())), preferred_element_type=F32
    )


def times_transpose(left_side, right_side):
    return lax.dot_general(
        left_side, right_side, (((1,), (1,)), ((), ())), preferred_element_type=F32
    )


def times(left_side, right_side):
    return jnp.dot(left_side, right_side, preferred_element_type=F32)


class Order:
    def __init__(self):
        self.last = None

    def step(self, work, *operands):
        if self.last is not None:
            operands, _ = lax.optimization_barrier((operands, self.last))
        result = work(*operands)
        self.last = jax.tree.leaves(result)
        return result

    def hold(self, array):
        return self.step(lambda a: a, array)


def doubled(row, place, line):
    bit = 1
    while bit < lax.axis_size("shard"):
        row = line.hold(row)
        other = swap(row, "shard", bit)
        upper = (place & bit) > 0
        row = jnp.concatenate([jnp.where(upper, other, row), jnp.where(upper, row, other)])
        bit *= 2
    return row


def owned_sum(line, values, place):
    bit = lax.axis_size("shard") >> 1
    while bit:
        upper = ((place & bit) > 0).astype(jnp.int32)
        count = values.shape[0] // 2
        sent, kept = (
            lax.dynamic_slice_in_dim(values, side * count, count, 0) for side in (1 - upper, upper)
        )
        values = line.hold(kept + swap(sent, "shard", bit))
        bit >>= 1
    return values[0]


class Halving:
    def __init__(self, rep, array, parts):
        count = lax.axis_size("rep").bit_length() - 2
        self.rep = rep
        array = array.reshape((2,) * count + (array.shape[0] >> count,) + array.shape[1:])
        rows = array.shape[count] // parts
        self.arrays = [array] * parts
        self.spans = [(part * rows, rows) for part in range(parts)]
        bits = list(range(count, 0, -1))
        self.bits = [list(bits) for _ in range(parts)]
        self.todo = [
            bits[::-1][part % count :] + bits[::-1][: part % count] for part in range(parts)
        ]

    def pick(self, part, array, mine):
        axis = self.bits[part].index(self.todo[part][0])
        bit = (self.rep >> self.todo[part][0]) & 1
        starts, sizes = [0] * array.ndim, list(array.shape)
        starts[axis], sizes[axis] = (bit if mine else 1 - bit), 1
        starts[len(self.bits[part])], sizes[len(self.bits[part])] = self.spans[part]
        half = lax.dynamic_slice(array, starts, sizes)
        return half.reshape(half.shape[:axis] + half.shape[axis + 1 :])

    def outgoing(self, *arrays):
        return tuple(self.pick(part, array, False) for part, array in enumerate(arrays))

    def added(self, *operands):
        count = len(operands) // 2
        return tuple(
            (self.pick(part, operands[part], True).astype(F32) + operands[count + part].astype(F32))
            .astype(BF)
            for part in range(count)
        )

    def send(self, line, sent=None):
        if sent is None:
            sent = line.step(self.outgoing, *self.arrays)
        self.came = [
            swap(piece, "rep", 1 << todo[0]) for piece, todo in zip(sent, self.todo)
        ]

    def take(self, line):
        self.arrays = line.step(self.added, *self.arrays, *self.came)
        for part, todo in enumerate(self.todo):
            self.bits[part].remove(todo[0])
            self.todo[part] = todo[1:]
            self.spans[part] = (0, self.spans[part][1])

    def further(self, line):
        if len(self.todo[0]) > 1:
            self.take(line)
            self.send(line)

    def end(self, line):
        while len(self.todo[0]) > 1:
            self.further(line)
        self.take(line)
        return jnp.concatenate(self.arrays, axis=0)


class Passing:
    def __init__(self, line, array, tokens):
        self.line, self.group = line, array.shape[0] // tokens
        self.block = lambda hop: (hop % self.group * tokens, tokens)
        self.array, self.hop = array, 1
        sent = line.step(lambda a: lax.slice_in_dim(a, tokens, 2 * tokens, axis=0), array)
        self.came = ring(sent, "shard", 1)

    def hold(self):
        self.came = self.line.hold(self.came)

    def further(self):
        self.hop += 1
        first, count = self.block(self.hop)
        sent = self.line.step(
            lambda a, b: (
                lax.slice_in_dim(a, first, first + count, axis=0).astype(F32) + b.astype(F32)
            ).astype(BF),
            self.array,
            self.came,
        )
        self.came = ring(sent, "shard", 1)

    def end(self):
        while self.hop + 1 < self.group:
            self.further()
        return lax.slice_in_dim(self.array, 0, self.block(0)[1], axis=0), self.came


def place_kernel(width, place_ref, *refs):
    *pieces, out_ref = refs
    size = len(pieces)
    length, columns = pieces[0].shape
    for hop, piece in enumerate(pieces):
        owner = lax.rem(place_ref[0] - hop + size, size)
        if width is None:
            out_ref[pl.ds(pl.multiple_of(owner * length, length), length), :] = piece[...]
        else:
            count = columns // width
            for at in range(count):
                first = pl.multiple_of((at * size + owner) * width, width)
                out_ref[:, pl.ds(first, width)] = piece[:, at * width : (at + 1) * width]


def placed(pieces, place, width=None):
    length, columns = pieces[0].shape
    shape = (
        (length * len(pieces), columns) if width is None else (length, columns * len(pieces))
    )
    whole = pl.BlockSpec(memory_space=pltpu.VMEM)
    return pl.pallas_call(
        functools.partial(place_kernel, width),
        in_specs=[pl.BlockSpec(memory_space=pltpu.SMEM)] + [whole] * len(pieces),
        out_specs=whole,
        out_shape=jax.ShapeDtypeStruct(shape, pieces[0].dtype),
        compiler_params=ROOM,
        name="placed",
    )(place.reshape(1), *pieces)


def exchanged(array):
    return lax.all_to_all(array, "shard", 0, 0, tiled=True)


def widen_kernel(size, width, rows_ref, out_ref):
    length = rows_ref.shape[0] // size
    for owner in range(size):
        for at in range(rows_ref.shape[1] // width):
            first = (at * size + owner) * width
            out_ref[:, first : first + width] = rows_ref[
                owner * length : (owner + 1) * length, at * width : (at + 1) * width
            ]


def widened(array, size, width):
    rows, columns = array.shape
    return pl.pallas_call(
        functools.partial(widen_kernel, size, width),
        out_shape=jax.ShapeDtypeStruct((rows // size, columns * size), array.dtype),
        compiler_params=ROOM,
        name="widened",
    )(array)


def split_kernel(in_ref, *refs):
    first = 0
    for ref in refs:
        ref[...] = in_ref[first : first + ref.shape[0]].astype(F32)
        first += ref.shape[0]


def split_rows(array, reps, heights):
    rows, columns = array.shape
    return pl.pallas_call(
        split_kernel,
        grid=(reps,),
        in_specs=[pl.BlockSpec((rows // reps, columns), lambda r: (r, 0))],
        out_specs=[pl.BlockSpec((height, columns), lambda r: (r, 0)) for height in heights],
        out_shape=[jax.ShapeDtypeStruct((height * reps, columns), F32) for height in heights],
        compiler_params=ROOM,
        name="split_rows",
    )(array)


class Spread:
    def __init__(self, line, array):
        self.line, self.size = line, lax.axis_size("rep")
        self.pieces = {0: array}
        steps = (2, 4) if self.size == 8 else range(2, self.size, 2)
        for mask in steps:
            self.pieces[mask] = swap(array, "rep", mask)

    def across(self):
        if self.size != 8:
            return
        half = self.pieces[0].shape[0] // 2
        self.pieces[2], self.pieces[4], first, second = self.line.step(
            lambda a, b: (a, b, a[:half], b[half:]), self.pieces[2], self.pieces[4]
        )
        self.halves = (swap(first, "rep", 4), swap(second, "rep", 2))

    def shared(self):
        masks = range(0, self.size, 2)
        if self.size == 8:
            self.pieces[6] = self.line.step(lambda *h: jnp.concatenate(h), *self.halves)
        held = self.line.step(lambda *p: p, *[self.pieces[mask] for mask in masks])
        return [piece for one in held for piece in (one, swap(one, "rep", 1))]


def assemble_kernel(rep_ref, *refs):
    for mask, piece in enumerate(refs[:-1]):

        @pl.when(pl.program_id(0) == mask)
        def _(piece=piece):
            refs[-1][...] = piece[...].astype(F32)


def assemble(pieces, rep):
    size = len(pieces)
    rows, columns = pieces[0].shape
    whole = pl.BlockSpec((rows, columns), lambda m, r: (0, 0), pipeline_mode=pl.Buffered(1))
    return pl.pallas_call(
        assemble_kernel,
        grid_spec=pltpu.PrefetchScalarGridSpec(
            num_scalar_prefetch=1,
            grid=(size,),
            in_specs=[whole] * size,
            out_specs=pl.BlockSpec((rows, columns), lambda m, r: (r[0] ^ m, 0)),
        ),
        out_shape=jax.ShapeDtypeStruct((rows * size, columns), F32),
        compiler_params=ROOM,
        name="assemble",
    )(rep.reshape(1), *pieces)


def grad_kernel(which_ref, left_ref, right_ref, *refs):
    *more, out_ref = refs
    left = left_ref[...]
    if more and more[0].shape[0] == left.shape[0]:
        both = more.pop(0)
        lanes = both.shape[1] // 2
        left = jnp.concatenate(
            [left, jnp.where(which_ref[0] == 0, both[:, :lanes], both[:, lanes:])], axis=1
        )
    total = contract_rows(left, right_ref[...])
    if more:
        total = total + more[0][...].astype(F32)
    out_ref[...] = total.astype(BF)


def chip_of(step):
    return step // 2, (step + 1) // 2 % 2


def grad_sum_kernel(at_ref, left_ref, right_ref, *refs):
    *more, came_ref, own_ref, fast_ref, slow_ref = refs
    left = left_ref[...]
    if more:
        both = more[0][...]
        lanes = both.shape[1] // 2
        left = jnp.concatenate(
            [left, jnp.where(at_ref[0] == 0, both[:, :lanes], both[:, lanes:])], axis=1
        )
    total = (contract_rows(left, right_ref[...]) + came_ref[...].astype(F32)).astype(BF)
    own_ref[...] = total
    slow, fast = chip_of(pl.program_id(0))
    half = total.shape[0] // 2

    @pl.when(fast == 1)
    def _():
        fast_ref[0] = total[:half]

    @pl.when(slow == 1)
    def _():
        slow_ref[0] = total[half:]


def grad_sums(left, right, rep, came, also=None):
    tokens, height = left.shape
    length = right.shape[1]
    height //= 8
    extra = 0 if also is None else also.shape[1] // 8
    total = height + extra
    block = lambda j, at: 2 * (at[2] ^ chip_of(j)[0]) + (at[1] ^ chip_of(j)[1])
    half = (1, total // 2, length)
    return pl.pallas_call(
        grad_sum_kernel,
        grid_spec=pltpu.PrefetchScalarGridSpec(
            num_scalar_prefetch=1,
            grid=(4,),
            in_specs=[
                pl.BlockSpec((tokens, height), lambda j, at: (0, 2 * block(j, at) + at[0])),
                pl.BlockSpec(memory_space=pltpu.VMEM),
            ]
            + (
                []
                if also is None
                else [pl.BlockSpec((tokens, 128), lambda j, at: (0, block(j, at)))]
            )
            + [pl.BlockSpec((total, length), lambda j, at: (block(j, at), 0))],
            out_specs=[
                pl.BlockSpec((total, length), lambda j, at: (block(j, at), 0)),
                pl.BlockSpec(half, lambda j, at: (at[2] ^ (j // 2), 0, 0)),
                pl.BlockSpec(half, lambda j, at: (at[1] ^ (1 - j // 3), 0, 0)),
            ],
        ),
        out_shape=[
            jax.ShapeDtypeStruct((4 * total, length), BF),
            jax.ShapeDtypeStruct((2,) + half[1:], BF),
            jax.ShapeDtypeStruct((2,) + half[1:], BF),
        ],
        compiler_params=ROOM,
        name="grad_sums",
    )(
        jnp.stack([rep & 1, (rep >> 1) & 1, rep >> 2]),
        left,
        right,
        *([] if also is None else [also]),
        came,
    )


def half_grads(left, right, which, reps, came=None, also=None):
    tokens, height = left.shape
    length = right.shape[1]
    height //= reps
    extra = 0 if also is None else also.shape[1] // reps
    if height % 128 or extra not in (0, 64):
        sides = [left] if also is None else [left, also]
        total = [
            contract_rows(
                lax.dynamic_index_in_dim(
                    side.reshape(tokens, reps // 2, 2, -1), which, 2, keepdims=False
                ).reshape(tokens, -1),
                right,
            ).reshape(reps // 2, -1, length)
            for side in sides
        ]
        total = jnp.concatenate(total, axis=1).reshape(-1, length)
        return (total if came is None else total + came.astype(F32)).astype(BF)
    block = pl.BlockSpec((height + extra, length), lambda b, w: (b, 0))
    more = [] if also is None else [also]
    more_specs = [] if also is None else [pl.BlockSpec((tokens, 128), lambda b, w: (0, b))]
    return pl.pallas_call(
        grad_kernel,
        grid_spec=pltpu.PrefetchScalarGridSpec(
            num_scalar_prefetch=1,
            grid=(reps // 2,),
            in_specs=[
                pl.BlockSpec((tokens, height), lambda b, w: (0, 2 * b + w[0])),
                pl.BlockSpec(memory_space=pltpu.VMEM),
            ]
            + more_specs
            + ([] if came is None else [block]),
            out_specs=block,
        ),
        out_shape=jax.ShapeDtypeStruct((reps // 2 * (height + extra), length), BF),
        compiler_params=ROOM,
        name="half_grads",
    )(which.reshape(1), left, right, *more, *([] if came is None else [came]))


def ln_forward_kernel(reps, group, x_ref, gain_ref, shift_ref, out_ref):
    x = x_ref[...].astype(F32)
    centred = x - jnp.mean(x, axis=-1, keepdims=True)
    spread = jnp.mean(centred * centred, axis=-1, keepdims=True)
    normed = (centred * lax.rsqrt(spread + 1e-05)) * gain_ref[...] + shift_ref[...]
    slab = x.shape[1] // (reps * group)
    out_ref[...] = jnp.concatenate(
        [
            normed[:, (g * reps + r) * slab : (g * reps + r + 1) * slab]
            for r in range(reps)
            for g in range(group)
        ],
        axis=1,
    ).astype(BF)


def ln_forward(inputs, gain, shift, reps, group):
    tokens, width = inputs.shape
    return pl.pallas_call(
        functools.partial(ln_forward_kernel, reps, group),
        out_shape=jax.ShapeDtypeStruct((tokens, width), BF),
        compiler_params=ROOM,
        name="ln_forward",
    )(inputs, gain.reshape(1, width), shift.reshape(1, width))


def ln_backward_kernel(reps, group, x_ref, gain_ref, cot_ref, a_ref, b_ref, out_ref, sums_ref):
    x = x_ref[...].astype(F32)
    centred = x - jnp.mean(x, axis=-1, keepdims=True)
    spread = jnp.mean(centred * centred, axis=-1, keepdims=True)
    inverse = lax.rsqrt(spread + 1e-05)
    xhat = centred * inverse
    mixed = a_ref[...].astype(F32) + b_ref[...].astype(F32)
    slab = x.shape[1] // (reps * group)
    d_normed = jnp.concatenate(
        [
            mixed[:, (r * group + g) * slab : (r * group + g + 1) * slab]
            for g in range(group)
            for r in range(reps)
        ],
        axis=1,
    )
    sums_ref[0:1] = jnp.sum(d_normed * xhat, axis=0, keepdims=True)
    sums_ref[1:2] = jnp.sum(d_normed, axis=0, keepdims=True)
    scaled = d_normed * gain_ref[...]
    out_ref[...] = cot_ref[...].astype(F32) + inverse * (
        scaled
        - jnp.mean(scaled, axis=-1, keepdims=True)
        - xhat * jnp.mean(scaled * xhat, axis=-1, keepdims=True)
    )


def ln_backward(inputs, gain, cotangent, parts, reps, group):
    tokens, width = inputs.shape
    return pl.pallas_call(
        functools.partial(ln_backward_kernel, reps, group),
        out_shape=[
            jax.ShapeDtypeStruct((tokens, width), F32),
            jax.ShapeDtypeStruct((2, width), F32),
        ],
        compiler_params=ROOM,
        name="ln_backward",
    )(inputs, gain.reshape(1, width), cotangent, *parts)


def pull_kernel(cot_ref, weight_ref, *refs):
    total = times_transpose(cot_ref[...], weight_ref[...])
    if len(refs) > 1:
        total = total * refs[0][...].astype(F32)
    refs[-1][...] = total.astype(BF)


def pull(cot_all, weight, *slope):
    height, width = cot_all.shape
    hidden = weight.shape[0]
    tile = min(512, hidden)
    block = pl.BlockSpec((height, tile), lambda j: (0, j))
    return pl.pallas_call(
        pull_kernel,
        grid=(hidden // tile,),
        in_specs=[
            pl.BlockSpec(memory_space=pltpu.VMEM),
            pl.BlockSpec((tile, width), lambda j: (j, 0)),
        ]
        + [block] * len(slope),
        out_specs=block,
        out_shape=jax.ShapeDtypeStruct((height, hidden), BF),
        compiler_params=ROOM,
        name="pull",
    )(cot_all, weight, *slope)


def push_kernel(transposed, size, place_ref, a_ref, b_ref, c_ref, d_ref, out_ref):
    product = times_transpose if transposed else times
    total = product(a_ref[...], b_ref[...]) + product(c_ref[...], d_ref[...])
    if size is None:
        out_ref[...] = total.astype(BF)
        return
    block = out_ref.shape[0] // size
    for hop in range(size):
        out_ref[token_block(place_ref[0], hop, size, block)] = total[
            hop * block : (hop + 1) * block
        ].astype(BF)


def push(a, b, c, d, transposed, place, size=None):
    height = a.shape[0]
    length = b.shape[0 if transposed else 1]
    tile = min(512, length)
    full = lambda x: pl.BlockSpec(memory_space=pltpu.VMEM)
    if transposed:
        part = lambda x: pl.BlockSpec((tile, x.shape[1]), lambda j, z: (j, 0))
    else:
        part = lambda x: pl.BlockSpec((x.shape[0], tile), lambda j, z: (0, j))
    return pl.pallas_call(
        functools.partial(push_kernel, transposed, size),
        grid_spec=pltpu.PrefetchScalarGridSpec(
            num_scalar_prefetch=1,
            grid=(length // tile,),
            in_specs=[full(a), part(b), full(c), part(d)],
            out_specs=pl.BlockSpec((height, tile), lambda j, z: (0, j)),
        ),
        out_shape=jax.ShapeDtypeStruct((height, length), BF),
        compiler_params=ROOM,
        name="push",
    )(place.reshape(1), a, b, c, d)


def project_kernel(rows_ref, weight_ref, bias_ref, *refs):
    refs[-1][...] = times(rows_ref[...], weight_ref[...]) + bias_ref[...]


def project(normed_all, weight, bias, tokens, first, count, before):
    height, width = normed_all.shape
    length = weight.shape[1]
    tile = length // 3
    here = first // count
    return pl.pallas_call(
        project_kernel,
        grid=(3,),
        in_specs=[
            pl.BlockSpec((count * tokens, width), lambda j: (here, 0)),
            pl.BlockSpec((width, tile), lambda j: (0, j)),
            pl.BlockSpec((1, tile), lambda j: (0, j)),
        ]
        + [ANY] * len(before),
        out_specs=pl.BlockSpec((count * tokens, tile), lambda j: (here, j)),
        out_shape=jax.ShapeDtypeStruct((height, length), F32),
        input_output_aliases={3: 0} if before else {},
        compiler_params=ROOM,
        name="project",
    )(normed_all, weight, bias, *before)


def turned(u, turn, sign):
    return (
        u * turn[0]
        + sign * (pltpu.roll(u, PAIR - ROT // 2, 1) * turn[1])
        + sign * (pltpu.roll(u, ROT // 2, 1) * turn[2])
    )


def spans(rows, block):
    first = 0
    for part in range(rows // block):
        yield part, first, (part + 1) * block
        first += (part + 1) * block


def token_block(place, hop, count, block):
    return pl.ds(pl.multiple_of(lax.rem(place - hop + count, count) * block, block), block)


def attend_kernel(block, place_ref, q_ref, k_ref, v_ref, turn_ref, start_ref, *refs):
    att_ref, prob_ref, low_ref, out_ref = refs[-4:]
    rows = q_ref.shape[0]
    count = rows // block
    for hop in range(count):
        here, there = slice(hop * block, (hop + 1) * block), token_block(place_ref[0], hop, count, block)
        turn = [turn_ref[k, here] for k in range(3)]
        query = turned(q_ref[here], turn, 1.0).astype(BF)
        low_ref[0, there] = (query * HEAD_DIM ** (-0.5)).astype(BF)
        low_ref[1, there] = turned(k_ref[here], turn, 1.0).astype(BF)
        low_ref[2, there] = v_ref[here].astype(BF)
    start = start_ref[0]
    for head in range(2):
        lanes = slice(head * HEAD_DIM, (head + 1) * HEAD_DIM)
        key_h = low_ref[1, :, lanes]
        value_t = low_ref[2, :, lanes].T
        for part, first, length in spans(rows, block):
            own = slice(part * block, (part + 1) * block)
            scores = times_transpose(key_h[:length], low_ref[0, own, lanes])
            place = lax.broadcasted_iota(jnp.int32, (length, block), 0)
            asker = lax.broadcasted_iota(jnp.int32, (length, block), 1) + part * block
            allowed = (place >= start[:, own]) & (place <= asker)
            scores = jnp.where(allowed, scores, -1e30)
            exponent = jnp.exp(scores - jnp.max(scores, axis=0, keepdims=True))
            softmax = exponent * (1.0 / jnp.sum(exponent, axis=0, keepdims=True))
            attention = softmax.astype(BF)
            prob_ref[0, head, first : first + length] = attention
            out_ref[own, lanes] = times(value_t[:, :length], attention).T.astype(BF)
    for hop in range(count):
        att_ref[hop * block : (hop + 1) * block] = out_ref[token_block(place_ref[0], hop, count, block)]


def attend(projected, turns, start, place, first, count, block, before):
    tokens, width = projected.shape
    pairs, seqs = width // (3 * PAIR), tokens // SEQ
    stored = sum(length for _, _, length in spans(SEQ, block))
    wide = lambda at: pl.BlockSpec((SEQ, PAIR), lambda s, p, z: (s, at * pairs + first + p))
    return pl.pallas_call(
        functools.partial(attend_kernel, block),
        grid_spec=pltpu.PrefetchScalarGridSpec(
            num_scalar_prefetch=1,
            grid=(seqs, count),
            in_specs=[
                wide(0),
                wide(1),
                wide(2),
                pl.BlockSpec((3, SEQ, PAIR), lambda s, p, z: (0, s, 0)),
                pl.BlockSpec((1, 1, SEQ), lambda s, p, z: (s, 0, 0)),
            ]
            + [ANY] * len(before),
            out_specs=[
                pl.BlockSpec((SEQ, PAIR), lambda s, p, z: (s, first + p)),
                pl.BlockSpec((1, 2, stored, block), lambda s, p, z: (s, p, 0, 0)),
                pl.BlockSpec((3, SEQ, PAIR), lambda s, p, z: (0, s, p)),
            ],
            scratch_shapes=[pltpu.VMEM((SEQ, PAIR), BF)],
        ),
        out_shape=[
            jax.ShapeDtypeStruct((tokens, pairs * PAIR), BF),
            jax.ShapeDtypeStruct((seqs, 2 * count, stored, block), BF),
            jax.ShapeDtypeStruct((3, tokens, count * PAIR), BF),
        ],
        input_output_aliases={6: 0} if before else {},
        compiler_params=ROOM,
        name="attend",
    )(place.reshape(1), projected, projected, projected, turns, start, *before)


def attend_back_kernel(block, place_ref, prob_ref, low_ref, datt_ref, turn_ref, *refs):
    dproj_ref, bsum_ref, d_ref, dq_ref, dk_ref, dv_ref, done_ref = refs[-7:]
    rows = datt_ref.shape[0]
    count = rows // block
    stage = pl.program_id(2)

    @pl.when(stage == 0)
    def _():
        for hop in range(count):
            d_ref[token_block(place_ref[0], hop, count, block)] = datt_ref[
                hop * block : (hop + 1) * block
            ]
        for head in range(2):
            lanes = slice(head * HEAD_DIM, (head + 1) * HEAD_DIM)
            key_t = low_ref[1, :, lanes].T
            value_h = low_ref[2, :, lanes]
            for part, first, length in reversed(list(spans(rows, block))):
                own = slice(part * block, (part + 1) * block)
                query_p = low_ref[0, own, lanes]
                d_att_p = d_ref[own, lanes]
                attention = prob_ref[0, head, first : first + length]
                d_attention = times_transpose(value_h[:length], d_att_p)
                softmax = attention.astype(F32)
                weighted = softmax * d_attention
                d_scores = (
                    weighted - softmax * jnp.sum(weighted, axis=0, keepdims=True)
                ).astype(BF)
                dq_ref[own, lanes] = times(key_t[:, :length], d_scores).T * HEAD_DIM ** (-0.5)
                d_value = times(attention, d_att_p)
                d_key = times(d_scores, query_p)
                if length == rows:
                    dv_ref[:, lanes] = d_value
                    dk_ref[:, lanes] = d_key
                else:
                    dv_ref[:length, lanes] += d_value
                    dk_ref[:length, lanes] += d_key
        for hop in range(count):
            here = slice(hop * block, (hop + 1) * block)
            there = token_block(place_ref[0], hop, count, block)
            turn = [turn_ref[k, here] for k in range(3)]
            done_ref[0, here] = turned(dq_ref[there], turn, -1.0).astype(BF)
            done_ref[1, here] = turned(dk_ref[there], turn, -1.0).astype(BF)
            done_ref[2, here] = dv_ref[there].astype(BF)

    piece = done_ref[stage]
    dproj_ref[...] = piece
    bsum_ref[0] = jnp.sum(piece.astype(F32), axis=0, keepdims=True)


def attend_back(kept, d_attended, turns, place, first, block, pairs, before):
    prob, low = kept
    tokens = d_attended.shape[0]
    seqs, count = tokens // SEQ, prob.shape[1] // 2
    width = 3 * pairs * PAIR
    return pl.pallas_call(
        functools.partial(attend_back_kernel, block),
        grid_spec=pltpu.PrefetchScalarGridSpec(
            num_scalar_prefetch=1,
            grid=(seqs, count, 3),
            in_specs=[
                pl.BlockSpec((1, 2) + prob.shape[2:], lambda s, p, j, z: (s, p, 0, 0)),
                pl.BlockSpec((3, SEQ, PAIR), lambda s, p, j, z: (0, s, p)),
                pl.BlockSpec((SEQ, PAIR), lambda s, p, j, z: (s, first + p)),
                pl.BlockSpec((3, SEQ, PAIR), lambda s, p, j, z: (0, s, 0)),
            ]
            + [ANY] * len(before),
            out_specs=[
                pl.BlockSpec((SEQ, PAIR), lambda s, p, j, z: (s, j * pairs + first + p)),
                pl.BlockSpec((1, 1, PAIR), lambda s, p, j, z: (s, 0, j * pairs + first + p)),
            ],
            scratch_shapes=[pltpu.VMEM((SEQ, PAIR), BF)]
            + [pltpu.VMEM((SEQ, PAIR), F32)] * 3
            + [pltpu.VMEM((3, SEQ, PAIR), BF)],
        ),
        out_shape=[
            jax.ShapeDtypeStruct((tokens, width), BF),
            jax.ShapeDtypeStruct((seqs, 1, width), F32),
        ],
        input_output_aliases={5: 0, 6: 1} if before else {},
        compiler_params=ROOM,
        name="attend_back",
    )(place.reshape(1), prob, low, d_attended, turns, *before)


def tables(positions):
    frequency = 10000.0 ** (-(jnp.arange(ROT // 2, dtype=F32) * 2.0) / ROT)
    angles = frequency[:, None] * positions[None, :]
    cosine, sine = jnp.cos(angles).T, jnp.sin(angles).T
    none = jnp.zeros_like(sine)
    still = jnp.zeros((sine.shape[0], HEAD_DIM - ROT), F32)
    return jnp.stack(
        [
            jnp.concatenate([cosine, cosine, still + 1.0] * 2, axis=1),
            jnp.concatenate([-sine, none, still] * 2, axis=1),
            jnp.concatenate([none, sine, still] * 2, axis=1),
        ]
    )


def feed_kernel(tokens, rows_ref, weight_ref, bias_ref, act_ref, slope_ref):
    root = (2.0 / jnp.pi) ** 0.5
    for first in range(0, rows_ref.shape[0], tokens):
        here = slice(first, first + tokens)
        pre_act = times(rows_ref[here], weight_ref[...]) + bias_ref[...]
        square = pre_act * pre_act
        curve = jnp.tanh(root * pre_act * (1.0 + 0.044715 * square))
        half = 0.5 * (1.0 + curve)
        act_ref[here] = (pre_act * half).astype(BF)
        slope_ref[here] = (
            half
            + 0.5 * pre_act * (1.0 - curve * curve) * root * (1.0 + 3 * 0.044715 * square)
        ).astype(BF)


def feed_forward(normed_all, fc1_cols, bias):
    height, width = normed_all.shape
    hidden = fc1_cols.shape[1]
    tile = min(512, hidden)
    block = pl.BlockSpec((height, tile), lambda j: (0, j))
    return pl.pallas_call(
        functools.partial(feed_kernel, min(256, height)),
        grid=(hidden // tile,),
        in_specs=[
            pl.BlockSpec(memory_space=pltpu.VMEM),
            pl.BlockSpec((width, tile), lambda j: (0, j)),
            pl.BlockSpec((1, tile), lambda j: (0, j)),
        ],
        out_specs=[block, block],
        out_shape=[jax.ShapeDtypeStruct((height, hidden), BF)] * 2,
        compiler_params=ROOM,
        name="feed_forward",
    )(normed_all, fc1_cols, bias.reshape(1, hidden))


def shards(
    inputs,
    segments,
    positions,
    ln_gain,
    ln_bias,
    w_qkv,
    b_qkv,
    w_dense,
    b_dense,
    w_fc1,
    b_fc1,
    w_fc2,
    b_fc2,
    cotangent,
):
    reps, group = lax.axis_size("rep"), lax.axis_size("shard")
    rep, place = lax.axis_index("rep"), lax.axis_index("shard")
    core = rep & 1
    tokens, width = inputs.shape
    rows = width // group
    slab = rows // reps
    hidden = w_fc1.shape[1] // group
    pairs = rows // PAIR
    line = Order()
    def gathered(array):
        return lax.all_gather(array, "rep", axis=0, tiled=True)

    owners = [(place + hop) % group for hop in range(group)]

    def qkv_rows(w):
        return tuple(
            jnp.concatenate(
                [
                    lax.dynamic_slice(w, (rep * slab, at * width + owner * rows), (slab, rows))
                    for at in range(3)
                ],
                axis=1,
            )
            for owner in owners
        )

    def fc1_rows(w):
        return jnp.concatenate(
            [
                lax.dynamic_slice(w, (rep * slab, owner * hidden), (slab, hidden))
                for owner in range(group)
            ]
        )

    qkv_pieces = [
        piece if hop == 0 else ring(piece, "shard", hop)
        for hop, piece in enumerate(line.step(qkv_rows, w_qkv))
    ]
    fc1_pieces = exchanged(line.step(fc1_rows, w_fc1))
    small = jnp.concatenate(
        [ln_gain, ln_bias, b_qkv, b_dense + b_fc2, positions.astype(F32)]
    ).reshape(1, -1)
    small = doubled(small, place, line)
    gain = small[:, :rows].reshape(width)
    shift = small[:, rows : 2 * rows].reshape(width)
    bias_qkv = lax.dynamic_slice_in_dim(
        small[:, 2 * rows : 5 * rows].reshape(3, width), place * rows, rows, 1
    ).reshape(1, 3 * rows)
    bias_out = small[:, 5 * rows : 6 * rows].reshape(width)
    group_positions = small[:, 6 * rows :]

    normed = [line.step(lambda *o: ln_forward(*o, reps, group), inputs, gain, shift)]
    normed.append(ring(line.hold(normed[0]), "shard", 1))
    qkv_cols = gathered(line.step(lambda *p: placed(p, place), *qkv_pieces))

    ring_order = [(place - hop) % group for hop in range(group)]
    ring_positions = jnp.concatenate(
        [lax.dynamic_index_in_dim(group_positions, at, 0, keepdims=False) for at in ring_order]
    )
    start = (
        jnp.arange(SEQ, dtype=jnp.int32)[None, None]
        - group_positions.astype(jnp.int32).reshape(-1, 1, SEQ)
    )
    per_seq = SEQ // tokens
    if group == per_seq:
        turn_place = place
        by_seq = from_seq = lambda array, axis=0: array
    else:
        turn_place = jnp.zeros_like(place)
        seq_order = [at // per_seq * per_seq + (-at) % per_seq for at in range(group)]

        def taken(array, order, axis):
            return jnp.concatenate(
                [
                    lax.dynamic_slice_in_dim(array, at * tokens, tokens, axis)
                    for at in order
                ],
                axis=axis,
            )

        by_seq = lambda array, axis=0: taken(
            array, [(place - at) % group for at in seq_order], axis
        )
        from_seq = lambda array, axis=0: taken(
            array, [at // per_seq * per_seq + (-at) % per_seq for at in ring_order], axis
        )

    turns = line.step(lambda p: by_seq(tables(p), 1), ring_positions)

    def begin(block):
        return jnp.concatenate([block, jnp.zeros(((group - 1) * tokens, width), BF)])

    def put(hop):
        return lambda whole, block: lax.dynamic_update_slice_in_dim(
            whole, block, hop * tokens, 0
        )

    normed_all = line.step(begin, normed[0])
    cot_all = line.step(begin, cotangent)
    def project_some(first, count, *before):
        return line.step(
            lambda a, b, c, *d: project(a, b, c, tokens, first, count, d),
            normed_all,
            qkv_cols,
            bias_qkv,
            *before,
        )

    for hop in range(1, group):
        normed[hop] = line.hold(normed[hop])
        if hop == 1:
            fc1_cols = gathered(line.hold(fc1_pieces))
        if hop + 1 < group:
            normed.append(ring(normed[hop], "shard", 1))
        else:
            cots = [line.hold(cotangent)]
            cots.append(ring(cots[0], "shard", 1))
        normed_all = line.step(put(hop), normed_all, normed[hop])
        if hop == group - 2:
            projected = project_some(0, group - 1)

    projected = by_seq(project_some(group - 1, 1, projected))
    calls = 2 if pairs > 1 else 1
    each = pairs // calls
    kept = []

    def attend_some(call, before):
        attended, *rest = line.step(
            lambda p, *b: attend(p, turns, start, turn_place, call * each, each, tokens, b),
            projected,
            *before,
        )
        kept.append(rest)
        return (attended,)

    attended = attend_some(0, ())
    for hop in range(1, group):
        cots[hop] = line.hold(cots[hop])
        if hop + 1 < group:
            cots.append(ring(cots[hop], "shard", 1))
        cot_all = line.step(put(hop), cot_all, cots[hop])
        if hop == 1:
            activation, slope = line.step(feed_forward, normed_all, fc1_cols, b_fc1)
        if hop == 2:
            if calls > 1:
                attended = attend_some(1, attended)
            out_part = line.step(
                lambda a, b, c, d: push(a, b, c, d, False, place, group),
                from_seq(attended[0]),
                w_dense,
                activation,
                w_fc2,
            )
            out_sum = lax.psum_scatter(out_part, "shard", scatter_dimension=0, tiled=True)
    (attended,) = attended
    attended = from_seq(attended)

    def grad(left, right, *also):
        sent = line.step(
            lambda a, b, *c: half_grads(a, b, 1 - core, reps, None, *c), left, right, *also
        )
        return swap(sent, "rep", 1)

    def grad_sum(left, right, came, *also):
        if reps == 8 and not (left.shape[1] // reps % 128):
            own, *sent = line.step(
                lambda a, b, c, *d: grad_sums(a, b, rep, c, *d), left, right, came, *also
            )
            halving = Halving(rep, own, 2)
            halving.send(line, sent)
            return halving
        own = line.step(
            lambda a, b, c, *d: half_grads(a, b, core, reps, c, *d), left, right, came, *also
        )
        halving = Halving(rep, own, 2)
        halving.send(line)
        return halving

    def attend_back_some(call, before):
        return line.step(
            lambda d, t, *b: attend_back(
                kept[call], d, t, turn_place, call * each, tokens, pairs, b
            ),
            d_attended,
            turns,
            *before,
        )

    out_came = grad(activation, cot_all, attended)
    d_pre = line.step(pull, cot_all, w_fc2, slope)
    fc1_came = grad(normed_all, d_pre)
    out_grads = grad_sum(activation, cot_all, out_came, attended)
    d_attended = by_seq(
        line.step(lambda c, w: times_transpose(c, w).astype(BF), cot_all, w_dense)
    )
    back = attend_back_some(0, ())
    fc1_sum = grad_sum(normed_all, d_pre, fc1_came)
    out_grads.further(line)
    for call in range(1, calls):
        back = attend_back_some(call, back)
    d_projected, d_bias_qkv = back
    d_projected = from_seq(d_projected)
    d_normed_part = line.step(
        lambda a, b, c, d: push(a, b, c, d, True, place), d_projected, qkv_cols, d_pre, fc1_cols
    )
    d_normed_sum = Passing(line, d_normed_part, tokens)
    out_piece = out_grads.end(line)
    fc1_sum.further(line)
    out_whole = gathered(line.hold(out_piece))
    qkv_came = grad(normed_all, d_projected)
    block_out = line.step(
        lambda x, b, p: x.astype(F32) + b + p.astype(F32), inputs, bias_out, out_sum
    )
    qkv_sum = grad_sum(normed_all, d_projected, qkv_came)
    fc1_pieces = exchanged(line.hold(fc1_sum.end(line)))
    d_normed_sum.further()
    qkv_sum.further(line)

    def bias_sums(d_bias_qkv, cotangent, d_pre):
        d_bias_all = lax.dynamic_update_slice_in_dim(
            jnp.zeros((3, width), F32),
            jnp.sum(d_bias_qkv[:, 0], axis=0).reshape(3, rows),
            place * rows,
            1,
        )
        ones = jnp.ones((8, group * tokens), BF)
        return (
            jnp.concatenate(
                [
                    d_bias_all.reshape(group, 3 * rows),
                    jnp.sum(cotangent.astype(F32), axis=0).reshape(group, rows),
                ],
                axis=1,
            ),
            times(ones, d_pre)[0],
        )

    early_sums, d_bias_fc1 = line.step(bias_sums, d_bias_qkv, cotangent, d_pre)
    qkv_piece = qkv_sum.end(line)
    d_normed_sum.hold()
    fc1_slab = line.step(lambda p: widened(p, group, hidden), fc1_pieces)
    qkv_pieces = exchanged(line.hold(qkv_piece))
    fc1_whole = gathered(line.hold(fc1_slab))
    qkv_spread = Spread(line, line.step(lambda p: widened(p, group, rows), qkv_pieces))
    d_normed_sum.further()
    fc2_total, dense_total = line.step(
        lambda a: split_rows(a, reps, (hidden // reps, slab)), out_whole
    )
    grad_inputs, norm_sums = line.step(
        lambda x, g, c, *p: ln_backward(x, g, c, p, reps, group),
        inputs,
        gain,
        cotangent,
        *d_normed_sum.end(),
    )

    sums = line.step(
        lambda early, norm_sums: jnp.concatenate(
            [early, norm_sums[0].reshape(group, rows), norm_sums[1].reshape(group, rows)], axis=1
        ),
        early_sums,
        norm_sums,
    )
    qkv_spread.across()
    sums = owned_sum(line, sums, place)
    sums = line.hold(jnp.concatenate([sums, d_bias_fc1]))
    sums = line.hold(sums + swap(sums, "rep", 1))
    (fc1_total,) = line.step(lambda a: split_rows(a, reps, (slab,)), fc1_whole)
    qkv_spread = qkv_spread.shared()
    bit = 2
    while bit < reps:
        sums = line.hold(sums + swap(sums, "rep", bit))
        bit *= 2
    qkv_total = line.step(lambda *p: assemble(p, rep), *qkv_spread)
    cot_total = sums[3 * rows : 4 * rows]
    return (
        block_out,
        grad_inputs,
        sums[4 * rows : 5 * rows],
        sums[5 * rows : 6 * rows],
        qkv_total,
        sums[: 3 * rows],
        dense_total,
        cot_total,
        fc1_total,
        sums[6 * rows :],
        fc2_total,
        cot_total,
    )


def solution(mesh):
    both, shard = P(("rep", "shard")), P("shard")
    wide, held = P(("rep", "shard"), None), P("shard", None)
    return jax.shard_map(
        shards,
        mesh=mesh,
        in_specs=(
            wide, both, both, shard, shard, held, shard, held, shard, held, shard, held, shard, wide
        ),
        out_specs=(
            wide, wide, shard, shard, held, shard, held, shard, held, shard, held, shard
        ),
        check_vma=False,
    )
```

```python
import functools

import jax
import jax.numpy as jnp
from jax import lax
from jax.experimental import pallas as pl
from jax.experimental.pallas import tpu as pltpu
from jax.sharding import PartitionSpec as P

HEAD_DIM = 64
ROT = 32
SEQ = 1024
PAIR = 2 * HEAD_DIM
BF = jnp.bfloat16
F32 = jnp.float32
ROOM = pltpu.CompilerParams(vmem_limit_bytes=56 * 2**20)
ANY = pl.BlockSpec(memory_space=pl.ANY)


def ring(array, axis, distance):
    size = lax.axis_size(axis)
    return lax.ppermute(array, axis, [(i, (i + distance) % size) for i in range(size)])


def swap(array, axis, mask):
    size = lax.axis_size(axis)
    return lax.ppermute(array, axis, [(i, i ^ mask) for i in range(size)])


def contract_rows(left_side, right_side):
    return lax.dot_general(
        left_side, right_side, (((0,), (0,)), ((), ())), preferred_element_type=F32
    )


def times_transpose(left_side, right_side):
    return lax.dot_general(
        left_side, right_side, (((1,), (1,)), ((), ())), preferred_element_type=F32
    )


def times(left_side, right_side):
    return jnp.dot(left_side, right_side, preferred_element_type=F32)


class Order:
    def __init__(self):
        self.last = None

    def step(self, work, *operands):
        if self.last is not None:
            operands, _ = lax.optimization_barrier((operands, self.last))
        result = work(*operands)
        self.last = jax.tree.leaves(result)
        return result

    def hold(self, array):
        return self.step(lambda a: a, array)


def doubled(row, place, line):
    bit = 1
    while bit < lax.axis_size("shard"):
        row = line.hold(row)
        other = swap(row, "shard", bit)
        upper = (place & bit) > 0
        row = jnp.concatenate([jnp.where(upper, other, row), jnp.where(upper, row, other)])
        bit *= 2
    return row


def owned_sum(line, values, place):
    bit = lax.axis_size("shard") >> 1
    while bit:
        upper = ((place & bit) > 0).astype(jnp.int32)
        count = values.shape[0] // 2
        sent, kept = (
            lax.dynamic_slice_in_dim(values, side * count, count, 0) for side in (1 - upper, upper)
        )
        values = line.hold(kept + swap(sent, "shard", bit))
        bit >>= 1
    return values[0]


class Halving:
    def __init__(self, rep, array, parts):
        count = lax.axis_size("rep").bit_length() - 2
        self.rep = rep
        array = array.reshape((2,) * count + (array.shape[0] >> count,) + array.shape[1:])
        rows = array.shape[count] // parts
        self.arrays = [array] * parts
        self.spans = [(part * rows, rows) for part in range(parts)]
        bits = list(range(count, 0, -1))
        self.bits = [list(bits) for _ in range(parts)]
        self.todo = [
            bits[::-1][part % count :] + bits[::-1][: part % count] for part in range(parts)
        ]

    def pick(self, part, array, mine):
        axis = self.bits[part].index(self.todo[part][0])
        bit = (self.rep >> self.todo[part][0]) & 1
        starts, sizes = [0] * array.ndim, list(array.shape)
        starts[axis], sizes[axis] = (bit if mine else 1 - bit), 1
        starts[len(self.bits[part])], sizes[len(self.bits[part])] = self.spans[part]
        half = lax.dynamic_slice(array, starts, sizes)
        return half.reshape(half.shape[:axis] + half.shape[axis + 1 :])

    def outgoing(self, *arrays):
        return tuple(self.pick(part, array, False) for part, array in enumerate(arrays))

    def added(self, *operands):
        count = len(operands) // 2
        return tuple(
            (self.pick(part, operands[part], True).astype(F32) + operands[count + part].astype(F32))
            .astype(BF)
            for part in range(count)
        )

    def send(self, line, sent=None):
        if sent is None:
            sent = line.step(self.outgoing, *self.arrays)
        self.came = [
            swap(piece, "rep", 1 << todo[0]) for piece, todo in zip(sent, self.todo)
        ]

    def take(self, line):
        self.arrays = line.step(self.added, *self.arrays, *self.came)
        for part, todo in enumerate(self.todo):
            self.bits[part].remove(todo[0])
            self.todo[part] = todo[1:]
            self.spans[part] = (0, self.spans[part][1])

    def further(self, line):
        if len(self.todo[0]) > 1:
            self.take(line)
            self.send(line)

    def end(self, line):
        while len(self.todo[0]) > 1:
            self.further(line)
        self.take(line)
        return jnp.concatenate(self.arrays, axis=0)


class Passing:
    def __init__(self, line, array, tokens):
        self.line, self.group = line, array.shape[0] // tokens
        self.block = lambda hop: (hop % self.group * tokens, tokens)
        self.array, self.hop = array, 1
        sent = line.step(lambda a: lax.slice_in_dim(a, tokens, 2 * tokens, axis=0), array)
        self.came = ring(sent, "shard", 1)

    def hold(self):
        self.came = self.line.hold(self.came)

    def further(self):
        self.hop += 1
        first, count = self.block(self.hop)
        sent = self.line.step(
            lambda a, b: (
                lax.slice_in_dim(a, first, first + count, axis=0).astype(F32) + b.astype(F32)
            ).astype(BF),
            self.array,
            self.came,
        )
        self.came = ring(sent, "shard", 1)

    def end(self):
        while self.hop + 1 < self.group:
            self.further()
        return lax.slice_in_dim(self.array, 0, self.block(0)[1], axis=0), self.came


def place_kernel(width, place_ref, *refs):
    *pieces, out_ref = refs
    size = len(pieces)
    length, columns = pieces[0].shape
    for hop, piece in enumerate(pieces):
        owner = lax.rem(place_ref[0] - hop + size, size)
        if width is None:
            out_ref[pl.ds(pl.multiple_of(owner * length, length), length), :] = piece[...]
        else:
            count = columns // width
            for at in range(count):
                first = pl.multiple_of((at * size + owner) * width, width)
                out_ref[:, pl.ds(first, width)] = piece[:, at * width : (at + 1) * width]


def placed(pieces, place, width=None):
    length, columns = pieces[0].shape
    shape = (
        (length * len(pieces), columns) if width is None else (length, columns * len(pieces))
    )
    whole = pl.BlockSpec(memory_space=pltpu.VMEM)
    return pl.pallas_call(
        functools.partial(place_kernel, width),
        in_specs=[pl.BlockSpec(memory_space=pltpu.SMEM)] + [whole] * len(pieces),
        out_specs=whole,
        out_shape=jax.ShapeDtypeStruct(shape, pieces[0].dtype),
        compiler_params=ROOM,
        name="placed",
    )(place.reshape(1), *pieces)


def exchanged(array):
    return lax.all_to_all(array, "shard", 0, 0, tiled=True)


def widen_kernel(size, width, rows_ref, out_ref):
    length = rows_ref.shape[0] // size
    for owner in range(size):
        for at in range(rows_ref.shape[1] // width):
            first = (at * size + owner) * width
            out_ref[:, first : first + width] = rows_ref[
                owner * length : (owner + 1) * length, at * width : (at + 1) * width
            ]


def widened(array, size, width):
    rows, columns = array.shape
    return pl.pallas_call(
        functools.partial(widen_kernel, size, width),
        out_shape=jax.ShapeDtypeStruct((rows // size, columns * size), array.dtype),
        compiler_params=ROOM,
        name="widened",
    )(array)


def split_kernel(in_ref, *refs):
    first = 0
    for ref in refs:
        ref[...] = in_ref[first : first + ref.shape[0]].astype(F32)
        first += ref.shape[0]


def split_rows(array, reps, heights):
    rows, columns = array.shape
    return pl.pallas_call(
        split_kernel,
        grid=(reps,),
        in_specs=[pl.BlockSpec((rows // reps, columns), lambda r: (r, 0))],
        out_specs=[pl.BlockSpec((height, columns), lambda r: (r, 0)) for height in heights],
        out_shape=[jax.ShapeDtypeStruct((height * reps, columns), F32) for height in heights],
        compiler_params=ROOM,
        name="split_rows",
    )(array)


class Spread:
    def __init__(self, line, array):
        self.line, self.size = line, lax.axis_size("rep")
        self.pieces = {0: array}
        steps = (2, 4) if self.size == 8 else range(2, self.size, 2)
        for mask in steps:
            self.pieces[mask] = swap(array, "rep", mask)

    def across(self):
        if self.size != 8:
            return
        half = self.pieces[0].shape[0] // 2
        self.pieces[2], self.pieces[4], first, second = self.line.step(
            lambda a, b: (a, b, a[:half], b[half:]), self.pieces[2], self.pieces[4]
        )
        self.halves = (swap(first, "rep", 4), swap(second, "rep", 2))

    def shared(self):
        masks = range(0, self.size, 2)
        if self.size == 8:
            self.pieces[6] = self.line.step(lambda *h: jnp.concatenate(h), *self.halves)
        held = self.line.step(lambda *p: p, *[self.pieces[mask] for mask in masks])
        return [piece for one in held for piece in (one, swap(one, "rep", 1))]


def assemble_kernel(rep_ref, *refs):
    for mask, piece in enumerate(refs[:-1]):

        @pl.when(pl.program_id(0) == mask)
        def _(piece=piece):
            refs[-1][...] = piece[...].astype(F32)


def assemble(pieces, rep):
    size = len(pieces)
    rows, columns = pieces[0].shape
    whole = pl.BlockSpec((rows, columns), lambda m, r: (0, 0), pipeline_mode=pl.Buffered(1))
    return pl.pallas_call(
        assemble_kernel,
        grid_spec=pltpu.PrefetchScalarGridSpec(
            num_scalar_prefetch=1,
            grid=(size,),
            in_specs=[whole] * size,
            out_specs=pl.BlockSpec((rows, columns), lambda m, r: (r[0] ^ m, 0)),
        ),
        out_shape=jax.ShapeDtypeStruct((rows * size, columns), F32),
        compiler_params=ROOM,
        name="assemble",
    )(rep.reshape(1), *pieces)


def grad_kernel(which_ref, left_ref, right_ref, *refs):
    *more, out_ref = refs
    left = left_ref[...]
    if more and more[0].shape[0] == left.shape[0]:
        both = more.pop(0)
        lanes = both.shape[1] // 2
        left = jnp.concatenate(
            [left, jnp.where(which_ref[0] == 0, both[:, :lanes], both[:, lanes:])], axis=1
        )
    total = contract_rows(left, right_ref[...])
    if more:
        total = total + more[0][...].astype(F32)
    out_ref[...] = total.astype(BF)


def chip_of(step):
    return step // 2, (step + 1) // 2 % 2


def grad_sum_kernel(at_ref, left_ref, right_ref, *refs):
    *more, came_ref, own_ref, fast_ref, slow_ref = refs
    left = left_ref[...]
    if more:
        both = more[0][...]
        lanes = both.shape[1] // 2
        left = jnp.concatenate(
            [left, jnp.where(at_ref[0] == 0, both[:, :lanes], both[:, lanes:])], axis=1
        )
    total = (contract_rows(left, right_ref[...]) + came_ref[...].astype(F32)).astype(BF)
    own_ref[...] = total
    slow, fast = chip_of(pl.program_id(0))
    half = total.shape[0] // 2

    @pl.when(fast == 1)
    def _():
        fast_ref[0] = total[:half]

    @pl.when(slow == 1)
    def _():
        slow_ref[0] = total[half:]


def grad_sums(left, right, rep, came, also=None):
    tokens, height = left.shape
    length = right.shape[1]
    height //= 8
    extra = 0 if also is None else also.shape[1] // 8
    total = height + extra
    block = lambda j, at: 2 * (at[2] ^ chip_of(j)[0]) + (at[1] ^ chip_of(j)[1])
    half = (1, total // 2, length)
    return pl.pallas_call(
        grad_sum_kernel,
        grid_spec=pltpu.PrefetchScalarGridSpec(
            num_scalar_prefetch=1,
            grid=(4,),
            in_specs=[
                pl.BlockSpec((tokens, height), lambda j, at: (0, 2 * block(j, at) + at[0])),
                pl.BlockSpec(memory_space=pltpu.VMEM),
            ]
            + (
                []
                if also is None
                else [pl.BlockSpec((tokens, 128), lambda j, at: (0, block(j, at)))]
            )
            + [pl.BlockSpec((total, length), lambda j, at: (block(j, at), 0))],
            out_specs=[
                pl.BlockSpec((total, length), lambda j, at: (block(j, at), 0)),
                pl.BlockSpec(half, lambda j, at: (at[2] ^ (j // 2), 0, 0)),
                pl.BlockSpec(half, lambda j, at: (at[1] ^ (1 - j // 3), 0, 0)),
            ],
        ),
        out_shape=[
            jax.ShapeDtypeStruct((4 * total, length), BF),
            jax.ShapeDtypeStruct((2,) + half[1:], BF),
            jax.ShapeDtypeStruct((2,) + half[1:], BF),
        ],
        compiler_params=ROOM,
        name="grad_sums",
    )(
        jnp.stack([rep & 1, (rep >> 1) & 1, rep >> 2]),
        left,
        right,
        *([] if also is None else [also]),
        came,
    )


def half_grads(left, right, which, reps, came=None, also=None):
    tokens, height = left.shape
    length = right.shape[1]
    height //= reps
    extra = 0 if also is None else also.shape[1] // reps
    if height % 128 or extra not in (0, 64):
        sides = [left] if also is None else [left, also]
        total = [
            contract_rows(
                lax.dynamic_index_in_dim(
                    side.reshape(tokens, reps // 2, 2, -1), which, 2, keepdims=False
                ).reshape(tokens, -1),
                right,
            ).reshape(reps // 2, -1, length)
            for side in sides
        ]
        total = jnp.concatenate(total, axis=1).reshape(-1, length)
        return (total if came is None else total + came.astype(F32)).astype(BF)
    block = pl.BlockSpec((height + extra, length), lambda b, w: (b, 0))
    more = [] if also is None else [also]
    more_specs = [] if also is None else [pl.BlockSpec((tokens, 128), lambda b, w: (0, b))]
    return pl.pallas_call(
        grad_kernel,
        grid_spec=pltpu.PrefetchScalarGridSpec(
            num_scalar_prefetch=1,
            grid=(reps // 2,),
            in_specs=[
                pl.BlockSpec((tokens, height), lambda b, w: (0, 2 * b + w[0])),
                pl.BlockSpec(memory_space=pltpu.VMEM),
            ]
            + more_specs
            + ([] if came is None else [block]),
            out_specs=block,
        ),
        out_shape=jax.ShapeDtypeStruct((reps // 2 * (height + extra), length), BF),
        compiler_params=ROOM,
        name="half_grads",
    )(which.reshape(1), left, right, *more, *([] if came is None else [came]))


def ln_forward_kernel(reps, group, x_ref, gain_ref, shift_ref, out_ref):
    x = x_ref[...].astype(F32)
    centred = x - jnp.mean(x, axis=-1, keepdims=True)
    spread = jnp.mean(centred * centred, axis=-1, keepdims=True)
    normed = (centred * lax.rsqrt(spread + 1e-05)) * gain_ref[...] + shift_ref[...]
    slab = x.shape[1] // (reps * group)
    out_ref[...] = jnp.concatenate(
        [
            normed[:, (g * reps + r) * slab : (g * reps + r + 1) * slab]
            for r in range(reps)
            for g in range(group)
        ],
        axis=1,
    ).astype(BF)


def ln_forward(inputs, gain, shift, reps, group):
    tokens, width = inputs.shape
    return pl.pallas_call(
        functools.partial(ln_forward_kernel, reps, group),
        out_shape=jax.ShapeDtypeStruct((tokens, width), BF),
        compiler_params=ROOM,
        name="ln_forward",
    )(inputs, gain.reshape(1, width), shift.reshape(1, width))


def ln_backward_kernel(reps, group, x_ref, gain_ref, cot_ref, a_ref, b_ref, out_ref, sums_ref):
    x = x_ref[...].astype(F32)
    centred = x - jnp.mean(x, axis=-1, keepdims=True)
    spread = jnp.mean(centred * centred, axis=-1, keepdims=True)
    inverse = lax.rsqrt(spread + 1e-05)
    xhat = centred * inverse
    mixed = a_ref[...].astype(F32) + b_ref[...].astype(F32)
    slab = x.shape[1] // (reps * group)
    d_normed = jnp.concatenate(
        [
            mixed[:, (r * group + g) * slab : (r * group + g + 1) * slab]
            for g in range(group)
            for r in range(reps)
        ],
        axis=1,
    )
    sums_ref[0:1] = jnp.sum(d_normed * xhat, axis=0, keepdims=True)
    sums_ref[1:2] = jnp.sum(d_normed, axis=0, keepdims=True)
    scaled = d_normed * gain_ref[...]
    out_ref[...] = cot_ref[...].astype(F32) + inverse * (
        scaled
        - jnp.mean(scaled, axis=-1, keepdims=True)
        - xhat * jnp.mean(scaled * xhat, axis=-1, keepdims=True)
    )


def ln_backward(inputs, gain, cotangent, parts, reps, group):
    tokens, width = inputs.shape
    return pl.pallas_call(
        functools.partial(ln_backward_kernel, reps, group),
        out_shape=[
            jax.ShapeDtypeStruct((tokens, width), F32),
            jax.ShapeDtypeStruct((2, width), F32),
        ],
        compiler_params=ROOM,
        name="ln_backward",
    )(inputs, gain.reshape(1, width), cotangent, *parts)


def pull_kernel(cot_ref, weight_ref, *refs):
    total = times_transpose(cot_ref[...], weight_ref[...])
    if len(refs) > 1:
        total = total * refs[0][...].astype(F32)
    refs[-1][...] = total.astype(BF)


def pull(cot_all, weight, *slope):
    height, width = cot_all.shape
    hidden = weight.shape[0]
    tile = min(512, hidden)
    block = pl.BlockSpec((height, tile), lambda j: (0, j))
    return pl.pallas_call(
        pull_kernel,
        grid=(hidden // tile,),
        in_specs=[
            pl.BlockSpec(memory_space=pltpu.VMEM),
            pl.BlockSpec((tile, width), lambda j: (j, 0)),
        ]
        + [block] * len(slope),
        out_specs=block,
        out_shape=jax.ShapeDtypeStruct((height, hidden), BF),
        compiler_params=ROOM,
        name="pull",
    )(cot_all, weight, *slope)


def push_kernel(transposed, size, place_ref, a_ref, b_ref, c_ref, d_ref, out_ref):
    product = times_transpose if transposed else times
    total = product(a_ref[...], b_ref[...]) + product(c_ref[...], d_ref[...])
    if size is None:
        out_ref[...] = total.astype(BF)
        return
    block = out_ref.shape[0] // size
    for hop in range(size):
        out_ref[token_block(place_ref[0], hop, size, block)] = total[
            hop * block : (hop + 1) * block
        ].astype(BF)


def push(a, b, c, d, transposed, place, size=None):
    height = a.shape[0]
    length = b.shape[0 if transposed else 1]
    tile = min(512, length)
    full = lambda x: pl.BlockSpec(memory_space=pltpu.VMEM)
    if transposed:
        part = lambda x: pl.BlockSpec((tile, x.shape[1]), lambda j, z: (j, 0))
    else:
        part = lambda x: pl.BlockSpec((x.shape[0], tile), lambda j, z: (0, j))
    return pl.pallas_call(
        functools.partial(push_kernel, transposed, size),
        grid_spec=pltpu.PrefetchScalarGridSpec(
            num_scalar_prefetch=1,
            grid=(length // tile,),
            in_specs=[full(a), part(b), full(c), part(d)],
            out_specs=pl.BlockSpec((height, tile), lambda j, z: (0, j)),
        ),
        out_shape=jax.ShapeDtypeStruct((height, length), BF),
        compiler_params=ROOM,
        name="push",
    )(place.reshape(1), a, b, c, d)


def project_kernel(rows_ref, weight_ref, bias_ref, *refs):
    refs[-1][...] = times(rows_ref[...], weight_ref[...]) + bias_ref[...]


def project(normed_all, weight, bias, tokens, first, count, before):
    height, width = normed_all.shape
    length = weight.shape[1]
    tile = length // 3
    here = first // count
    return pl.pallas_call(
        project_kernel,
        grid=(3,),
        in_specs=[
            pl.BlockSpec((count * tokens, width), lambda j: (here, 0)),
            pl.BlockSpec((width, tile), lambda j: (0, j)),
            pl.BlockSpec((1, tile), lambda j: (0, j)),
        ]
        + [ANY] * len(before),
        out_specs=pl.BlockSpec((count * tokens, tile), lambda j: (here, j)),
        out_shape=jax.ShapeDtypeStruct((height, length), F32),
        input_output_aliases={3: 0} if before else {},
        compiler_params=ROOM,
        name="project",
    )(normed_all, weight, bias, *before)


def turned(u, turn, sign):
    return (
        u * turn[0]
        + sign * (pltpu.roll(u, PAIR - ROT // 2, 1) * turn[1])
        + sign * (pltpu.roll(u, ROT // 2, 1) * turn[2])
    )


def spans(rows, block):
    first = 0
    for part in range(rows // block):
        yield part, first, (part + 1) * block
        first += (part + 1) * block


def token_block(place, hop, count, block):
    return pl.ds(pl.multiple_of(lax.rem(place - hop + count, count) * block, block), block)


def attend_kernel(block, place_ref, q_ref, k_ref, v_ref, turn_ref, start_ref, *refs):
    att_ref, prob_ref, low_ref, out_ref = refs[-4:]
    rows = q_ref.shape[0]
    count = rows // block
    for hop in range(count):
        here, there = slice(hop * block, (hop + 1) * block), token_block(place_ref[0], hop, count, block)
        turn = [turn_ref[k, here] for k in range(3)]
        query = turned(q_ref[here], turn, 1.0).astype(BF)
        low_ref[0, there] = (query * HEAD_DIM ** (-0.5)).astype(BF)
        low_ref[1, there] = turned(k_ref[here], turn, 1.0).astype(BF)
        low_ref[2, there] = v_ref[here].astype(BF)
    start = start_ref[0]
    for head in range(2):
        lanes = slice(head * HEAD_DIM, (head + 1) * HEAD_DIM)
        key_h = low_ref[1, :, lanes]
        value_t = low_ref[2, :, lanes].T
        for part, first, length in spans(rows, block):
            own = slice(part * block, (part + 1) * block)
            scores = times_transpose(key_h[:length], low_ref[0, own, lanes])
            place = lax.broadcasted_iota(jnp.int32, (length, block), 0)
            asker = lax.broadcasted_iota(jnp.int32, (length, block), 1) + part * block
            allowed = (place >= start[:, own]) & (place <= asker)
            scores = jnp.where(allowed, scores, -1e30)
            exponent = jnp.exp(scores - jnp.max(scores, axis=0, keepdims=True))
            softmax = exponent * (1.0 / jnp.sum(exponent, axis=0, keepdims=True))
            attention = softmax.astype(BF)
            prob_ref[0, head, first : first + length] = attention
            out_ref[own, lanes] = times(value_t[:, :length], attention).T.astype(BF)
    for hop in range(count):
        att_ref[hop * block : (hop + 1) * block] = out_ref[token_block(place_ref[0], hop, count, block)]


def attend(projected, turns, start, place, first, count, block, before):
    tokens, width = projected.shape
    pairs, seqs = width // (3 * PAIR), tokens // SEQ
    stored = sum(length for _, _, length in spans(SEQ, block))
    wide = lambda at: pl.BlockSpec((SEQ, PAIR), lambda s, p, z: (s, at * pairs + first + p))
    return pl.pallas_call(
        functools.partial(attend_kernel, block),
        grid_spec=pltpu.PrefetchScalarGridSpec(
            num_scalar_prefetch=1,
            grid=(seqs, count),
            in_specs=[
                wide(0),
                wide(1),
                wide(2),
                pl.BlockSpec((3, SEQ, PAIR), lambda s, p, z: (0, s, 0)),
                pl.BlockSpec((1, 1, SEQ), lambda s, p, z: (s, 0, 0)),
            ]
            + [ANY] * len(before),
            out_specs=[
                pl.BlockSpec((SEQ, PAIR), lambda s, p, z: (s, first + p)),
                pl.BlockSpec((1, 2, stored, block), lambda s, p, z: (s, p, 0, 0)),
                pl.BlockSpec((3, SEQ, PAIR), lambda s, p, z: (0, s, p)),
            ],
            scratch_shapes=[pltpu.VMEM((SEQ, PAIR), BF)],
        ),
        out_shape=[
            jax.ShapeDtypeStruct((tokens, pairs * PAIR), BF),
            jax.ShapeDtypeStruct((seqs, 2 * count, stored, block), BF),
            jax.ShapeDtypeStruct((3, tokens, count * PAIR), BF),
        ],
        input_output_aliases={6: 0} if before else {},
        compiler_params=ROOM,
        name="attend",
    )(place.reshape(1), projected, projected, projected, turns, start, *before)


def attend_back_kernel(block, place_ref, prob_ref, low_ref, datt_ref, turn_ref, *refs):
    dproj_ref, bsum_ref, d_ref, dq_ref, dk_ref, dv_ref, done_ref = refs[-7:]
    rows = datt_ref.shape[0]
    count = rows // block
    stage = pl.program_id(2)

    @pl.when(stage == 0)
    def _():
        for hop in range(count):
            d_ref[token_block(place_ref[0], hop, count, block)] = datt_ref[
                hop * block : (hop + 1) * block
            ]
        for head in range(2):
            lanes = slice(head * HEAD_DIM, (head + 1) * HEAD_DIM)
            key_t = low_ref[1, :, lanes].T
            value_h = low_ref[2, :, lanes]
            for part, first, length in reversed(list(spans(rows, block))):
                own = slice(part * block, (part + 1) * block)
                query_p = low_ref[0, own, lanes]
                d_att_p = d_ref[own, lanes]
                attention = prob_ref[0, head, first : first + length]
                d_attention = times_transpose(value_h[:length], d_att_p)
                softmax = attention.astype(F32)
                weighted = softmax * d_attention
                d_scores = (
                    weighted - softmax * jnp.sum(weighted, axis=0, keepdims=True)
                ).astype(BF)
                dq_ref[own, lanes] = times(key_t[:, :length], d_scores).T * HEAD_DIM ** (-0.5)
                d_value = times(attention, d_att_p)
                d_key = times(d_scores, query_p)
                if length == rows:
                    dv_ref[:, lanes] = d_value
                    dk_ref[:, lanes] = d_key
                else:
                    dv_ref[:length, lanes] += d_value
                    dk_ref[:length, lanes] += d_key
        for hop in range(count):
            here = slice(hop * block, (hop + 1) * block)
            there = token_block(place_ref[0], hop, count, block)
            turn = [turn_ref[k, here] for k in range(3)]
            done_ref[0, here] = turned(dq_ref[there], turn, -1.0).astype(BF)
            done_ref[1, here] = turned(dk_ref[there], turn, -1.0).astype(BF)
            done_ref[2, here] = dv_ref[there].astype(BF)

    piece = done_ref[stage]
    dproj_ref[...] = piece
    bsum_ref[0] = jnp.sum(piece.astype(F32), axis=0, keepdims=True)


def attend_back(kept, d_attended, turns, place, first, block, pairs, before):
    prob, low = kept
    tokens = d_attended.shape[0]
    seqs, count = tokens // SEQ, prob.shape[1] // 2
    width = 3 * pairs * PAIR
    return pl.pallas_call(
        functools.partial(attend_back_kernel, block),
        grid_spec=pltpu.PrefetchScalarGridSpec(
            num_scalar_prefetch=1,
            grid=(seqs, count, 3),
            in_specs=[
                pl.BlockSpec((1, 2) + prob.shape[2:], lambda s, p, j, z: (s, p, 0, 0)),
                pl.BlockSpec((3, SEQ, PAIR), lambda s, p, j, z: (0, s, p)),
                pl.BlockSpec((SEQ, PAIR), lambda s, p, j, z: (s, first + p)),
                pl.BlockSpec((3, SEQ, PAIR), lambda s, p, j, z: (0, s, 0)),
            ]
            + [ANY] * len(before),
            out_specs=[
                pl.BlockSpec((SEQ, PAIR), lambda s, p, j, z: (s, j * pairs + first + p)),
                pl.BlockSpec((1, 1, PAIR), lambda s, p, j, z: (s, 0, j * pairs + first + p)),
            ],
            scratch_shapes=[pltpu.VMEM((SEQ, PAIR), BF)]
            + [pltpu.VMEM((SEQ, PAIR), F32)] * 3
            + [pltpu.VMEM((3, SEQ, PAIR), BF)],
        ),
        out_shape=[
            jax.ShapeDtypeStruct((tokens, width), BF),
            jax.ShapeDtypeStruct((seqs, 1, width), F32),
        ],
        input_output_aliases={5: 0, 6: 1} if before else {},
        compiler_params=ROOM,
        name="attend_back",
    )(place.reshape(1), prob, low, d_attended, turns, *before)


def tables(positions):
    frequency = 10000.0 ** (-(jnp.arange(ROT // 2, dtype=F32) * 2.0) / ROT)
    angles = frequency[:, None] * positions[None, :]
    cosine, sine = jnp.cos(angles).T, jnp.sin(angles).T
    none = jnp.zeros_like(sine)
    still = jnp.zeros((sine.shape[0], HEAD_DIM - ROT), F32)
    return jnp.stack(
        [
            jnp.concatenate([cosine, cosine, still + 1.0] * 2, axis=1),
            jnp.concatenate([-sine, none, still] * 2, axis=1),
            jnp.concatenate([none, sine, still] * 2, axis=1),
        ]
    )


def feed_kernel(tokens, rows_ref, weight_ref, bias_ref, act_ref, slope_ref):
    root = (2.0 / jnp.pi) ** 0.5
    for first in range(0, rows_ref.shape[0], tokens):
        here = slice(first, first + tokens)
        pre_act = times(rows_ref[here], weight_ref[...]) + bias_ref[...]
        square = pre_act * pre_act
        curve = jnp.tanh(root * pre_act * (1.0 + 0.044715 * square))
        half = 0.5 * (1.0 + curve)
        act_ref[here] = (pre_act * half).astype(BF)
        slope_ref[here] = (
            half
            + 0.5 * pre_act * (1.0 - curve * curve) * root * (1.0 + 3 * 0.044715 * square)
        ).astype(BF)


def feed_forward(normed_all, fc1_cols, bias):
    height, width = normed_all.shape
    hidden = fc1_cols.shape[1]
    tile = min(512, hidden)
    block = pl.BlockSpec((height, tile), lambda j: (0, j))
    return pl.pallas_call(
        functools.partial(feed_kernel, min(256, height)),
        grid=(hidden // tile,),
        in_specs=[
            pl.BlockSpec(memory_space=pltpu.VMEM),
            pl.BlockSpec((width, tile), lambda j: (0, j)),
            pl.BlockSpec((1, tile), lambda j: (0, j)),
        ],
        out_specs=[block, block],
        out_shape=[jax.ShapeDtypeStruct((height, hidden), BF)] * 2,
        compiler_params=ROOM,
        name="feed_forward",
    )(normed_all, fc1_cols, bias.reshape(1, hidden))


def shards(
    inputs,
    segments,
    positions,
    ln_gain,
    ln_bias,
    w_qkv,
    b_qkv,
    w_dense,
    b_dense,
    w_fc1,
    b_fc1,
    w_fc2,
    b_fc2,
    cotangent,
):
    reps, group = lax.axis_size("rep"), lax.axis_size("shard")
    rep, place = lax.axis_index("rep"), lax.axis_index("shard")
    core = rep & 1
    tokens, width = inputs.shape
    rows = width // group
    slab = rows // reps
    hidden = w_fc1.shape[1] // group
    pairs = rows // PAIR
    line = Order()
    def gathered(array):
        return lax.all_gather(array, "rep", axis=0, tiled=True)

    owners = [(place + hop) % group for hop in range(group)]

    def qkv_rows(w):
        return tuple(
            jnp.concatenate(
                [
                    lax.dynamic_slice(w, (rep * slab, at * width + owner * rows), (slab, rows))
                    for at in range(3)
                ],
                axis=1,
            )
            for owner in owners
        )

    def fc1_rows(w):
        return jnp.concatenate(
            [
                lax.dynamic_slice(w, (rep * slab, owner * hidden), (slab, hidden))
                for owner in range(group)
            ]
        )

    qkv_pieces = [
        piece if hop == 0 else ring(piece, "shard", hop)
        for hop, piece in enumerate(line.step(qkv_rows, w_qkv))
    ]
    fc1_pieces = exchanged(line.step(fc1_rows, w_fc1))
    qkv_cols = gathered(line.step(lambda *p: placed(p, place), *qkv_pieces))
    small = jnp.concatenate(
        [ln_gain, ln_bias, b_qkv, b_dense + b_fc2, positions.astype(F32)]
    ).reshape(1, -1)
    small = doubled(small, place, line)
    gain = small[:, :rows].reshape(width)
    shift = small[:, rows : 2 * rows].reshape(width)
    bias_qkv = lax.dynamic_slice_in_dim(
        small[:, 2 * rows : 5 * rows].reshape(3, width), place * rows, rows, 1
    ).reshape(1, 3 * rows)
    bias_out = small[:, 5 * rows : 6 * rows].reshape(width)
    group_positions = small[:, 6 * rows :]

    normed = [line.step(lambda *o: ln_forward(*o, reps, group), inputs, gain, shift)]
    normed.append(ring(line.hold(normed[0]), "shard", 1))

    ring_order = [(place - hop) % group for hop in range(group)]
    ring_positions = jnp.concatenate(
        [lax.dynamic_index_in_dim(group_positions, at, 0, keepdims=False) for at in ring_order]
    )
    start = (
        jnp.arange(SEQ, dtype=jnp.int32)[None, None]
        - group_positions.astype(jnp.int32).reshape(-1, 1, SEQ)
    )
    per_seq = SEQ // tokens
    if group == per_seq:
        turn_place = place
        by_seq = from_seq = lambda array, axis=0: array
    else:
        turn_place = jnp.zeros_like(place)
        seq_order = [at // per_seq * per_seq + (-at) % per_seq for at in range(group)]

        def taken(array, order, axis):
            return jnp.concatenate(
                [
                    lax.dynamic_slice_in_dim(array, at * tokens, tokens, axis)
                    for at in order
                ],
                axis=axis,
            )

        by_seq = lambda array, axis=0: taken(
            array, [(place - at) % group for at in seq_order], axis
        )
        from_seq = lambda array, axis=0: taken(
            array, [at // per_seq * per_seq + (-at) % per_seq for at in ring_order], axis
        )

    turns = line.step(lambda p: by_seq(tables(p), 1), ring_positions)

    def begin(block):
        return jnp.concatenate([block, jnp.zeros(((group - 1) * tokens, width), BF)])

    def put(hop):
        return lambda whole, block: lax.dynamic_update_slice_in_dim(
            whole, block, hop * tokens, 0
        )

    normed_all = line.step(begin, normed[0])
    cot_all = line.step(begin, cotangent)
    def project_some(first, count, *before):
        return line.step(
            lambda a, b, c, *d: project(a, b, c, tokens, first, count, d),
            normed_all,
            qkv_cols,
            bias_qkv,
            *before,
        )

    for hop in range(1, group):
        normed[hop] = line.hold(normed[hop])
        if hop == 1:
            fc1_cols = gathered(line.hold(fc1_pieces))
        if hop + 1 < group:
            normed.append(ring(normed[hop], "shard", 1))
        else:
            cots = [line.hold(cotangent)]
            cots.append(ring(cots[0], "shard", 1))
        normed_all = line.step(put(hop), normed_all, normed[hop])
        if hop == group - 2:
            projected = project_some(0, group - 1)

    projected = by_seq(project_some(group - 1, 1, projected))
    calls = 2 if pairs > 1 else 1
    each = pairs // calls
    kept = []

    def attend_some(call, before):
        attended, *rest = line.step(
            lambda p, *b: attend(p, turns, start, turn_place, call * each, each, tokens, b),
            projected,
            *before,
        )
        kept.append(rest)
        return (attended,)

    attended = attend_some(0, ())
    for hop in range(1, group):
        cots[hop] = line.hold(cots[hop])
        if hop + 1 < group:
            cots.append(ring(cots[hop], "shard", 1))
        cot_all = line.step(put(hop), cot_all, cots[hop])
        if hop == 1:
            activation, slope = line.step(feed_forward, normed_all, fc1_cols, b_fc1)
        if hop == 2:
            if calls > 1:
                attended = attend_some(1, attended)
            out_part = line.step(
                lambda a, b, c, d: push(a, b, c, d, False, place, group),
                from_seq(attended[0]),
                w_dense,
                activation,
                w_fc2,
            )
            out_sum = lax.psum_scatter(out_part, "shard", scatter_dimension=0, tiled=True)
    (attended,) = attended
    attended = from_seq(attended)

    def grad(left, right, *also):
        sent = line.step(
            lambda a, b, *c: half_grads(a, b, 1 - core, reps, None, *c), left, right, *also
        )
        return swap(sent, "rep", 1)

    def grad_sum(left, right, came, *also):
        if reps == 8 and not (left.shape[1] // reps % 128):
            own, *sent = line.step(
                lambda a, b, c, *d: grad_sums(a, b, rep, c, *d), left, right, came, *also
            )
            halving = Halving(rep, own, 2)
            halving.send(line, sent)
            return halving
        own = line.step(
            lambda a, b, c, *d: half_grads(a, b, core, reps, c, *d), left, right, came, *also
        )
        halving = Halving(rep, own, 2)
        halving.send(line)
        return halving

    def attend_back_some(call, before):
        return line.step(
            lambda d, t, *b: attend_back(
                kept[call], d, t, turn_place, call * each, tokens, pairs, b
            ),
            d_attended,
            turns,
            *before,
        )

    out_came = grad(activation, cot_all, attended)
    d_pre = line.step(pull, cot_all, w_fc2, slope)
    fc1_came = grad(normed_all, d_pre)
    out_grads = grad_sum(activation, cot_all, out_came, attended)
    d_attended = by_seq(
        line.step(lambda c, w: times_transpose(c, w).astype(BF), cot_all, w_dense)
    )
    back = attend_back_some(0, ())
    fc1_sum = grad_sum(normed_all, d_pre, fc1_came)
    out_grads.further(line)
    for call in range(1, calls):
        back = attend_back_some(call, back)
    d_projected, d_bias_qkv = back
    d_projected = from_seq(d_projected)
    d_normed_part = line.step(
        lambda a, b, c, d: push(a, b, c, d, True, place), d_projected, qkv_cols, d_pre, fc1_cols
    )
    d_normed_sum = Passing(line, d_normed_part, tokens)
    out_piece = out_grads.end(line)
    fc1_sum.further(line)
    out_whole = gathered(line.hold(out_piece))
    qkv_came = grad(normed_all, d_projected)
    block_out = line.step(
        lambda x, b, p: x.astype(F32) + b + p.astype(F32), inputs, bias_out, out_sum
    )
    qkv_sum = grad_sum(normed_all, d_projected, qkv_came)
    fc1_pieces = exchanged(line.hold(fc1_sum.end(line)))
    d_normed_sum.further()
    qkv_sum.further(line)

    def bias_sums(d_bias_qkv, cotangent, d_pre):
        d_bias_all = lax.dynamic_update_slice_in_dim(
            jnp.zeros((3, width), F32),
            jnp.sum(d_bias_qkv[:, 0], axis=0).reshape(3, rows),
            place * rows,
            1,
        )
        ones = jnp.ones((8, group * tokens), BF)
        return (
            jnp.concatenate(
                [
                    d_bias_all.reshape(group, 3 * rows),
                    jnp.sum(cotangent.astype(F32), axis=0).reshape(group, rows),
                ],
                axis=1,
            ),
            times(ones, d_pre)[0],
        )

    early_sums, d_bias_fc1 = line.step(bias_sums, d_bias_qkv, cotangent, d_pre)
    qkv_piece = qkv_sum.end(line)
    d_normed_sum.hold()
    fc1_slab = line.step(lambda p: widened(p, group, hidden), fc1_pieces)
    qkv_pieces = exchanged(line.hold(qkv_piece))
    fc1_whole = gathered(line.hold(fc1_slab))
    qkv_spread = Spread(line, line.step(lambda p: widened(p, group, rows), qkv_pieces))
    d_normed_sum.further()
    fc2_total, dense_total = line.step(
        lambda a: split_rows(a, reps, (hidden // reps, slab)), out_whole
    )
    grad_inputs, norm_sums = line.step(
        lambda x, g, c, *p: ln_backward(x, g, c, p, reps, group),
        inputs,
        gain,
        cotangent,
        *d_normed_sum.end(),
    )

    sums = line.step(
        lambda early, norm_sums: jnp.concatenate(
            [early, norm_sums[0].reshape(group, rows), norm_sums[1].reshape(group, rows)], axis=1
        ),
        early_sums,
        norm_sums,
    )
    qkv_spread.across()
    sums = owned_sum(line, sums, place)
    sums = line.hold(jnp.concatenate([sums, d_bias_fc1]))
    sums = line.hold(sums + swap(sums, "rep", 1))
    (fc1_total,) = line.step(lambda a: split_rows(a, reps, (slab,)), fc1_whole)
    qkv_spread = qkv_spread.shared()
    bit = 2
    while bit < reps:
        sums = line.hold(sums + swap(sums, "rep", bit))
        bit *= 2
    qkv_total = line.step(lambda *p: assemble(p, rep), *qkv_spread)
    cot_total = sums[3 * rows : 4 * rows]
    return (
        block_out,
        grad_inputs,
        sums[4 * rows : 5 * rows],
        sums[5 * rows : 6 * rows],
        qkv_total,
        sums[: 3 * rows],
        dense_total,
        cot_total,
        fc1_total,
        sums[6 * rows :],
        fc2_total,
        cot_total,
    )


def solution(mesh):
    both, shard = P(("rep", "shard")), P("shard")
    wide, held = P(("rep", "shard"), None), P("shard", None)
    return jax.shard_map(
        shards,
        mesh=mesh,
        in_specs=(
            wide, both, both, shard, shard, held, shard, held, shard, held, shard, held, shard, wide
        ),
        out_specs=(
            wide, wide, shard, shard, held, shard, held, shard, held, shard, held, shard
        ),
        check_vma=False,
    )
```
